1024 devices in a mesh: lon: 64 (over y_hi, z), lat: 16 (over x, y_lo, core).
Axes of the slice: x: 4, y: 4 (y_hi: 2, y_lo: 2; y = y_hi * 2 + y_lo), z: 32, core: 2. Of those that a mesh axis runs over, the one named last changes fastest.
Arguments:
- ocean_state: float32 [4, 16, 512, 8192], P(None, None, 'lat', 'lon'), may hold values from -4 to 4
- surface_state: float32 [3, 512, 8192], P(None, 'lat', 'lon'), may hold values from -3 to 3
- column_levels: int32 [512, 8192], P('lat', 'lon'), may hold values from 0 to 16
Outputs:
- ocean_next: float32 [4, 16, 512, 8192], P(None, None, 'lat', 'lon')
- surface_next: float32 [3, 512, 8192], P(None, 'lat', 'lon')
The draws below stay inside these ranges and needn't reach their ends.
Inputs may be any that keep to these rules, and one draw needn't show every extreme that they name: A column holds sea in the levels k < column_levels, counted from the surface; 0 marks land.
All inputs are finite; a program needn't handle non-finite values.
Results may differ from the reference program's by a relative error of at most 0.0003.
Values sent between devices are 32-bit elements; how exact they have to be, the bound alone decides.
No kernel may reach another device: no remote copies, remote signals or barrier semaphores. Data moves between devices by JAX's collectives and lax.ppermute only.
A program may use at most 32 MiB of HBM per device.

```python
import math
import jax
import jax.numpy as jnp
from jax import lax

LEVELS = 16
NSUB = 4
NLAT = 512
NLON = 8192


def plant(values, own_key, smallest, largest):
    place = [jax.random.randint(jax.random.fold_in(own_key, axis), (), 0, length) for axis, length in enumerate(values.shape)]
    longest = values.shape.index(max(values.shape))
    neighbour = place[:longest] + [(place[longest] + 1) % values.shape[longest]] + place[longest + 1:]
    return values.at[tuple(place)].set(smallest).at[tuple(neighbour)].set(largest)


def block_scale(rng, dims, pieces, least, top_value):
    def one(position, parts):
        steps = jax.random.uniform(jax.random.fold_in(jax.random.fold_in(rng, 6), position), (parts,), jnp.float32, least / len(pieces), top_value / len(pieces))
        return jnp.repeat(jnp.exp(steps), dims[position] // parts).reshape((-1,) + (1,) * (len(dims) - position - 1))

    factor_of = one(*pieces[0])
    for cut in pieces[1:]:
        factor_of = factor_of * one(*cut)
    return factor_of


def gaussian(key, dims, spread, limit, pieces=(), held_as=jnp.bfloat16):
    values = spread * jax.random.normal(key, dims, jnp.float32)
    if pieces:
        values = values * block_scale(key, dims, pieces, -0.22, 0.18)
    return jnp.clip(values, -limit, limit).astype(held_as)


def setup_inputs(seed: int = 0) -> dict:
    seeds = jax.random.split(jax.random.key(seed), 4)
    return {
        "ocean_state": gaussian(seeds[0], (4, LEVELS, NLAT, NLON), 1.0, 4.0, ((2, 16), (3, 64)), jnp.float32),
        "surface_state": gaussian(seeds[1], (3, NLAT, NLON), 0.5, 3.0, ((1, 16), (2, 64)), jnp.float32),
        "column_levels": plant(jax.random.randint(seeds[2], (NLAT, NLON), 0, LEVELS + 1), jax.random.fold_in(seeds[2], 1), 0, LEVELS).astype(jnp.int32),
    }


epsilon = 1e-6
tracer_step = 0.1
surface_step = 1.2


def weno_pick(a, b, c, d, e):
    first_poly = (2.0 * a - 7.0 * b + 11.0 * c) / 6.0
    second_poly = (-b + 5.0 * c + 2.0 * d) / 6.0
    third_poly = (2.0 * c + 5.0 * d - e) / 6.0
    first_bend = a - 2.0 * b + c
    first_tilt = a - 4.0 * b + 3.0 * c
    middle_curvature = b - 2.0 * c + d
    second_tilt = b - d
    third_bend = c - 2.0 * d + e
    third_tilt = 3.0 * c - 4.0 * d + e
    first_smooth = epsilon + (13.0 / 12.0) * first_bend * first_bend + 0.25 * first_tilt * first_tilt
    second_smooth = epsilon + (13.0 / 12.0) * middle_curvature * middle_curvature + 0.25 * second_tilt * second_tilt
    third_smooth = epsilon + (13.0 / 12.0) * third_bend * third_bend + 0.25 * third_tilt * third_tilt
    leading_weight = 0.1 / (first_smooth * first_smooth)
    second_weight = 0.6 / (second_smooth * second_smooth)
    third_weight = 0.3 / (third_smooth * third_smooth)
    total_weight = leading_weight + second_weight + third_weight
    return (leading_weight * first_poly + second_weight * second_poly + third_weight * third_poly) / total_weight


def take_slab(source, offset, length, direction):
    return lax.slice_in_dim(source, offset, offset + length, axis=direction)


def flow_divergence(quantity, velocity, wet_mask, cell_count, direction):
    face_count = cell_count + 1
    a = take_slab(quantity, 0, face_count, direction)
    b = take_slab(quantity, 1, face_count, direction)
    c = take_slab(quantity, 2, face_count, direction)
    d = take_slab(quantity, 3, face_count, direction)
    e = take_slab(quantity, 4, face_count, direction)
    far_ahead = take_slab(quantity, 5, face_count, direction)
    left_value = weno_pick(a, b, c, d, e)
    eastern_reconstruction = weno_pick(far_ahead, e, d, c, b)
    face_speed = 0.5 * (take_slab(velocity, 2, face_count, direction) + take_slab(velocity, 3, face_count, direction))
    face_speed = face_speed * take_slab(wet_mask, 2, face_count, direction) * take_slab(wet_mask, 3, face_count, direction)
    face_flux = face_speed * jnp.where(face_speed >= 0.0, left_value, eastern_reconstruction)
    return take_slab(face_flux, 1, cell_count, direction) - take_slab(face_flux, 0, cell_count, direction)


def level_advection(quantities, wet_level):
    row_count = quantities.shape[1] - 6
    col_count = quantities.shape[2] - 6
    along_lon = flow_divergence(quantities[:, 3:-3, :], quantities[2:3, 3:-3, :], wet_level[None, 3:-3, :], col_count, 2)
    along_lat = flow_divergence(quantities[:, :, 3:-3], quantities[3:4, :, 3:-3], wet_level[None, :, 3:-3], row_count, 1)
    return along_lon + along_lat


def layer_step(gathered_arrays, ocean_layer_masks, advection, coriolis):
    levels = gathered_arrays.shape[1]
    thickness = 1.0 / levels
    theta_heat_tracer = gathered_arrays[0]
    haline_tracer = gathered_arrays[1]
    seawater_mass_per_volume = (-0.2 * theta_heat_tracer + 0.8 * haline_tracer - 0.05 * theta_heat_tracer * theta_heat_tracer
               + 0.03 * theta_heat_tracer * haline_tracer) * ocean_layer_masks
    pressure = thickness * (jnp.cumsum(seawater_mass_per_volume, axis=0) - 0.5 * seawater_mass_per_volume)
    grad_lon = 0.5 * (pressure[:, 3:-3, 4:-2] - pressure[:, 3:-3, 2:-4])
    grad_lat = 0.5 * (pressure[:, 4:-2, 3:-3] - pressure[:, 2:-4, 3:-3])
    interior = gathered_arrays[:, :, 3:-3, 3:-3]
    wet_mask = ocean_layer_masks[:, 3:-3, 3:-3]
    rotation = coriolis[None, :, None]
    accel_u = wet_mask * (-advection[2] + rotation * interior[3] - grad_lon)
    accel_v = wet_mask * (-advection[3] - rotation * interior[2] - grad_lat)
    new_temp = wet_mask * (interior[0] - tracer_step * advection[0])
    new_salt = wet_mask * (interior[1] - tracer_step * advection[1])
    u_star = wet_mask * interior[2] + tracer_step * accel_u
    v_star = wet_mask * interior[3] + tracer_step * accel_v
    depth_rim = thickness * jnp.sum(ocean_layer_masks[:, 1:-1, 1:-1], axis=0)
    safe_depth = jnp.maximum(depth_rim[2:-2, 2:-2], thickness)
    force_lon = thickness * jnp.sum(accel_u, axis=0) / safe_depth
    force_lat = thickness * jnp.sum(accel_v, axis=0) / safe_depth
    return new_temp, new_salt, u_star, v_star, force_lon, force_lat, depth_rim, safe_depth, wet_mask


def centered_lon(field):
    padded = jnp.pad(field, ((0, 0), (1, 1)))
    return 0.5 * (padded[:, 2:] - padded[:, :-2])


def centered_lat(field):
    padded = jnp.pad(field, ((1, 1), (0, 0)))
    return 0.5 * (padded[2:, :] - padded[:-2, :])


def substep_update(height, mean_u, mean_v, depth_rim, force_lon, force_lat):
    sea_mask = (depth_rim > 0.0).astype(depth_rim.dtype)
    height = sea_mask * (height - surface_step * (centered_lon(depth_rim * mean_u) + centered_lat(depth_rim * mean_v)))
    mean_u = sea_mask * (mean_u + surface_step * (force_lon - centered_lon(height)))
    mean_v = sea_mask * (mean_v + surface_step * (force_lat - centered_lat(height)))
    return height, mean_u, mean_v


def padded_globe(field, rim_width, signs):
    wide = jnp.concatenate([field[..., -rim_width:], field, field[..., :rim_width]], axis=-1)
    north = jnp.flip(wide[..., -rim_width:, :], axis=(-2, -1)) * signs
    return jnp.concatenate([jnp.zeros_like(north), wide, north], axis=-2)


def advect_level(level_pair):
    return level_advection(level_pair[0], level_pair[1])


def reference(ocean_state, surface_state, column_levels):
    thickness = 1.0 / LEVELS
    level_index = jnp.arange(LEVELS, dtype=jnp.int32)
    ocean_layer_masks = (level_index[:, None, None] < column_levels[None]).astype(ocean_state.dtype)
    field_signs = jnp.array([1.0, 1.0, -1.0, -1.0], dtype=ocean_state.dtype)[:, None, None, None]
    gathered_arrays = padded_globe(ocean_state, 3, field_signs)
    wet_rim = padded_globe(ocean_layer_masks, 3, 1.0)
    advection = jnp.moveaxis(lax.map(advect_level, (jnp.moveaxis(gathered_arrays, 1, 0), wet_rim)), 0, 1)
    latitude = (jnp.arange(NLAT, dtype=ocean_state.dtype) + 0.5) / NLAT
    coriolis = jnp.sin(math.pi * latitude - 0.5 * math.pi)
    new_temp, new_salt, u_star, v_star, force_lon, force_lat, depth_rim, safe_depth, wet_mask = layer_step(
        gathered_arrays, wet_rim, advection, coriolis)
    force_lon_rim = jnp.pad(force_lon, 2)
    force_lat_rim = jnp.pad(force_lat, 2)
    surface_signs = jnp.array([1.0, -1.0, -1.0], dtype=ocean_state.dtype)[:, None, None]
    height = surface_state[0]
    mean_u = surface_state[1]
    mean_v = surface_state[2]
    for substep in range(NSUB):
        rim_stack = padded_globe(jnp.stack([height, mean_u, mean_v]), 2, surface_signs)
        height, mean_u, mean_v = substep_update(rim_stack[0], rim_stack[1], rim_stack[2], depth_rim,
                                                force_lon_rim, force_lat_rim)
        height = height[2:-2, 2:-2]
        mean_u = mean_u[2:-2, 2:-2]
        mean_v = mean_v[2:-2, 2:-2]
    mean_star_u = thickness * jnp.sum(u_star, axis=0) / safe_depth
    mean_star_v = thickness * jnp.sum(v_star, axis=0) / safe_depth
    u_final = wet_mask * (u_star + mean_u - mean_star_u)
    v_final = wet_mask * (v_star + mean_v - mean_star_v)
    return (jnp.stack([new_temp, new_salt, u_final, v_final]), jnp.stack([height, mean_u, mean_v]))
```

```python
import math

import jax
import jax.numpy as jnp
from jax import lax
from jax.sharding import PartitionSpec as P

NSUB = 4


epsilon = 1e-06
tracer_step = 0.1
surface_step = 1.2


def weno_pick(a, b, c, d, e):
    first_poly = (2.0 * a - 7.0 * b + 11.0 * c) / 6.0
    second_poly = (-b + 5.0 * c + 2.0 * d) / 6.0
    third_poly = (2.0 * c + 5.0 * d - e) / 6.0
    first_bend = a - 2.0 * b + c
    first_tilt = a - 4.0 * b + 3.0 * c
    middle_curvature = b - 2.0 * c + d
    second_tilt = b - d
    third_bend = c - 2.0 * d + e
    third_tilt = 3.0 * c - 4.0 * d + e
    first_smooth = epsilon + 13.0 / 12.0 * first_bend * first_bend + 0.25 * first_tilt * first_tilt
    second_smooth = (
        epsilon
        + 13.0 / 12.0 * middle_curvature * middle_curvature
        + 0.25 * second_tilt * second_tilt
    )
    third_smooth = epsilon + 13.0 / 12.0 * third_bend * third_bend + 0.25 * third_tilt * third_tilt
    leading_weight = 0.1 / (first_smooth * first_smooth)
    second_weight = 0.6 / (second_smooth * second_smooth)
    third_weight = 0.3 / (third_smooth * third_smooth)
    total_weight = leading_weight + second_weight + third_weight
    return (
        leading_weight * first_poly + second_weight * second_poly + third_weight * third_poly
    ) / total_weight


def take_slab(source, offset, length, direction):
    return lax.slice_in_dim(source, offset, offset + length, axis=direction)


def flow_divergence(quantity, velocity, wet_mask, cell_count, direction):
    face_count = cell_count + 1
    a = take_slab(quantity, 0, face_count, direction)
    b = take_slab(quantity, 1, face_count, direction)
    c = take_slab(quantity, 2, face_count, direction)
    d = take_slab(quantity, 3, face_count, direction)
    e = take_slab(quantity, 4, face_count, direction)
    far_ahead = take_slab(quantity, 5, face_count, direction)
    left_value = weno_pick(a, b, c, d, e)
    eastern_reconstruction = weno_pick(far_ahead, e, d, c, b)
    face_speed = 0.5 * (
        take_slab(velocity, 2, face_count, direction)
        + take_slab(velocity, 3, face_count, direction)
    )
    face_speed = (
        face_speed
        * take_slab(wet_mask, 2, face_count, direction)
        * take_slab(wet_mask, 3, face_count, direction)
    )
    face_flux = face_speed * jnp.where(face_speed >= 0.0, left_value, eastern_reconstruction)
    return take_slab(face_flux, 1, cell_count, direction) - take_slab(
        face_flux, 0, cell_count, direction
    )


def level_advection(quantities, wet_level):
    row_count = quantities.shape[1] - 6
    col_count = quantities.shape[2] - 6
    along_lon = flow_divergence(
        quantities[:, 3:-3, :], quantities[2:3, 3:-3, :], wet_level[None, 3:-3, :], col_count, 2
    )
    along_lat = flow_divergence(
        quantities[:, :, 3:-3], quantities[3:4, :, 3:-3], wet_level[None, :, 3:-3], row_count, 1
    )
    return along_lon + along_lat


def advect_level(level_pair):
    return level_advection(level_pair[0], level_pair[1])


def layer_step(gathered_arrays, ocean_layer_masks, advection, coriolis):
    levels = gathered_arrays.shape[1]
    thickness = 1.0 / levels
    theta_heat_tracer = gathered_arrays[0]
    haline_tracer = gathered_arrays[1]
    seawater_mass_per_volume = (
        -0.2 * theta_heat_tracer
        + 0.8 * haline_tracer
        - 0.05 * theta_heat_tracer * theta_heat_tracer
        + 0.03 * theta_heat_tracer * haline_tracer
    ) * ocean_layer_masks
    pressure = thickness * (
        jnp.cumsum(seawater_mass_per_volume, axis=0) - 0.5 * seawater_mass_per_volume
    )
    grad_lon = 0.5 * (pressure[:, 3:-3, 4:-2] - pressure[:, 3:-3, 2:-4])
    grad_lat = 0.5 * (pressure[:, 4:-2, 3:-3] - pressure[:, 2:-4, 3:-3])
    interior = gathered_arrays[:, :, 3:-3, 3:-3]
    wet_mask = ocean_layer_masks[:, 3:-3, 3:-3]
    rotation = coriolis[None, :, None]
    accel_u = wet_mask * (-advection[2] + rotation * interior[3] - grad_lon)
    accel_v = wet_mask * (-advection[3] - rotation * interior[2] - grad_lat)
    new_temp = wet_mask * (interior[0] - tracer_step * advection[0])
    new_salt = wet_mask * (interior[1] - tracer_step * advection[1])
    u_star = wet_mask * interior[2] + tracer_step * accel_u
    v_star = wet_mask * interior[3] + tracer_step * accel_v
    depth_rim = thickness * jnp.sum(ocean_layer_masks[:, 1:-1, 1:-1], axis=0)
    safe_depth = jnp.maximum(depth_rim[2:-2, 2:-2], thickness)
    force_lon = thickness * jnp.sum(accel_u, axis=0) / safe_depth
    force_lat = thickness * jnp.sum(accel_v, axis=0) / safe_depth
    return (
        new_temp,
        new_salt,
        u_star,
        v_star,
        force_lon,
        force_lat,
        depth_rim,
        safe_depth,
        wet_mask,
    )


def centered_lon(field):
    padded = jnp.pad(field, ((0, 0), (1, 1)))
    return 0.5 * (padded[:, 2:] - padded[:, :-2])


def centered_lat(field):
    padded = jnp.pad(field, ((1, 1), (0, 0)))
    return 0.5 * (padded[2:, :] - padded[:-2, :])


def substep_update(height, mean_u, mean_v, depth_rim, force_lon, force_lat):
    sea_mask = (depth_rim > 0.0).astype(depth_rim.dtype)
    height = sea_mask * (
        height
        - surface_step * (centered_lon(depth_rim * mean_u) + centered_lat(depth_rim * mean_v))
    )
    mean_u = sea_mask * (mean_u + surface_step * (force_lon - centered_lon(height)))
    mean_v = sea_mask * (mean_v + surface_step * (force_lat - centered_lat(height)))
    return (height, mean_u, mean_v)


def lon_ring(step):
    count = lax.axis_size("lon")
    return [(i, (i + step) % count) for i in range(count)]


def fold_path(backward):
    lon_count = lax.axis_size("lon")
    lat_count = lax.axis_size("lat")
    pairs = []
    for p in range(lon_count // 2):
        q = lon_count - 1 - p
        path = [p * lat_count + r for r in range(lat_count)]
        path += [q * lat_count + r for r in reversed(range(lat_count))]
        pairs += list(zip(path[:-1], path[1:]))
    return [(t, s) for s, t in pairs] if backward else pairs


def exchange_lon(from_low_edge, from_high_edge):
    low = lax.ppermute(from_high_edge, "lon", lon_ring(1))
    high = lax.ppermute(from_low_edge, "lon", lon_ring(-1))
    return low, high


def exchange_lat(south_edge, north_edge):
    west_half = lax.axis_index("lon") < lax.axis_size("lon") // 2
    up = lax.ppermute(jnp.where(west_half, north_edge, south_edge), ("lon", "lat"), fold_path(False))
    down = lax.ppermute(jnp.where(west_half, south_edge, north_edge), ("lon", "lat"), fold_path(True))
    south = jnp.where(west_half, up, down)
    north = jnp.where(west_half, down, up)
    south = jnp.where(lax.axis_index("lat") == 0, jnp.zeros_like(south), south)
    return south, north


def fold_north(north, signs):
    top = lax.axis_index("lat") == lax.axis_size("lat") - 1
    return jnp.where(top, jnp.flip(north, axis=(-2, -1)) * signs, north)


def edge_columns(planes, start, width):
    return jnp.moveaxis(lax.slice_in_dim(planes, start, start + width, axis=-1), -1, 0)


def on_device(ocean_state, surface_state, column_levels):
    levels, row_count, col_count = ocean_state.shape[1:]
    thickness = 1.0 / levels
    state = ocean_state.reshape(4 * levels, row_count, col_count)
    flat = jnp.concatenate([surface_state, column_levels.astype(jnp.float32)[None]])

    def pack(start3, start8):
        deep = edge_columns(state, start3, 3).reshape(-1, 128)
        shallow = edge_columns(flat, start8, 8).reshape(-1, 128)
        return jnp.concatenate([deep, shallow])

    def unpack(packed):
        deep_size = 3 * 4 * levels * row_count // 128
        deep = packed[:deep_size].reshape(3, 4 * levels, row_count)
        shallow = packed[deep_size:].reshape(8, 4, row_count)
        return jnp.moveaxis(deep, 0, -1), jnp.moveaxis(shallow, 0, -1)

    rows_out = jnp.concatenate([state, flat[3:]])
    south, north = exchange_lat(rows_out[:, :3], rows_out[:, -3:])
    low, high = exchange_lon(pack(0, 0), pack(col_count - 3, col_count - 8))
    deep_low, flat_low = unpack(low)
    deep_high, flat_high = unpack(high)
    plane_signs = jnp.concatenate(
        [jnp.ones((2 * levels,)), -jnp.ones((2 * levels,)), jnp.ones((1,))]
    ).astype(jnp.float32)[:, None, None]
    north = fold_north(north, plane_signs)
    flat_wide = jnp.concatenate([flat_low, flat, flat_high], axis=-1)

    mid = jnp.concatenate([deep_low, state, deep_high], axis=-1)
    rim = ((0, 0), (0, 0), (3, 3))
    padded = jnp.concatenate(
        [jnp.pad(south[:-1], rim), mid, jnp.pad(north[:-1], rim)], axis=1
    )
    gathered_arrays = padded.reshape(4, levels, row_count + 6, col_count + 6)
    level_rim = jnp.concatenate(
        [
            jnp.pad(south[-1], rim[1:]),
            flat_wide[3, :, 5:-5],
            jnp.pad(north[-1], rim[1:]),
        ],
        axis=0,
    )
    level_index = jnp.arange(levels, dtype=jnp.int32).astype(jnp.float32)[:, None, None]
    wet_rim = (level_index < level_rim[None]).astype(jnp.float32)
    advection = jnp.moveaxis(
        lax.map(advect_level, (jnp.moveaxis(gathered_arrays, 1, 0), wet_rim)), 0, 1
    )
    first_row = lax.axis_index("lat") * row_count
    latitude = (
        (first_row + jnp.arange(row_count, dtype=jnp.int32)).astype(jnp.float32) + 0.5
    ) / float(lax.axis_size("lat") * row_count)
    coriolis = jnp.sin(math.pi * latitude - 0.5 * math.pi)
    new_temp, new_salt, u_star, v_star, force_lon, force_lat, _, safe_depth, wet_mask = layer_step(
        gathered_arrays, wet_rim, advection, coriolis
    )
    forces = jnp.stack([force_lon, force_lat])
    flow, fhigh = exchange_lon(
        jnp.moveaxis(forces[..., :8], -1, 0).reshape(-1, 128),
        jnp.moveaxis(forces[..., -8:], -1, 0).reshape(-1, 128),
    )
    flow = jnp.moveaxis(flow.reshape(8, 2, row_count), 0, -1)
    fhigh = jnp.moveaxis(fhigh.reshape(8, 2, row_count), 0, -1)
    forces_wide = jnp.concatenate([flow, forces, fhigh], axis=-1)
    six = jnp.concatenate([flat_wide, forces_wide])
    south6, north6 = exchange_lat(six[:, :8], six[:, -8:])
    signs6 = jnp.array([1.0, -1.0, -1.0, 1.0, -1.0, -1.0], jnp.float32)[:, None, None]
    six = jnp.concatenate([south6, six, fold_north(north6, signs6)], axis=1)
    height, mean_u, mean_v, level_map, force_lon, force_lat = six
    depth_rim = thickness * level_map
    for substep in range(NSUB):
        height, mean_u, mean_v = substep_update(
            height, mean_u, mean_v, depth_rim, force_lon, force_lat
        )
    height, mean_u, mean_v = (part[8:-8, 8:-8] for part in (height, mean_u, mean_v))
    mean_star_u = thickness * jnp.sum(u_star, axis=0) / safe_depth
    mean_star_v = thickness * jnp.sum(v_star, axis=0) / safe_depth
    u_final = wet_mask * (u_star + mean_u - mean_star_u)
    v_final = wet_mask * (v_star + mean_v - mean_star_v)
    return (jnp.stack([new_temp, new_salt, u_final, v_final]), jnp.stack([height, mean_u, mean_v]))


def solution(mesh):
    return jax.shard_map(
        on_device,
        mesh=mesh,
        in_specs=(P(None, None, "lat", "lon"), P(None, "lat", "lon"), P("lat", "lon")),
        out_specs=(P(None, None, "lat", "lon"), P(None, "lat", "lon")),
        check_vma=False,
    )
```

```python
import functools
import math

import jax
import jax.numpy as jnp
import numpy as np
from jax import lax
from jax.experimental import pallas as pl
from jax.experimental.pallas import tpu as pltpu
from jax.sharding import PartitionSpec as P

NSUB = 4
LEVELS = 16
ROWS = 32
COLS = 128
BLOCKS = ROWS // 8
THICKNESS = 1.0 / LEVELS
TRACER_STEP = 0.1
SURFACE_STEP = 1.2
PIECES = 2 * LEVELS + 6

F32 = jnp.float32


def lane_index(rows=8):
    return lax.broadcasted_iota(jnp.int32, (rows, COLS), 1)


def row_index(rows=8):
    return lax.broadcasted_iota(jnp.int32, (rows, COLS), 0)


def roll(x, shift, axis):
    if isinstance(shift, int):
        shift %= x.shape[axis]
        if shift == 0:
            return x
    return pltpu.roll(x, shift, axis)


def upwind_flux(speed, qm2, qm1, q0, q1, q2, q3):
    ahead = speed >= 0.0
    a = jnp.where(ahead, qm2, q3)
    b = jnp.where(ahead, qm1, q2)
    c = jnp.where(ahead, q0, q1)
    d = jnp.where(ahead, q1, q0)
    e = jnp.where(ahead, q2, qm1)
    ab = a - b
    bc = b - c
    cd = c - d
    de = d - e
    x1 = ab - bc
    y1 = ab - 3.0 * bc
    x2 = bc - cd
    y2 = bc + cd
    x3 = cd - de
    y3 = 3.0 * cd - de
    third = 13.0 / 3.0
    s1 = third * (x1 * x1) + (y1 * y1 + 4e-6)
    s2 = third * (x2 * x2) + (y2 * y2 + 4e-6)
    s3 = third * (x3 * x3) + (y3 * y3 + 4e-6)
    r1 = s2 * s3
    r2 = s1 * s3
    r3 = s1 * s2
    w1 = r1 * r1
    w2 = 6.0 * (r2 * r2)
    w3 = 3.0 * (r3 * r3)
    top = w1 * (2.0 * ab - 5.0 * bc) - w2 * (bc + 2.0 * cd) + w3 * (de - 4.0 * cd)
    low = 6.0 * (w1 + w2 + w3)
    return speed * (c + top / low)


def density(t, s, wet):
    return wet * (t * (0.03 * s - 0.2 - 0.05 * t) + 0.8 * s)


def wet_of(level_map, k):
    return jnp.where(level_map > k, 1.0, 0.0).astype(F32)


def pack_kernel(ocean, levels, out):
    group = lane_index() // 8
    for b in range(BLOCKS):
        rows = pl.ds(8 * b, 8)
        for q in range(4):

            def place(k, packed, q=q, rows=rows):
                moved = pltpu.roll(ocean[q, k, rows, :], 8 * k + 4, 1)
                return jnp.where(group == k, moved, packed)

            packed = jnp.zeros((8, COLS), F32)
            for k in range(LEVELS):
                packed = place(k, packed)
            out[q, rows, :] = packed
        out[4, rows, :] = roll(levels[rows, :].astype(F32), 4, 1)


def halo_pack(q, rows, low, high):
    from_low = lane_index() % 8 < 4
    return jnp.where(from_low, low[q, rows, :], high[q, rows, :])


def next_lon(main, halo, step):
    lane = lane_index()
    if step > 0:
        return roll(jnp.where(lane < step, halo, main), -step, 1)
    return roll(jnp.where(lane >= COLS + step, halo, main), -step, 1)


def lon_shifts(main, halo):
    return [main if d == 0 else next_lon(main, halo, d) for d in (-2, -1, 0, 1, 2, 3)]


def west_faces(own, low, levels, quantities, halos, west_flux):
    lane = lane_index()
    from_low = lane % 8 < 4
    level_of = lane // 8
    for b in range(BLOCKS):
        rows = pl.ds(8 * b, 8)
        lev = levels[rows, :].astype(F32)
        own_col = lev[:, 0:1]
        west_col = low[4, rows, :][:, 3:4]
        both = jnp.minimum(own_col, west_col)
        wet = jnp.where(both > level_of.astype(F32), 1.0, 0.0)
        u = jnp.where(from_low, low[2, rows, :], own[2, rows, :])
        speed = 0.5 * (u + roll(u, -1, 1)) * wet
        for n, q in enumerate(quantities):
            x = jnp.where(from_low, low[q, rows, :], own[q, rows, :])
            west_flux[n, rows, :] = upwind_flux(speed, *[roll(x, -d, 1) for d in (-2, -1, 0, 1, 2, 3)])
        for n, q in enumerate(halos[0]):
            halos[1][n, rows, :] = halo_pack(q, rows, low, halos[2])


def lat_shift(ocean, q, k, b, d):
    start = 8 * b + d
    if 0 <= start and start + 8 <= ROWS:
        return ocean[q, k, start : start + 8, :]
    return roll(ocean[q, k, pl.ds(8 * b, 8), :], -d, 0)


def level_map_shift(levels, b, d):
    start = 8 * b + d
    if 0 <= start and start + 8 <= ROWS:
        return levels[start : start + 8, :].astype(F32)
    return roll(levels[pl.ds(8 * b, 8), :].astype(F32), -d, 0)


def tile_divergence(ocean, levels, k, halo_of, lev_halo, quantities, west_flux):
    lane = lane_index()
    sub = row_index()
    unplace = 124 - 8 * k
    result = {}
    last = {}
    for b in range(BLOCKS):
        rows = pl.ds(8 * b, 8)
        lev = levels[rows, :].astype(F32)
        wet = wet_of(lev, k)
        u = ocean[2, k, rows, :]
        wet_east = wet_of(next_lon(lev, lev_halo[rows, :], 1), k)
        speed_lon = 0.5 * (u + next_lon(u, halo_of(2, rows), 1)) * (wet * wet_east)
        wet_north = wet_of(level_map_shift(levels, b, 1), k)
        speed_lat = 0.5 * (ocean[3, k, rows, :] + lat_shift(ocean, 3, k, b, 1)) * (wet * wet_north)
        for n, q in enumerate(quantities):
            main = ocean[q, k, rows, :]
            east = upwind_flux(speed_lon, *lon_shifts(main, halo_of(q, rows)))
            west = pltpu.roll(west_flux[n, rows, :], unplace, 1)
            west = roll(jnp.where(lane == COLS - 1, west, east), 1, 1)
            north = upwind_flux(speed_lat, *[lat_shift(ocean, q, k, b, d) for d in (-2, -1, 0, 1, 2, 3)])
            if b == 0:
                north = jnp.where(sub >= 2, north, 0.0)
            if b == BLOCKS - 1:
                north = jnp.where(sub <= 4, north, 0.0)
            rolled = roll(north, 1, 0)
            south = jnp.where(sub == 0, last[n] if b else 0.0, rolled)
            last[n] = rolled
            result[n, b] = (east - west) + (north - south)
    return result


def momentum_kernel(
    flags, ocean, levels, surface, coriolis, own, low, high,
    accel, up, down, sums, west_flux, packed, cum, cum_halo, lev_halo,
):
    sub = row_index()
    west_half = flags[0] == 1
    west_faces(own, low, levels, (2, 3), ((0, 1, 2, 3), packed, high), west_flux)
    for b in range(BLOCKS):
        rows = pl.ds(8 * b, 8)
        lev_halo[rows, :] = roll(halo_pack(4, rows, low, high), -4, 1)
    cum[...] = jnp.zeros_like(cum)
    cum_halo[...] = jnp.zeros_like(cum_halo)
    sums[...] = jnp.zeros_like(sums)

    def send(index, south, north):
        up[index] = jnp.where(west_half, north, south)
        down[index] = jnp.where(west_half, south, north)

    first, last_rows = pl.ds(0, 8), pl.ds(ROWS - 8, 8)

    def level(k, carry):
        unplace = 124 - 8 * k
        halo = {}

        def halo_of(q, rows):
            key = (q, rows.start)
            if key not in halo:
                halo[key] = pltpu.roll(packed[q, rows, :], unplace, 1)
            return halo[key]

        for pair in range(2):
            t0, t3 = ocean[pair, k, first, :], ocean[pair, k, last_rows, :]
            u0, u3 = ocean[pair + 2, k, first, :], ocean[pair + 2, k, last_rows, :]
            send(
                pair * LEVELS + k,
                jnp.where(sub < 5, u0, roll(t0, 5, 0)),
                jnp.where(sub < 3, roll(t3, 3, 0), u3),
            )
        advection = tile_divergence(ocean, levels, k, halo_of, lev_halo, (2, 3), west_flux)
        pressure, pressure_halo = [], []
        for b in range(BLOCKS):
            rows = pl.ds(8 * b, 8)
            wet = wet_of(levels[rows, :].astype(F32), k)
            here = density(ocean[0, k, rows, :], ocean[1, k, rows, :], wet)
            total = cum[rows, :] + here
            cum[rows, :] = total
            pressure.append(THICKNESS * (total - 0.5 * here))
            here = density(halo_of(0, rows), halo_of(1, rows), wet_of(lev_halo[rows, :], k))
            total = cum_halo[rows, :] + here
            cum_halo[rows, :] = total
            pressure_halo.append(THICKNESS * (total - 0.5 * here))
        for b in range(BLOCKS):
            rows = pl.ds(8 * b, 8)
            wet = wet_of(levels[rows, :].astype(F32), k)
            grad_lon = 0.5 * (
                next_lon(pressure[b], pressure_halo[b], 1) - next_lon(pressure[b], pressure_halo[b], -1)
            )
            ahead = pressure[b] if b == BLOCKS - 1 else jnp.where(sub == 0, pressure[b + 1], pressure[b])
            behind = pressure[b] if b == 0 else jnp.where(sub == 7, pressure[b - 1], pressure[b])
            grad_lat = 0.5 * (roll(ahead, -1, 0) - roll(behind, 1, 0))
            if b == 0:
                grad_lat = jnp.where(sub >= 1, grad_lat, 0.0)
            if b == BLOCKS - 1:
                grad_lat = jnp.where(sub <= 6, grad_lat, 0.0)
            u, v, turn = ocean[2, k, rows, :], ocean[3, k, rows, :], coriolis[rows, :]
            accel_u = wet * (turn * v - grad_lon - advection[0, b])
            accel_v = wet * (-turn * u - grad_lat - advection[1, b])
            accel[0, k, rows, :] = accel_u
            accel[1, k, rows, :] = accel_v
            sums[0, rows, :] += accel_u
            sums[1, rows, :] += accel_v
            sums[2, rows, :] += wet * u
            sums[3, rows, :] += wet * v
        return carry

    lax.fori_loop(0, LEVELS, level, 0)
    flat = [sums.at[0], sums.at[1], surface.at[0], surface.at[1], surface.at[2], levels]
    for n, field in enumerate(flat):
        send(2 * LEVELS + n, field[first, :].astype(F32), field[last_rows, :].astype(F32))


def tracer_kernel(ocean, levels, own, low, high, tracers, west_flux, packed, lev_halo):
    west_faces(own, low, levels, (0, 1), ((0, 1, 2), packed, high), west_flux)
    for b in range(BLOCKS):
        rows = pl.ds(8 * b, 8)
        lev_halo[rows, :] = roll(halo_pack(4, rows, low, high), -4, 1)

    def level(k, carry):
        unplace = 124 - 8 * k
        halo = {}

        def halo_of(q, rows):
            key = (q, rows.start)
            if key not in halo:
                halo[key] = pltpu.roll(packed[q, rows, :], unplace, 1)
            return halo[key]

        advection = tile_divergence(ocean, levels, k, halo_of, lev_halo, (0, 1), west_flux)
        for b in range(BLOCKS):
            rows = pl.ds(8 * b, 8)
            wet = wet_of(levels[rows, :].astype(F32), k)
            for n in range(2):
                tracers[n, k, rows, :] = wet * (ocean[n, k, rows, :] - TRACER_STEP * advection[n, b])
        return carry

    lax.fori_loop(0, LEVELS, level, 0)


def window(low_block, high_block, d):
    if d == 8:
        return high_block
    return roll(jnp.where(row_index() >= d, low_block, high_block), -d, 0)


def edge_blocks(ocean, arrived, q, k, side):
    own = ocean[q, k, pl.ds(0 if side == 0 else ROWS - 8, 8), :]
    piece = arrived[(q % 2) * LEVELS + k]
    if side == 0:
        return (roll(piece, 5, 0) if q < 2 else piece), own
    return own, (roll(piece, 3, 0) if q < 2 else piece)


def edge_levels(levels, arrived, side):
    own = levels[pl.ds(0 if side == 0 else ROWS - 8, 8), :].astype(F32)
    return (arrived[PIECES - 1], own) if side == 0 else (own, arrived[PIECES - 1])


def edge_terms(ocean, k, arrived, side, lev5, lev6, quantities):
    sub = row_index()
    v = edge_blocks(ocean, arrived, 3, k, side)
    speed = 0.5 * (window(*v, 5) + window(*v, 6)) * wet_of(jnp.minimum(lev5, lev6), k)
    terms = []
    for q in quantities:
        x = v if q == 3 else edge_blocks(ocean, arrived, q, k, side)
        flux = upwind_flux(speed, *[window(*x, d) for d in (3, 4, 5, 6, 7, 8)])
        flux = jnp.where(sub < 5, flux, 0.0)
        terms.append(flux - jnp.where(sub == 0, 0.0, roll(flux, 1, 0)))
    return terms


def own_rows(term, side):
    sub = row_index()
    if side == 0:
        return jnp.where(sub < 3, roll(term, -3, 0), 0.0)
    return jnp.where(sub >= 5, roll(term, 5, 0), 0.0)


def halo_rows(term, side):
    sub = row_index()
    if side == 0:
        return jnp.where(sub >= 5, roll(term, 5, 0), 0.0)
    return jnp.where(sub < 3, roll(term, -3, 0), 0.0)


def edge_kernel(ocean, levels, surface, sums, south, north, edges, fields, packed, means, cum, total):
    sub = row_index()
    cum[...] = jnp.zeros_like(cum)
    total[...] = jnp.zeros_like(total)
    arrived = (south, north)

    def level(k, carry):
        for side in range(2):
            lev = edge_levels(levels, arrived[side], side)
            lev5, lev6 = window(*lev, 5), window(*lev, 6)
            terms = edge_terms(ocean, k, arrived[side], side, lev5, lev6, (2, 3))
            t = edge_blocks(ocean, arrived[side], 0, k, side)
            s = edge_blocks(ocean, arrived[side], 1, k, side)
            pressure = []
            for half in range(2):
                here = density(t[half], s[half], wet_of(lev[half], k))
                column = cum[side, half] + here
                cum[side, half] = column
                pressure.append(THICKNESS * (column - 0.5 * here))
            grad = 0.5 * (window(*pressure, 6) - window(*pressure, 4))
            grad = jnp.where((sub == 2) | (sub == 3), grad, 0.0)
            wet = wet_of(lev5, k)
            for n, term in enumerate((-wet * terms[0], -wet * (terms[1] + grad))):
                total[side, n] += term
                edges[side, n, k] = own_rows(term, side)
        return carry

    lax.fori_loop(0, LEVELS, level, 0)
    rim = ROWS + 16
    own = pl.ds(8, ROWS)
    for n in range(3):
        fields[n, pl.ds(0, 8), :] = south[2 * LEVELS + 2 + n]
        fields[n, own, :] = surface[n]
        fields[n, pl.ds(rim - 8, 8), :] = north[2 * LEVELS + 2 + n]
    fields[3, pl.ds(0, 8), :] = south[PIECES - 1]
    fields[3, own, :] = levels[...].astype(F32)
    fields[3, pl.ds(rim - 8, 8), :] = north[PIECES - 1]
    for n in range(2):
        fields[4 + n, pl.ds(0, 8), :] = south[2 * LEVELS + n] + halo_rows(total[0, n], 0)
        fields[4 + n, own, :] = sums[n]
        fields[4 + n, pl.ds(8, 8), :] += own_rows(total[0, n], 0)
        fields[4 + n, pl.ds(ROWS, 8), :] += own_rows(total[1, n], 1)
        fields[4 + n, pl.ds(rim - 8, 8), :] = north[2 * LEVELS + n] + halo_rows(total[1, n], 1)
    for n in range(2):
        safe = jnp.maximum(THICKNESS * levels[...].astype(F32), THICKNESS)
        means[n] = THICKNESS * (sums[2 + n] + TRACER_STEP * fields[4 + n, own, :]) / safe
    for b in range(rim // 8):
        rows = pl.ds(8 * b, 8)
        safe = jnp.maximum(THICKNESS * fields[3, rows, :], THICKNESS)
        group = lane_index() // 16
        out = jnp.zeros((8, COLS), F32)
        for n in range(6):
            if n >= 4:
                fields[n, rows, :] = THICKNESS * fields[n, rows, :] / safe
            out = jnp.where(group == n, roll(fields[n, rows, :], 16 * n + 8, 1), out)
        packed[rows, :] = out


def tracer_edge_kernel(ocean, levels, south, north, edges):
    arrived = (south, north)

    def level(k, carry):
        for side in range(2):
            lev = edge_levels(levels, arrived[side], side)
            lev5, lev6 = window(*lev, 5), window(*lev, 6)
            wet = wet_of(lev5, k)
            terms = edge_terms(ocean, k, arrived[side], side, lev5, lev6, (0, 1))
            for n in range(2):
                edges[side, n, k] = own_rows(-wet * terms[n], side)
        return carry

    lax.fori_loop(0, LEVELS, level, 0)


def final_kernel(
    ocean, levels, accel, tracers, edges, tracer_edges, fields, means, low, high, ocean_out, surface_out, shift,
):
    rim = ROWS + 16
    lane = lane_index(rim)
    halos = jnp.where(lane % 16 < 8, low[...], high[...])
    both = []
    for n in range(6):
        both.append((fields[n], roll(halos, -(16 * n + 8), 1)))
    height, mean_u, mean_v, level_map, force_lon, force_lat = both
    depth = tuple(THICKNESS * x for x in level_map)
    sea = tuple(jnp.where(x > 0.0, 1.0, 0.0) for x in level_map)

    def d_lon(x):
        main, halo = x
        result = []
        for here, other in ((main, halo), (halo, main)):
            ahead = roll(jnp.where(lane == 0, other, here), -1, 1)
            behind = roll(jnp.where(lane == COLS - 1, other, here), 1, 1)
            result.append(0.5 * (ahead - behind))
        return result

    def d_lat(x):
        return [0.5 * (roll(part, -1, 0) - roll(part, 1, 0)) for part in x]

    def times(x, y):
        return [p * q for p, q in zip(x, y)]

    for _ in range(NSUB):
        along, across = d_lon(times(depth, mean_u)), d_lat(times(depth, mean_v))
        height = [s * (h - SURFACE_STEP * (p + q)) for s, h, p, q in zip(sea, height, along, across)]
        mean_u = [
            s * (m + SURFACE_STEP * (f - d)) for s, m, f, d in zip(sea, mean_u, force_lon, d_lon(height))
        ]
        mean_v = [
            s * (m + SURFACE_STEP * (f - d)) for s, m, f, d in zip(sea, mean_v, force_lat, d_lat(height))
        ]
    for n, field in enumerate((height, mean_u, mean_v)):
        surface_out[n] = field[0][8 : 8 + ROWS]
    shift[0] = mean_u[0][8 : 8 + ROWS] - means[0]
    shift[1] = mean_v[0][8 : 8 + ROWS] - means[1]

    def level(k, carry):
        wet = wet_of(levels[...].astype(F32), k)
        for n in range(2):
            ocean_out[n, k] = tracers[n, k]
            ocean_out[2 + n, k] = wet * (ocean[2 + n, k] + TRACER_STEP * accel[n, k] + shift[n])
            for side, rows in enumerate((pl.ds(0, 8), pl.ds(ROWS - 8, 8))):
                ocean_out[n, k, rows, :] += TRACER_STEP * tracer_edges[side, n, k]
                ocean_out[2 + n, k, rows, :] += TRACER_STEP * edges[side, n, k]
        return carry

    lax.fori_loop(0, LEVELS, level, 0)


def lon_ring(step):
    count = lax.axis_size("lon")
    return [(i, (i + step) % count) for i in range(count)]


def fold_path(backward):
    lon_count = lax.axis_size("lon")
    lat_count = lax.axis_size("lat")
    pairs = []
    for p in range(lon_count // 2):
        q = lon_count - 1 - p
        path = [p * lat_count + r for r in range(lat_count)]
        path += [q * lat_count + r for r in reversed(range(lat_count))]
        pairs += list(zip(path[:-1], path[1:]))
    return [(t, s) for s, t in pairs] if backward else pairs


def north_signs():
    signs = np.ones((PIECES, 8, 1), np.float32)
    signs[: 2 * LEVELS, :5] = -1.0
    for n in (0, 1, 3, 4):
        signs[2 * LEVELS + n] = -1.0
    return signs


def call(kernel, outs, scratch=(), scalars=0, operands=1, cost=1000000):
    def vmem():
        return pl.BlockSpec(memory_space=pltpu.VMEM)

    specs = [pl.BlockSpec(memory_space=pltpu.SMEM)] * scalars + [vmem()] * operands
    single = len(outs) == 1
    shapes = [jax.ShapeDtypeStruct(shape, F32) for shape in outs]
    return pl.pallas_call(
        kernel,
        out_shape=shapes[0] if single else shapes,
        in_specs=specs,
        out_specs=vmem() if single else [vmem() for _ in outs],
        scratch_shapes=[pltpu.VMEM(shape, F32) for shape in scratch],
        cost_estimate=pl.CostEstimate(flops=cost, bytes_accessed=cost, transcendentals=0),
    )


def on_device(ocean, surface, levels):
    tile = (ROWS, COLS)
    rim = (ROWS + 16, COLS)
    own = call(pack_kernel, [(5, *tile)], operands=2)(ocean, levels)
    low = lax.ppermute(own, "lon", lon_ring(1))
    high = lax.ppermute(own, "lon", lon_ring(-1))
    lat_index, lat_count = lax.axis_index("lat"), lax.axis_size("lat")
    west_half = lax.axis_index("lon") < lax.axis_size("lon") // 2
    row = lat_index * ROWS + jnp.arange(ROWS, dtype=jnp.int32)
    latitude = (row.astype(F32) + 0.5) / float(lat_count * ROWS)
    coriolis = jnp.sin(math.pi * latitude - 0.5 * math.pi)
    coriolis = jnp.broadcast_to(coriolis[:, None], tile)
    accel, up, down, sums = call(
        momentum_kernel,
        [(2, LEVELS, *tile), (PIECES, 8, COLS), (PIECES, 8, COLS), (4, *tile)],
        scratch=[(2, *tile), (4, *tile), tile, tile, tile],
        scalars=1,
        operands=7,
    )(west_half.astype(jnp.int32).reshape(1), ocean, levels, surface, coriolis, own, low, high)
    up = lax.ppermute(up, ("lon", "lat"), fold_path(False))
    down = lax.ppermute(down, ("lon", "lat"), fold_path(True))
    tracers = call(
        tracer_kernel, [(2, LEVELS, *tile)], scratch=[(2, *tile), (3, *tile), tile], operands=5, cost=100000000
    )(ocean, levels, own, low, high)
    south = jnp.where(lat_index == 0, 0.0, jnp.where(west_half, up, down))
    north = jnp.where(west_half, down, up)
    north = jnp.where(lat_index == lat_count - 1, jnp.flip(north, axis=(1, 2)) * north_signs(), north)
    edges, fields, packed, means = call(
        edge_kernel,
        [(2, 2, LEVELS, 8, COLS), (6, *rim), rim, (2, *tile)],
        scratch=[(2, 2, 8, COLS), (2, 2, 8, COLS)],
        operands=6,
    )(ocean, levels, surface, sums, south, north)
    west = lax.ppermute(packed, "lon", lon_ring(1))
    east = lax.ppermute(packed, "lon", lon_ring(-1))
    tracer_edges = call(tracer_edge_kernel, [(2, 2, LEVELS, 8, COLS)], operands=4)(ocean, levels, south, north)
    return call(final_kernel, [(4, LEVELS, *tile), (3, *tile)], scratch=[(2, *tile)], operands=10)(
        ocean, levels, accel, tracers, edges, tracer_edges, fields, means, west, east
    )


def solution(mesh):
    return jax.shard_map(
        on_device,
        mesh=mesh,
        in_specs=(P(None, None, "lat", "lon"), P(None, "lat", "lon"), P("lat", "lon")),
        out_specs=(P(None, None, "lat", "lon"), P(None, "lat", "lon")),
        check_vma=False,
    )
```

```python
import functools
import math

import jax
import jax.numpy as jnp
from jax import lax
from jax.experimental import pallas as pl
from jax.experimental.pallas import tpu as pltpu
from jax.sharding import PartitionSpec as P

NSUB = 4
LEVELS = 16
ROWS = 32
COLS = 128
BLOCKS = ROWS // 8
THICKNESS = 1.0 / LEVELS
TRACER_STEP = 0.1
SURFACE_STEP = 1.2
PIECES = 2 * LEVELS + 6

F32 = jnp.float32


def lane_index(rows=8):
    return lax.broadcasted_iota(jnp.int32, (rows, COLS), 1)


def row_index(rows=8):
    return lax.broadcasted_iota(jnp.int32, (rows, COLS), 0)


def roll(x, shift, axis):
    if isinstance(shift, int):
        shift %= x.shape[axis]
        if shift == 0:
            return x
    return pltpu.roll(x, shift, axis)


def upwind_flux(speed, qm2, qm1, q0, q1, q2, q3):
    ahead = speed >= 0.0
    a = jnp.where(ahead, qm2, q3)
    b = jnp.where(ahead, qm1, q2)
    c = jnp.where(ahead, q0, q1)
    d = jnp.where(ahead, q1, q0)
    e = jnp.where(ahead, q2, qm1)
    ab = a - b
    bc = b - c
    cd = c - d
    de = d - e
    x1 = ab - bc
    y1 = ab - 3.0 * bc
    x2 = bc - cd
    y2 = bc + cd
    x3 = cd - de
    y3 = 3.0 * cd - de
    third = 13.0 / 3.0
    s1 = third * (x1 * x1) + (y1 * y1 + 4e-6)
    s2 = third * (x2 * x2) + (y2 * y2 + 4e-6)
    s3 = third * (x3 * x3) + (y3 * y3 + 4e-6)
    r1 = s2 * s3
    r2 = s1 * s3
    r3 = s1 * s2
    w1 = r1 * r1
    w2 = 6.0 * (r2 * r2)
    w3 = 3.0 * (r3 * r3)
    top = w1 * (2.0 * ab - 5.0 * bc) - w2 * (bc + 2.0 * cd) + w3 * (de - 4.0 * cd)
    low = 6.0 * (w1 + w2 + w3)
    return speed * (c + top / low)


def density(t, s, wet):
    return wet * (t * (0.03 * s - 0.2 - 0.05 * t) + 0.8 * s)


def wet_of(level_map, k):
    return jnp.where(level_map > k, 1.0, 0.0).astype(F32)


def pack_kernel(ocean, levels, out):
    group = lane_index() // 8
    for b in range(BLOCKS):
        rows = pl.ds(8 * b, 8)
        for q in range(4):

            def place(k, packed, q=q, rows=rows):
                moved = pltpu.roll(ocean[q, k, rows, :], 8 * k + 4, 1)
                return jnp.where(group == k, moved, packed)

            packed = jnp.zeros((8, COLS), F32)
            for k in range(LEVELS):
                packed = place(k, packed)
            out[q, rows, :] = packed
        out[4, rows, :] = roll(levels[rows, :].astype(F32), 4, 1)


def halo_pack(q, rows, low, high):
    from_low = lane_index() % 8 < 4
    return jnp.where(from_low, low[q, rows, :], high[q, rows, :])


def next_lon(main, halo, step):
    lane = lane_index()
    if step > 0:
        return roll(jnp.where(lane < step, halo, main), -step, 1)
    return roll(jnp.where(lane >= COLS + step, halo, main), -step, 1)


def lon_shifts(main, halo):
    return [main if d == 0 else next_lon(main, halo, d) for d in (-2, -1, 0, 1, 2, 3)]


def west_faces(own, low, levels, quantities, halos, west_flux):
    lane = lane_index()
    from_low = lane % 8 < 4
    level_of = lane // 8
    for b in range(BLOCKS):
        rows = pl.ds(8 * b, 8)
        lev = levels[rows, :].astype(F32)
        own_col = lev[:, 0:1]
        west_col = low[4, rows, :][:, 3:4]
        both = jnp.minimum(own_col, west_col)
        wet = jnp.where(both > level_of.astype(F32), 1.0, 0.0)
        u = jnp.where(from_low, low[2, rows, :], own[2, rows, :])
        speed = 0.5 * (u + roll(u, -1, 1)) * wet
        for n, q in enumerate(quantities):
            x = jnp.where(from_low, low[q, rows, :], own[q, rows, :])
            west_flux[n, rows, :] = upwind_flux(speed, *[roll(x, -d, 1) for d in (-2, -1, 0, 1, 2, 3)])
        for n, q in enumerate(halos[0]):
            halos[1][n, rows, :] = halo_pack(q, rows, low, halos[2])


def lat_shift(ocean, q, k, b, d):
    start = 8 * b + d
    if 0 <= start and start + 8 <= ROWS:
        return ocean[q, k, start : start + 8, :]
    return roll(ocean[q, k, pl.ds(8 * b, 8), :], -d, 0)


def level_map_shift(levels, b, d):
    start = 8 * b + d
    if 0 <= start and start + 8 <= ROWS:
        return levels[start : start + 8, :].astype(F32)
    return roll(levels[pl.ds(8 * b, 8), :].astype(F32), -d, 0)


def tile_divergence(ocean, levels, k, halo_of, lev_halo, quantities, west_flux):
    lane = lane_index()
    sub = row_index()
    unplace = 124 - 8 * k
    result = {}
    last = {}
    for b in range(BLOCKS):
        rows = pl.ds(8 * b, 8)
        lev = levels[rows, :].astype(F32)
        wet = wet_of(lev, k)
        u = ocean[2, k, rows, :]
        wet_east = wet_of(next_lon(lev, lev_halo[rows, :], 1), k)
        speed_lon = 0.5 * (u + next_lon(u, halo_of(2, rows), 1)) * (wet * wet_east)
        wet_north = wet_of(level_map_shift(levels, b, 1), k)
        speed_lat = 0.5 * (ocean[3, k, rows, :] + lat_shift(ocean, 3, k, b, 1)) * (wet * wet_north)
        for n, q in enumerate(quantities):
            main = ocean[q, k, rows, :]
            east = upwind_flux(speed_lon, *lon_shifts(main, halo_of(q, rows)))
            west = pltpu.roll(west_flux[n, rows, :], unplace, 1)
            west = roll(jnp.where(lane == COLS - 1, west, east), 1, 1)
            north = upwind_flux(speed_lat, *[lat_shift(ocean, q, k, b, d) for d in (-2, -1, 0, 1, 2, 3)])
            if b == 0:
                north = jnp.where(sub >= 2, north, 0.0)
            if b == BLOCKS - 1:
                north = jnp.where(sub <= 4, north, 0.0)
            rolled = roll(north, 1, 0)
            south = jnp.where(sub == 0, last[n] if b else 0.0, rolled)
            last[n] = rolled
            result[n, b] = (east - west) + (north - south)
    return result


def momentum_kernel(
    flags, ocean, levels, surface, coriolis, own, low, high,
    accel, up, down, sums, west_flux, packed, cum, cum_halo, lev_halo,
):
    sub = row_index()
    west_half = flags[0] == 1
    west_faces(own, low, levels, (2, 3), ((0, 1, 2, 3), packed, high), west_flux)
    for b in range(BLOCKS):
        rows = pl.ds(8 * b, 8)
        lev_halo[rows, :] = roll(halo_pack(4, rows, low, high), -4, 1)
    cum[...] = jnp.zeros_like(cum)
    cum_halo[...] = jnp.zeros_like(cum_halo)
    sums[...] = jnp.zeros_like(sums)

    def send(index, south, north):
        up[index] = jnp.where(west_half, north, south)
        down[index] = jnp.where(west_half, south, north)

    first, last_rows = pl.ds(0, 8), pl.ds(ROWS - 8, 8)

    def level(k, carry):
        unplace = 124 - 8 * k
        halo = {}

        def halo_of(q, rows):
            key = (q, rows.start)
            if key not in halo:
                halo[key] = pltpu.roll(packed[q, rows, :], unplace, 1)
            return halo[key]

        for pair in range(2):
            t0, t3 = ocean[pair, k, first, :], ocean[pair, k, last_rows, :]
            u0, u3 = ocean[pair + 2, k, first, :], ocean[pair + 2, k, last_rows, :]
            send(
                pair * LEVELS + k,
                jnp.where(sub < 5, u0, roll(t0, 5, 0)),
                jnp.where(sub < 3, roll(t3, 3, 0), u3),
            )
        advection = tile_divergence(ocean, levels, k, halo_of, lev_halo, (2, 3), west_flux)
        pressure, pressure_halo = [], []
        for b in range(BLOCKS):
            rows = pl.ds(8 * b, 8)
            wet = wet_of(levels[rows, :].astype(F32), k)
            here = density(ocean[0, k, rows, :], ocean[1, k, rows, :], wet)
            total = cum[rows, :] + here
            cum[rows, :] = total
            pressure.append(THICKNESS * (total - 0.5 * here))
            here = density(halo_of(0, rows), halo_of(1, rows), wet_of(lev_halo[rows, :], k))
            total = cum_halo[rows, :] + here
            cum_halo[rows, :] = total
            pressure_halo.append(THICKNESS * (total - 0.5 * here))
        for b in range(BLOCKS):
            rows = pl.ds(8 * b, 8)
            wet = wet_of(levels[rows, :].astype(F32), k)
            grad_lon = 0.5 * (
                next_lon(pressure[b], pressure_halo[b], 1) - next_lon(pressure[b], pressure_halo[b], -1)
            )
            ahead = pressure[b] if b == BLOCKS - 1 else jnp.where(sub == 0, pressure[b + 1], pressure[b])
            behind = pressure[b] if b == 0 else jnp.where(sub == 7, pressure[b - 1], pressure[b])
            grad_lat = 0.5 * (roll(ahead, -1, 0) - roll(behind, 1, 0))
            if b == 0:
                grad_lat = jnp.where(sub >= 1, grad_lat, 0.0)
            if b == BLOCKS - 1:
                grad_lat = jnp.where(sub <= 6, grad_lat, 0.0)
            u, v, turn = ocean[2, k, rows, :], ocean[3, k, rows, :], coriolis[rows, :]
            accel_u = wet * (turn * v - grad_lon - advection[0, b])
            accel_v = wet * (-turn * u - grad_lat - advection[1, b])
            accel[0, k, rows, :] = accel_u
            accel[1, k, rows, :] = accel_v
            sums[0, rows, :] += accel_u
            sums[1, rows, :] += accel_v
            sums[2, rows, :] += wet * u
            sums[3, rows, :] += wet * v
        return carry

    lax.fori_loop(0, LEVELS, level, 0)
    flat = [sums.at[0], sums.at[1], surface.at[0], surface.at[1], surface.at[2], levels]
    for n, field in enumerate(flat):
        send(2 * LEVELS + n, field[first, :].astype(F32), field[last_rows, :].astype(F32))


def tracer_kernel(ocean, levels, own, low, high, after, tracers, west_flux, packed, lev_halo):
    del after
    west_faces(own, low, levels, (0, 1), ((0, 1, 2), packed, high), west_flux)
    for b in range(BLOCKS):
        rows = pl.ds(8 * b, 8)
        lev_halo[rows, :] = roll(halo_pack(4, rows, low, high), -4, 1)

    def level(k, carry):
        unplace = 124 - 8 * k
        halo = {}

        def halo_of(q, rows):
            key = (q, rows.start)
            if key not in halo:
                halo[key] = pltpu.roll(packed[q, rows, :], unplace, 1)
            return halo[key]

        advection = tile_divergence(ocean, levels, k, halo_of, lev_halo, (0, 1), west_flux)
        for b in range(BLOCKS):
            rows = pl.ds(8 * b, 8)
            wet = wet_of(levels[rows, :].astype(F32), k)
            for n in range(2):
                tracers[n, k, rows, :] = wet * (ocean[n, k, rows, :] - TRACER_STEP * advection[n, b])
        return carry

    lax.fori_loop(0, LEVELS, level, 0)


def window(low_block, high_block, d):
    if d == 8:
        return high_block
    return roll(jnp.where(row_index() >= d, low_block, high_block), -d, 0)


def edge_blocks(ocean, arrived, q, k, side):
    own = ocean[q, k, pl.ds(0 if side == 0 else ROWS - 8, 8), :]
    piece = arrived[(q % 2) * LEVELS + k]
    if side == 0:
        return (roll(piece, 5, 0) if q < 2 else piece), own
    return own, (roll(piece, 3, 0) if q < 2 else piece)


def edge_levels(levels, arrived, side):
    own = levels[pl.ds(0 if side == 0 else ROWS - 8, 8), :].astype(F32)
    return (arrived[PIECES - 1], own) if side == 0 else (own, arrived[PIECES - 1])


def edge_terms(ocean, k, arrived, side, lev5, lev6, quantities):
    sub = row_index()
    v = edge_blocks(ocean, arrived, 3, k, side)
    speed = 0.5 * (window(*v, 5) + window(*v, 6)) * wet_of(jnp.minimum(lev5, lev6), k)
    terms = []
    for q in quantities:
        x = v if q == 3 else edge_blocks(ocean, arrived, q, k, side)
        flux = upwind_flux(speed, *[window(*x, d) for d in (3, 4, 5, 6, 7, 8)])
        flux = jnp.where(sub < 5, flux, 0.0)
        terms.append(flux - jnp.where(sub == 0, 0.0, roll(flux, 1, 0)))
    return terms


def own_rows(term, side):
    sub = row_index()
    if side == 0:
        return jnp.where(sub < 3, roll(term, -3, 0), 0.0)
    return jnp.where(sub >= 5, roll(term, 5, 0), 0.0)


def halo_rows(term, side):
    sub = row_index()
    if side == 0:
        return jnp.where(sub >= 5, roll(term, 5, 0), 0.0)
    return jnp.where(sub < 3, roll(term, -3, 0), 0.0)


def place_arrivals(flags, up, down, south, north):
    west_half = flags[0] == 1
    at_south = flags[1] == 1
    turned_row, turned_lane = 7 - row_index(), COLS - 1 - lane_index()
    pair_sign = jnp.where(row_index() < 5, -1.0, 1.0)

    def piece(n, sign):
        south[n] = jnp.where(at_south, 0.0, jnp.where(west_half, up[n], down[n]))
        here = jnp.where(west_half, down[n], up[n])

        @pl.when(flags[2] == 1)
        def _():
            turned = jnp.take_along_axis(jnp.take_along_axis(here, turned_lane, axis=1), turned_row, axis=0)
            north[n] = turned * sign

        @pl.when(flags[2] == 0)
        def _():
            north[n] = here

    def pair(n, carry):
        piece(n, pair_sign)
        return carry

    lax.fori_loop(0, 2 * LEVELS, pair, 0)
    for n, sign in enumerate((-1.0, -1.0, 1.0, -1.0, -1.0, 1.0)):
        piece(2 * LEVELS + n, sign)


def edge_kernel(
    flags, ocean, levels, surface, sums, up, down, after,
    edges, fields, packed, means, south, north, cum, total,
):
    del after
    place_arrivals(flags, up, down, south, north)
    sub = row_index()
    cum[...] = jnp.zeros_like(cum)
    total[...] = jnp.zeros_like(total)
    arrived = (south, north)

    def level(k, carry):
        for side in range(2):
            lev = edge_levels(levels, arrived[side], side)
            lev5, lev6 = window(*lev, 5), window(*lev, 6)
            terms = edge_terms(ocean, k, arrived[side], side, lev5, lev6, (2, 3))
            t = edge_blocks(ocean, arrived[side], 0, k, side)
            s = edge_blocks(ocean, arrived[side], 1, k, side)
            pressure = []
            for half in range(2):
                here = density(t[half], s[half], wet_of(lev[half], k))
                column = cum[side, half] + here
                cum[side, half] = column
                pressure.append(THICKNESS * (column - 0.5 * here))
            grad = 0.5 * (window(*pressure, 6) - window(*pressure, 4))
            grad = jnp.where((sub == 2) | (sub == 3), grad, 0.0)
            wet = wet_of(lev5, k)
            for n, term in enumerate((-wet * terms[0], -wet * (terms[1] + grad))):
                total[side, n] += term
                edges[side, n, k] = own_rows(term, side)
        return carry

    lax.fori_loop(0, LEVELS, level, 0)
    rim = ROWS + 16
    own = pl.ds(8, ROWS)
    for n in range(3):
        fields[n, pl.ds(0, 8), :] = south[2 * LEVELS + 2 + n]
        fields[n, own, :] = surface[n]
        fields[n, pl.ds(rim - 8, 8), :] = north[2 * LEVELS + 2 + n]
    fields[3, pl.ds(0, 8), :] = south[PIECES - 1]
    fields[3, own, :] = levels[...].astype(F32)
    fields[3, pl.ds(rim - 8, 8), :] = north[PIECES - 1]
    for n in range(2):
        fields[4 + n, pl.ds(0, 8), :] = south[2 * LEVELS + n] + halo_rows(total[0, n], 0)
        fields[4 + n, own, :] = sums[n]
        fields[4 + n, pl.ds(8, 8), :] += own_rows(total[0, n], 0)
        fields[4 + n, pl.ds(ROWS, 8), :] += own_rows(total[1, n], 1)
        fields[4 + n, pl.ds(rim - 8, 8), :] = north[2 * LEVELS + n] + halo_rows(total[1, n], 1)
    for n in range(2):
        safe = jnp.maximum(THICKNESS * levels[...].astype(F32), THICKNESS)
        means[n] = THICKNESS * (sums[2 + n] + TRACER_STEP * fields[4 + n, own, :]) / safe
    for b in range(rim // 8):
        rows = pl.ds(8 * b, 8)
        safe = jnp.maximum(THICKNESS * fields[3, rows, :], THICKNESS)
        group = lane_index() // 16
        out = jnp.zeros((8, COLS), F32)
        for n in range(6):
            if n >= 4:
                fields[n, rows, :] = THICKNESS * fields[n, rows, :] / safe
            out = jnp.where(group == n, roll(fields[n, rows, :], 16 * n + 8, 1), out)
        packed[rows, :] = out


def tracer_edge_kernel(ocean, levels, south, north, edges):
    arrived = (south, north)

    def level(k, carry):
        for side in range(2):
            lev = edge_levels(levels, arrived[side], side)
            lev5, lev6 = window(*lev, 5), window(*lev, 6)
            wet = wet_of(lev5, k)
            terms = edge_terms(ocean, k, arrived[side], side, lev5, lev6, (0, 1))
            for n in range(2):
                edges[side, n, k] = own_rows(-wet * terms[n], side)
        return carry

    lax.fori_loop(0, LEVELS, level, 0)


def final_kernel(
    ocean, levels, accel, tracers, edges, tracer_edges, fields, means, low, high, ocean_out, surface_out, shift,
):
    rim = ROWS + 16
    lane = lane_index(rim)
    halos = jnp.where(lane % 16 < 8, low[...], high[...])
    both = []
    for n in range(6):
        both.append((fields[n], roll(halos, -(16 * n + 8), 1)))
    height, mean_u, mean_v, level_map, force_lon, force_lat = both
    depth = tuple(THICKNESS * x for x in level_map)
    sea = tuple(jnp.where(x > 0.0, 1.0, 0.0) for x in level_map)

    def d_lon(x):
        main, halo = x
        result = []
        for here, other in ((main, halo), (halo, main)):
            ahead = roll(jnp.where(lane == 0, other, here), -1, 1)
            behind = roll(jnp.where(lane == COLS - 1, other, here), 1, 1)
            result.append(0.5 * (ahead - behind))
        return result

    def d_lat(x):
        return [0.5 * (roll(part, -1, 0) - roll(part, 1, 0)) for part in x]

    def times(x, y):
        return [p * q for p, q in zip(x, y)]

    for _ in range(NSUB):
        along, across = d_lon(times(depth, mean_u)), d_lat(times(depth, mean_v))
        height = [s * (h - SURFACE_STEP * (p + q)) for s, h, p, q in zip(sea, height, along, across)]
        mean_u = [
            s * (m + SURFACE_STEP * (f - d)) for s, m, f, d in zip(sea, mean_u, force_lon, d_lon(height))
        ]
        mean_v = [
            s * (m + SURFACE_STEP * (f - d)) for s, m, f, d in zip(sea, mean_v, force_lat, d_lat(height))
        ]
    for n, field in enumerate((height, mean_u, mean_v)):
        surface_out[n] = field[0][8 : 8 + ROWS]
    shift[0] = mean_u[0][8 : 8 + ROWS] - means[0]
    shift[1] = mean_v[0][8 : 8 + ROWS] - means[1]

    def level(k, carry):
        for b in range(BLOCKS):
            rows = pl.ds(8 * b, 8)
            wet = wet_of(levels[rows, :].astype(F32), k)
            for n in range(2):
                tracer, force = tracers[n, k, rows, :], accel[n, k, rows, :]
                if b in (0, BLOCKS - 1):
                    side = min(b, 1)
                    tracer = tracer + TRACER_STEP * tracer_edges[side, n, k]
                    force = force + edges[side, n, k]
                ocean_out[n, k, rows, :] = tracer
                ocean_out[2 + n, k, rows, :] = wet * (
                    ocean[2 + n, k, rows, :] + TRACER_STEP * force + shift[n, rows, :]
                )
        return carry

    lax.fori_loop(0, LEVELS, level, 0)


def lon_ring(step):
    count = lax.axis_size("lon")
    return [(i, (i + step) % count) for i in range(count)]


def fold_path(backward):
    lon_count = lax.axis_size("lon")
    lat_count = lax.axis_size("lat")
    pairs = []
    for p in range(lon_count // 2):
        q = lon_count - 1 - p
        path = [p * lat_count + r for r in range(lat_count)]
        path += [q * lat_count + r for r in reversed(range(lat_count))]
        pairs += list(zip(path[:-1], path[1:]))
    return [(t, s) for s, t in pairs] if backward else pairs


def call(kernel, outs, scratch=(), scalars=0, operands=1, unread=0, cost=1000000, limit=16):
    def vmem():
        return pl.BlockSpec(memory_space=pltpu.VMEM)

    specs = [pl.BlockSpec(memory_space=pltpu.SMEM)] * scalars + [vmem()] * operands
    specs += [pl.BlockSpec(memory_space=pl.ANY)] * unread
    single = len(outs) == 1
    shapes = [jax.ShapeDtypeStruct(shape, F32) for shape in outs]
    return pl.pallas_call(
        kernel,
        out_shape=shapes[0] if single else shapes,
        in_specs=specs,
        out_specs=vmem() if single else [vmem() for _ in outs],
        scratch_shapes=[pltpu.VMEM(shape, F32) for shape in scratch],
        cost_estimate=pl.CostEstimate(flops=cost, bytes_accessed=cost, transcendentals=0),
        compiler_params=pltpu.CompilerParams(vmem_limit_bytes=limit << 20),
    )


def on_device(ocean, surface, levels):
    tile = (ROWS, COLS)
    rim = (ROWS + 16, COLS)
    own = call(pack_kernel, [(5, *tile)], operands=2)(ocean, levels)
    low = lax.ppermute(own, "lon", lon_ring(1))
    high = lax.ppermute(own, "lon", lon_ring(-1))
    lat_index, lat_count = lax.axis_index("lat"), lax.axis_size("lat")
    west_half = lax.axis_index("lon") < lax.axis_size("lon") // 2
    row = lat_index * ROWS + lax.broadcasted_iota(jnp.int32, tile, 0)
    latitude = (row.astype(F32) + 0.5) / float(lat_count * ROWS)
    coriolis = jnp.sin(math.pi * latitude - 0.5 * math.pi)
    flags = jnp.stack([west_half, lat_index == 0, lat_index == lat_count - 1]).astype(jnp.int32)
    accel, up, down, sums = call(
        momentum_kernel,
        [(2, LEVELS, *tile), (PIECES, 8, COLS), (PIECES, 8, COLS), (4, *tile)],
        scratch=[(2, *tile), (4, *tile), tile, tile, tile],
        scalars=1,
        operands=7,
    )(flags, ocean, levels, surface, coriolis, own, low, high)
    up = lax.ppermute(up, ("lon", "lat"), fold_path(False))
    down = lax.ppermute(down, ("lon", "lat"), fold_path(True))
    tracers = call(
        tracer_kernel,
        [(2, LEVELS, *tile)],
        scratch=[(2, *tile), (3, *tile), tile],
        operands=5,
        unread=1,
        cost=100000000,
    )(ocean, levels, own, low, high, sums)
    edges, fields, packed, means, south, north = call(
        edge_kernel,
        [(2, 2, LEVELS, 8, COLS), (6, *rim), rim, (2, *tile), (PIECES, 8, COLS), (PIECES, 8, COLS)],
        scratch=[(2, 2, 8, COLS), (2, 2, 8, COLS)],
        scalars=1,
        operands=6,
        unread=1,
    )(flags, ocean, levels, surface, sums, up, down, tracers)
    west = lax.ppermute(packed, "lon", lon_ring(1))
    east = lax.ppermute(packed, "lon", lon_ring(-1))
    tracer_edges = call(tracer_edge_kernel, [(2, 2, LEVELS, 8, COLS)], operands=4)(ocean, levels, south, north)
    return call(final_kernel, [(4, LEVELS, *tile), (3, *tile)], scratch=[(2, *tile)], operands=10)(
        ocean, levels, accel, tracers, edges, tracer_edges, fields, means, west, east
    )


def solution(mesh):
    return jax.shard_map(
        on_device,
        mesh=mesh,
        in_specs=(P(None, None, "lat", "lon"), P(None, "lat", "lon"), P("lat", "lon")),
        out_specs=(P(None, None, "lat", "lon"), P(None, "lat", "lon")),
        check_vma=False,
    )
```

```python
import math

import jax
import jax.numpy as jnp
from jax import lax
from jax.experimental import pallas as pl
from jax.experimental.pallas import tpu as pltpu
from jax.sharding import PartitionSpec as P


NSUB = 4
LEVELS = 16
ROWS = 32
COLS = 128
BLOCKS = ROWS // 8
THICKNESS = 1.0 / LEVELS
TRACER_STEP = 0.1
SURFACE_STEP = 1.2
PIECES = 2 * LEVELS + 6

F32 = jnp.float32


def lane_index(rows=8):
    return lax.broadcasted_iota(jnp.int32, (rows, COLS), 1)


def row_index(rows=8):
    return lax.broadcasted_iota(jnp.int32, (rows, COLS), 0)


def roll(x, shift, axis):
    if isinstance(shift, int):
        shift %= x.shape[axis]
        if shift == 0:
            return x
    return pltpu.roll(x, shift, axis)


def upwind_flux(speed, qm2, qm1, q0, q1, q2, q3):
    ahead = speed >= 0.0
    a = jnp.where(ahead, qm2, q3)
    b = jnp.where(ahead, qm1, q2)
    c = jnp.where(ahead, q0, q1)
    d = jnp.where(ahead, q1, q0)
    e = jnp.where(ahead, q2, qm1)
    ab = a - b
    bc = b - c
    cd = c - d
    de = d - e
    x1 = ab - bc
    y1 = ab - 3.0 * bc
    x2 = bc - cd
    y2 = bc + cd
    x3 = cd - de
    y3 = 3.0 * cd - de
    third = 13.0 / 3.0
    s1 = third * (x1 * x1) + (y1 * y1 + 4e-6)
    s2 = third * (x2 * x2) + (y2 * y2 + 4e-6)
    s3 = third * (x3 * x3) + (y3 * y3 + 4e-6)
    r1 = s2 * s3
    r2 = s1 * s3
    r3 = s1 * s2
    w1 = r1 * r1
    w2 = 6.0 * (r2 * r2)
    w3 = 3.0 * (r3 * r3)
    top = w1 * (2.0 * ab - 5.0 * bc) - w2 * (bc + 2.0 * cd) + w3 * (de - 4.0 * cd)
    low = 6.0 * (w1 + w2 + w3)
    return speed * (c + top / low)


def density(t, s, wet):
    return wet * (t * (0.03 * s - 0.2 - 0.05 * t) + 0.8 * s)


def wet_of(level_map, k):
    return jnp.where(level_map > k, 1.0, 0.0).astype(F32)


def pack_kernel(ocean_hbm, levels_hbm, out, ocean, levels, sems, level_sem):
    copies = [pltpu.make_async_copy(ocean_hbm.at[q], ocean.at[q], sems.at[q]) for q in range(4)]
    level_copy = pltpu.make_async_copy(levels_hbm, levels, level_sem)
    for copy in copies:
        copy.start()
    level_copy.start()
    group = lane_index() // 8
    for q in range(4):
        copies[q].wait()
        for b in range(BLOCKS):
            rows = pl.ds(8 * b, 8)
            packed = jnp.zeros((8, COLS), F32)
            for k in range(LEVELS):
                packed = jnp.where(group == k, roll(ocean[q, k, rows, :], 8 * k + 4, 1), packed)
            out[q, rows, :] = packed
    level_copy.wait()
    for b in range(BLOCKS):
        rows = pl.ds(8 * b, 8)
        out[4, rows, :] = roll(levels[rows, :].astype(F32), 4, 1)


def low_piece(q, rows, even, swaps):
    return jnp.where(even, swaps[1][q, rows, :], swaps[0][q, rows, :])


def halo_pack(q, rows, even, swaps):
    from_low = lane_index() % 8 < 4
    high = jnp.where(even, swaps[0][q, rows, :], swaps[1][q, rows, :])
    return jnp.where(from_low, low_piece(q, rows, even, swaps), high)


def next_lon(main, halo, step):
    lane = lane_index()
    if step > 0:
        return roll(jnp.where(lane < step, halo, main), -step, 1)
    return roll(jnp.where(lane >= COLS + step, halo, main), -step, 1)


def lon_shifts(main, halo):
    return [main if d == 0 else next_lon(main, halo, d) for d in (-2, -1, 0, 1, 2, 3)]


def west_faces(own, even, swaps, levels, quantities, halo_quantities, packed, lev_halo, west_flux):
    lane = lane_index()
    from_low = lane % 8 < 4
    level_of = lane // 8
    for b in range(BLOCKS):
        rows = pl.ds(8 * b, 8)
        lev = levels[rows, :].astype(F32)
        own_col = lev[:, 0:1]
        west_col = low_piece(4, rows, even, swaps)[:, 3:4]
        both = jnp.minimum(own_col, west_col)
        wet = jnp.where(both > level_of.astype(F32), 1.0, 0.0)
        u = jnp.where(from_low, low_piece(2, rows, even, swaps), own[2, rows, :])
        speed = 0.5 * (u + roll(u, -1, 1)) * wet
        for n, q in enumerate(quantities):
            x = jnp.where(from_low, low_piece(q, rows, even, swaps), own[q, rows, :])
            west_flux[n, rows, :] = upwind_flux(speed, *[roll(x, -d, 1) for d in (-2, -1, 0, 1, 2, 3)])
        for q in halo_quantities:
            packed[q, rows, :] = halo_pack(q, rows, even, swaps)
        lev_halo[rows, :] = roll(halo_pack(4, rows, even, swaps), -4, 1)


def lat_shift(ocean, q, k, b, d):
    start = 8 * b + d
    if 0 <= start and start + 8 <= ROWS:
        return ocean[q, k, start : start + 8, :]
    return roll(ocean[q, k, pl.ds(8 * b, 8), :], -d, 0)


def level_map_shift(levels, b, d):
    start = 8 * b + d
    if 0 <= start and start + 8 <= ROWS:
        return levels[start : start + 8, :].astype(F32)
    return roll(levels[pl.ds(8 * b, 8), :].astype(F32), -d, 0)


def tile_divergence(ocean, levels, k, halo_of, lev_halo, quantities, west_flux):
    lane = lane_index()
    sub = row_index()
    unplace = 124 - 8 * k
    result = {}
    last = {}
    for b in range(BLOCKS):
        rows = pl.ds(8 * b, 8)
        lev = levels[rows, :].astype(F32)
        wet = wet_of(lev, k)
        u = ocean[2, k, rows, :]
        wet_east = wet_of(next_lon(lev, lev_halo[rows, :], 1), k)
        speed_lon = 0.5 * (u + next_lon(u, halo_of(2, rows), 1)) * (wet * wet_east)
        wet_north = wet_of(level_map_shift(levels, b, 1), k)
        speed_lat = 0.5 * (ocean[3, k, rows, :] + lat_shift(ocean, 3, k, b, 1)) * (wet * wet_north)
        for n, q in enumerate(quantities):
            main = ocean[q, k, rows, :]
            east = upwind_flux(speed_lon, *lon_shifts(main, halo_of(q, rows)))
            west = pltpu.roll(west_flux[n, rows, :], unplace, 1)
            west = roll(jnp.where(lane == COLS - 1, west, east), 1, 1)
            north = upwind_flux(speed_lat, *[lat_shift(ocean, q, k, b, d) for d in (-2, -1, 0, 1, 2, 3)])
            if b == 0:
                north = jnp.where(sub >= 2, north, 0.0)
            if b == BLOCKS - 1:
                north = jnp.where(sub <= 4, north, 0.0)
            rolled = roll(north, 1, 0)
            south = jnp.where(sub == 0, last[n] if b else 0.0, rolled)
            last[n] = rolled
            result[n, b] = (east - west) + (north - south)
    return result


def momentum_kernel(
    flags, ocean, levels, surface, coriolis, own, swap_0, swap_1,
    accel, up, down, sums, west_flux, packed, cum, cum_halo, lev_halo,
):
    sub = row_index()
    even_lat = flags[0] == 1
    west_faces(
        own, flags[3] == 1, (swap_0, swap_1), levels, (2, 3), (0, 1, 2, 3), packed, lev_halo, west_flux
    )
    cum[...] = jnp.zeros_like(cum)
    cum_halo[...] = jnp.zeros_like(cum_halo)
    sums[...] = jnp.zeros_like(sums)

    def send(index, south, north):
        up[index] = jnp.where(even_lat, north, south)
        down[index] = jnp.where(even_lat, south, north)

    first, last_rows = pl.ds(0, 8), pl.ds(ROWS - 8, 8)

    def level(k, carry):
        unplace = 124 - 8 * k
        halo = {}

        def halo_of(q, rows):
            key = (q, rows.start)
            if key not in halo:
                halo[key] = pltpu.roll(packed[q, rows, :], unplace, 1)
            return halo[key]

        for pair in range(2):
            t0, t3 = ocean[pair, k, first, :], ocean[pair, k, last_rows, :]
            u0, u3 = ocean[pair + 2, k, first, :], ocean[pair + 2, k, last_rows, :]
            send(
                pair * LEVELS + k,
                jnp.where(sub < 5, u0, roll(t0, 5, 0)),
                jnp.where(sub < 3, roll(t3, 3, 0), u3),
            )
        advection = tile_divergence(ocean, levels, k, halo_of, lev_halo, (2, 3), west_flux)
        pressure, pressure_halo = [], []
        for b in range(BLOCKS):
            rows = pl.ds(8 * b, 8)
            wet = wet_of(levels[rows, :].astype(F32), k)
            here = density(ocean[0, k, rows, :], ocean[1, k, rows, :], wet)
            total = cum[rows, :] + here
            cum[rows, :] = total
            pressure.append(THICKNESS * (total - 0.5 * here))
            here = density(halo_of(0, rows), halo_of(1, rows), wet_of(lev_halo[rows, :], k))
            total = cum_halo[rows, :] + here
            cum_halo[rows, :] = total
            pressure_halo.append(THICKNESS * (total - 0.5 * here))
        for b in range(BLOCKS):
            rows = pl.ds(8 * b, 8)
            wet = wet_of(levels[rows, :].astype(F32), k)
            grad_lon = 0.5 * (
                next_lon(pressure[b], pressure_halo[b], 1) - next_lon(pressure[b], pressure_halo[b], -1)
            )
            ahead = pressure[b] if b == BLOCKS - 1 else jnp.where(sub == 0, pressure[b + 1], pressure[b])
            behind = pressure[b] if b == 0 else jnp.where(sub == 7, pressure[b - 1], pressure[b])
            grad_lat = 0.5 * (roll(ahead, -1, 0) - roll(behind, 1, 0))
            if b == 0:
                grad_lat = jnp.where(sub >= 1, grad_lat, 0.0)
            if b == BLOCKS - 1:
                grad_lat = jnp.where(sub <= 6, grad_lat, 0.0)
            u, v, turn = ocean[2, k, rows, :], ocean[3, k, rows, :], coriolis[rows, :]
            accel_u = wet * (turn * v - grad_lon - advection[0, b])
            accel_v = wet * (-turn * u - grad_lat - advection[1, b])
            accel[0, k, rows, :] = accel_u
            accel[1, k, rows, :] = accel_v
            sums[0, rows, :] += accel_u
            sums[1, rows, :] += accel_v
            sums[2, rows, :] += wet * u
            sums[3, rows, :] += wet * v
        return carry

    lax.fori_loop(0, LEVELS, level, 0)
    flat = [sums.at[0], sums.at[1], surface.at[0], surface.at[1], surface.at[2], levels]
    for n, field in enumerate(flat):
        send(2 * LEVELS + n, field[first, :].astype(F32), field[last_rows, :].astype(F32))


def tracer_kernel(flags, ocean, levels, own, swap_0, swap_1, after, tracers, west_flux, packed, lev_halo):
    del after
    west_faces(
        own, flags[3] == 1, (swap_0, swap_1), levels, (0, 1), (0, 1, 2), packed, lev_halo, west_flux
    )

    def level(k, carry):
        unplace = 124 - 8 * k
        halo = {}

        def halo_of(q, rows):
            key = (q, rows.start)
            if key not in halo:
                halo[key] = pltpu.roll(packed[q, rows, :], unplace, 1)
            return halo[key]

        advection = tile_divergence(ocean, levels, k, halo_of, lev_halo, (0, 1), west_flux)
        for b in range(BLOCKS):
            rows = pl.ds(8 * b, 8)
            wet = wet_of(levels[rows, :].astype(F32), k)
            for n in range(2):
                tracers[n, k, rows, :] = wet * (ocean[n, k, rows, :] - TRACER_STEP * advection[n, b])
        return carry

    lax.fori_loop(0, LEVELS, level, 0)


def window(low_block, high_block, d):
    if d == 8:
        return high_block
    return roll(jnp.where(row_index() >= d, low_block, high_block), -d, 0)


def edge_blocks(ocean, arrived, q, k, side):
    own = ocean[q, k, pl.ds(0 if side == 0 else ROWS - 8, 8), :]
    piece = arrived[(q % 2) * LEVELS + k]
    if side == 0:
        return (roll(piece, 5, 0) if q < 2 else piece), own
    return own, (roll(piece, 3, 0) if q < 2 else piece)


def edge_levels(levels, arrived, side):
    own = levels[pl.ds(0 if side == 0 else ROWS - 8, 8), :].astype(F32)
    return (arrived[PIECES - 1], own) if side == 0 else (own, arrived[PIECES - 1])


def edge_terms(ocean, k, arrived, side, lev5, lev6, quantities):
    sub = row_index()
    v = edge_blocks(ocean, arrived, 3, k, side)
    speed = 0.5 * (window(*v, 5) + window(*v, 6)) * wet_of(jnp.minimum(lev5, lev6), k)
    terms = []
    for q in quantities:
        x = v if q == 3 else edge_blocks(ocean, arrived, q, k, side)
        flux = upwind_flux(speed, *[window(*x, d) for d in (3, 4, 5, 6, 7, 8)])
        flux = jnp.where(sub < 5, flux, 0.0)
        terms.append(flux - jnp.where(sub == 0, 0.0, roll(flux, 1, 0)))
    return terms


def own_rows(term, side):
    sub = row_index()
    if side == 0:
        return jnp.where(sub < 3, roll(term, -3, 0), 0.0)
    return jnp.where(sub >= 5, roll(term, 5, 0), 0.0)


def halo_rows(term, side):
    sub = row_index()
    if side == 0:
        return jnp.where(sub >= 5, roll(term, 5, 0), 0.0)
    return jnp.where(sub < 3, roll(term, -3, 0), 0.0)


def place_arrivals(flags, up, down, south, north):
    even_lat = flags[0] == 1
    at_south, at_fold = flags[1] == 1, flags[2] == 1
    turned_row, turned_lane = 7 - row_index(), COLS - 1 - lane_index()
    pair_sign = jnp.where(row_index() < 5, -1.0, 1.0)

    def piece(n, sign):
        south[n] = jnp.where(at_south, 0.0, jnp.where(even_lat, down[n], up[n]))
        here = jnp.where(even_lat, up[n], down[n])
        turned = jnp.take_along_axis(jnp.take_along_axis(here, turned_lane, axis=1), turned_row, axis=0)
        north[n] = jnp.where(at_fold, turned * sign, here)

    def pairs(first, carry):
        for n in range(8):
            piece(8 * first + n, pair_sign)
        return carry

    lax.fori_loop(0, 2 * LEVELS // 8, pairs, 0)
    for n, sign in enumerate((-1.0, -1.0, 1.0, -1.0, -1.0, 1.0)):
        piece(2 * LEVELS + n, sign)


def edge_kernel(
    flags, ocean, levels, surface, sums, up, down, after,
    edges, fields, packed, means, south, north, cum, total,
):
    del after
    place_arrivals(flags, up, down, south, north)
    sub = row_index()
    cum[...] = jnp.zeros_like(cum)
    total[...] = jnp.zeros_like(total)
    arrived = (south, north)

    def level(k, carry):
        for side in range(2):
            lev = edge_levels(levels, arrived[side], side)
            lev5, lev6 = window(*lev, 5), window(*lev, 6)
            terms = edge_terms(ocean, k, arrived[side], side, lev5, lev6, (2, 3))
            t = edge_blocks(ocean, arrived[side], 0, k, side)
            s = edge_blocks(ocean, arrived[side], 1, k, side)
            pressure = []
            for half in range(2):
                here = density(t[half], s[half], wet_of(lev[half], k))
                column = cum[side, half] + here
                cum[side, half] = column
                pressure.append(THICKNESS * (column - 0.5 * here))
            grad = 0.5 * (window(*pressure, 6) - window(*pressure, 4))
            grad = jnp.where((sub == 2) | (sub == 3), grad, 0.0)
            wet = wet_of(lev5, k)
            for n, term in enumerate((-wet * terms[0], -wet * (terms[1] + grad))):
                total[side, n] += term
                edges[side, n, k] = own_rows(term, side)
        return carry

    lax.fori_loop(0, LEVELS, level, 0)
    rim = ROWS + 16
    own = pl.ds(8, ROWS)
    for n in range(3):
        fields[n, pl.ds(0, 8), :] = south[2 * LEVELS + 2 + n]
        fields[n, own, :] = surface[n]
        fields[n, pl.ds(rim - 8, 8), :] = north[2 * LEVELS + 2 + n]
    fields[3, pl.ds(0, 8), :] = south[PIECES - 1]
    fields[3, own, :] = levels[...].astype(F32)
    fields[3, pl.ds(rim - 8, 8), :] = north[PIECES - 1]
    for n in range(2):
        fields[4 + n, pl.ds(0, 8), :] = south[2 * LEVELS + n] + halo_rows(total[0, n], 0)
        fields[4 + n, own, :] = sums[n]
        fields[4 + n, pl.ds(8, 8), :] += own_rows(total[0, n], 0)
        fields[4 + n, pl.ds(ROWS, 8), :] += own_rows(total[1, n], 1)
        fields[4 + n, pl.ds(rim - 8, 8), :] = north[2 * LEVELS + n] + halo_rows(total[1, n], 1)
    for n in range(2):
        safe = jnp.maximum(THICKNESS * levels[...].astype(F32), THICKNESS)
        means[n] = THICKNESS * (sums[2 + n] + TRACER_STEP * fields[4 + n, own, :]) / safe
    for b in range(rim // 8):
        rows = pl.ds(8 * b, 8)
        safe = jnp.maximum(THICKNESS * fields[3, rows, :], THICKNESS)
        group = lane_index() // 16
        out = jnp.zeros((8, COLS), F32)
        for n in range(6):
            if n >= 4:
                fields[n, rows, :] = THICKNESS * fields[n, rows, :] / safe
            out = jnp.where(group == n, roll(fields[n, rows, :], 16 * n + 8, 1), out)
        packed[rows, :] = out


def tracer_edge_kernel(ocean, levels, south, north, edges):
    arrived = (south, north)

    def level(k, carry):
        for side in range(2):
            lev = edge_levels(levels, arrived[side], side)
            lev5, lev6 = window(*lev, 5), window(*lev, 6)
            wet = wet_of(lev5, k)
            terms = edge_terms(ocean, k, arrived[side], side, lev5, lev6, (0, 1))
            for n in range(2):
                edges[side, n, k] = own_rows(-wet * terms[n], side)
        return carry

    lax.fori_loop(0, LEVELS, level, 0)


def final_kernel(
    flags, ocean, levels, accel, tracers, edges, tracer_edges, fields, means, swap_0, swap_1,
    ocean_out, surface_out, shift,
):
    rim = ROWS + 16
    lane = lane_index(rim)
    even = flags[3] == 1
    low = jnp.where(even, swap_1[...], swap_0[...])
    high = jnp.where(even, swap_0[...], swap_1[...])
    halos = jnp.where(lane % 16 < 8, low, high)
    both = []
    for n in range(6):
        both.append((fields[n], roll(halos, -(16 * n + 8), 1)))
    height, mean_u, mean_v, level_map, force_lon, force_lat = both
    depth = tuple(THICKNESS * x for x in level_map)
    sea = tuple(jnp.where(x > 0.0, 1.0, 0.0) for x in level_map)

    def d_lon(x):
        main, halo = x
        result = []
        for here, other in ((main, halo), (halo, main)):
            ahead = roll(jnp.where(lane == 0, other, here), -1, 1)
            behind = roll(jnp.where(lane == COLS - 1, other, here), 1, 1)
            result.append(0.5 * (ahead - behind))
        return result

    def d_lat(x):
        return [0.5 * (roll(part, -1, 0) - roll(part, 1, 0)) for part in x]

    def times(x, y):
        return [p * q for p, q in zip(x, y)]

    for _ in range(NSUB):
        along, across = d_lon(times(depth, mean_u)), d_lat(times(depth, mean_v))
        height = [s * (h - SURFACE_STEP * (p + q)) for s, h, p, q in zip(sea, height, along, across)]
        mean_u = [
            s * (m + SURFACE_STEP * (f - d)) for s, m, f, d in zip(sea, mean_u, force_lon, d_lon(height))
        ]
        mean_v = [
            s * (m + SURFACE_STEP * (f - d)) for s, m, f, d in zip(sea, mean_v, force_lat, d_lat(height))
        ]
    for n, field in enumerate((height, mean_u, mean_v)):
        surface_out[n] = field[0][8 : 8 + ROWS]
    shift[0] = mean_u[0][8 : 8 + ROWS] - means[0]
    shift[1] = mean_v[0][8 : 8 + ROWS] - means[1]

    def level(k, carry):
        for b in range(BLOCKS):
            rows = pl.ds(8 * b, 8)
            wet = wet_of(levels[rows, :].astype(F32), k)
            for n in range(2):
                tracer, force = tracers[n, k, rows, :], accel[n, k, rows, :]
                if b in (0, BLOCKS - 1):
                    side = min(b, 1)
                    tracer = tracer + TRACER_STEP * tracer_edges[side, n, k]
                    force = force + edges[side, n, k]
                ocean_out[n, k, rows, :] = tracer
                ocean_out[2 + n, k, rows, :] = wet * (
                    ocean[2 + n, k, rows, :] + TRACER_STEP * force + shift[n, rows, :]
                )
        return carry

    lax.fori_loop(0, LEVELS, level, 0)


def swapped(pairs):
    return list(pairs) + [(b, a) for a, b in pairs]


def swap_lon(x):
    count = lax.axis_size("lon")
    first = swapped([(i, i + 1) for i in range(0, count, 2)])
    second = swapped([(i, (i + 1) % count) for i in range(1, count, 2)])
    second = lax.ppermute(x, "lon", second)
    return lax.ppermute(x, "lon", first), second


def swap_lat(x, y):
    lon_count, lat_count = lax.axis_size("lon"), lax.axis_size("lat")
    first, second = [], []
    for p in range(lon_count):
        base = p * lat_count
        first += [(base + r, base + r + 1) for r in range(0, lat_count, 2)]
        second += [(base + r, base + r + 1) for r in range(1, lat_count - 1, 2)]
        if p < lon_count // 2:
            second.append((base + lat_count - 1, (lon_count - p) * lat_count - 1))
    y = lax.ppermute(y, ("lon", "lat"), swapped(second))
    x = lax.ppermute(x, ("lon", "lat"), swapped(first))
    return x, y


def call(kernel, outs, scratch=(), scalars=0, operands=1, unread=0, cost=1000000, limit=16):
    def vmem():
        return pl.BlockSpec(memory_space=pltpu.VMEM)

    specs = [pl.BlockSpec(memory_space=pltpu.SMEM)] * scalars + [vmem()] * operands
    specs += [pl.BlockSpec(memory_space=pl.ANY)] * unread
    single = len(outs) == 1
    shapes = [jax.ShapeDtypeStruct(shape, F32) for shape in outs]
    return pl.pallas_call(
        kernel,
        out_shape=shapes[0] if single else shapes,
        in_specs=specs,
        out_specs=vmem() if single else [vmem() for _ in outs],
        scratch_shapes=[pltpu.VMEM(shape, F32) for shape in scratch],
        cost_estimate=pl.CostEstimate(flops=cost, bytes_accessed=cost, transcendentals=0),
        compiler_params=pltpu.CompilerParams(vmem_limit_bytes=limit << 20),
    )


def on_device(ocean, surface, levels):
    tile = (ROWS, COLS)
    rim = (ROWS + 16, COLS)
    own = pl.pallas_call(
        pack_kernel,
        out_shape=jax.ShapeDtypeStruct((5, *tile), F32),
        in_specs=[pl.BlockSpec(memory_space=pl.ANY)] * 2,
        out_specs=pl.BlockSpec(memory_space=pltpu.VMEM),
        scratch_shapes=[
            pltpu.VMEM(ocean.shape, F32),
            pltpu.VMEM(tile, jnp.int32),
            pltpu.SemaphoreType.DMA((4,)),
            pltpu.SemaphoreType.DMA(()),
        ],
    )(ocean, levels)
    lon_0, lon_1 = swap_lon(own)
    lon_index = lax.axis_index("lon")
    lat_index, lat_count = lax.axis_index("lat"), lax.axis_size("lat")
    row = lat_index * ROWS + lax.broadcasted_iota(jnp.int32, tile, 0)
    latitude = (row.astype(F32) + 0.5) / float(lat_count * ROWS)
    coriolis = jnp.sin(math.pi * latitude - 0.5 * math.pi)
    flags = [lat_index % 2 == 0, lat_index == 0, lat_index == lat_count - 1, lon_index % 2 == 0]
    flags = jnp.stack(flags).astype(jnp.int32)
    accel, lat_0, lat_1, sums = call(
        momentum_kernel,
        [(2, LEVELS, *tile), (PIECES, 8, COLS), (PIECES, 8, COLS), (4, *tile)],
        scratch=[(2, *tile), (4, *tile), tile, tile, tile],
        scalars=1,
        operands=7,
    )(flags, ocean, levels, surface, coriolis, own, lon_0, lon_1)
    lat_0, lat_1 = swap_lat(lat_0, lat_1)
    tracers = call(
        tracer_kernel,
        [(2, LEVELS, *tile)],
        scratch=[(2, *tile), (3, *tile), tile],
        scalars=1,
        operands=5,
        unread=1,
        cost=100000000,
    )(flags, ocean, levels, own, lon_0, lon_1, sums)
    edges, fields, packed, means, south, north = call(
        edge_kernel,
        [(2, 2, LEVELS, 8, COLS), (6, *rim), rim, (2, *tile), (PIECES, 8, COLS), (PIECES, 8, COLS)],
        scratch=[(2, 2, 8, COLS), (2, 2, 8, COLS)],
        scalars=1,
        operands=6,
        unread=1,
    )(flags, ocean, levels, surface, sums, lat_0, lat_1, tracers)
    rim_0, rim_1 = swap_lon(packed)
    tracer_edges = call(tracer_edge_kernel, [(2, 2, LEVELS, 8, COLS)], operands=4)(ocean, levels, south, north)
    return call(
        final_kernel, [(4, LEVELS, *tile), (3, *tile)], scratch=[(2, *tile)], scalars=1, operands=10
    )(flags, ocean, levels, accel, tracers, edges, tracer_edges, fields, means, rim_0, rim_1)


def solution(mesh):
    return jax.shard_map(
        on_device,
        mesh=mesh,
        in_specs=(P(None, None, "lat", "lon"), P(None, "lat", "lon"), P("lat", "lon")),
        out_specs=(P(None, None, "lat", "lon"), P(None, "lat", "lon")),
        check_vma=False,
    )
```

```python
import math

import jax
import jax.numpy as jnp
from jax import lax
from jax.experimental import pallas as pl
from jax.experimental.pallas import tpu as pltpu
from jax.sharding import PartitionSpec as P


NSUB = 4
LEVELS = 16
ROWS = 32
COLS = 128
BLOCKS = ROWS // 8
THICKNESS = 1.0 / LEVELS
TRACER_STEP = 0.1
SURFACE_STEP = 1.2
PIECES = 2 * LEVELS + 6

F32 = jnp.float32


def even_tile(axis):
    return lax.rem(lax.axis_index(axis), 2) == 0


def lane_index(rows=8):
    return lax.broadcasted_iota(jnp.int32, (rows, COLS), 1)


def row_index(rows=8):
    return lax.broadcasted_iota(jnp.int32, (rows, COLS), 0)


def roll(x, shift, axis):
    if isinstance(shift, int):
        shift %= x.shape[axis]
        if shift == 0:
            return x
    return pltpu.roll(x, shift, axis)


def upwind_flux(speed, qm2, qm1, q0, q1, q2, q3):
    ahead = speed >= 0.0
    a = jnp.where(ahead, qm2, q3)
    b = jnp.where(ahead, qm1, q2)
    c = jnp.where(ahead, q0, q1)
    d = jnp.where(ahead, q1, q0)
    e = jnp.where(ahead, q2, qm1)
    ab = a - b
    bc = b - c
    cd = c - d
    de = d - e
    x1 = ab - bc
    y1 = ab - 3.0 * bc
    x2 = bc - cd
    y2 = bc + cd
    x3 = cd - de
    y3 = 3.0 * cd - de
    third = 13.0 / 3.0
    s1 = third * (x1 * x1) + (y1 * y1 + 4e-6)
    s2 = third * (x2 * x2) + (y2 * y2 + 4e-6)
    s3 = third * (x3 * x3) + (y3 * y3 + 4e-6)
    r1 = s2 * s3
    r2 = s1 * s3
    r3 = s1 * s2
    w1 = r1 * r1
    w2 = 6.0 * (r2 * r2)
    w3 = 3.0 * (r3 * r3)
    top = w1 * (2.0 * ab - 5.0 * bc) - w2 * (bc + 2.0 * cd) + w3 * (de - 4.0 * cd)
    low = 6.0 * (w1 + w2 + w3)
    return speed * (c + top / low)


def density(t, s, wet):
    return wet * (t * (0.03 * s - 0.2 - 0.05 * t) + 0.8 * s)


def wet_of(level_map, k):
    return jnp.where(level_map > k, 1.0, 0.0).astype(F32)


def pack_kernel(ocean_hbm, levels_hbm, out, ocean, levels, sems, level_sem):
    copies = [pltpu.make_async_copy(ocean_hbm.at[q], ocean.at[q], sems.at[q]) for q in range(4)]
    level_copy = pltpu.make_async_copy(levels_hbm, levels, level_sem)
    for copy in copies:
        copy.start()
    level_copy.start()
    group = lane_index() // 8
    for q in range(4):
        copies[q].wait()
        for b in range(BLOCKS):
            rows = pl.ds(8 * b, 8)
            packed = jnp.zeros((8, COLS), F32)
            for k in range(LEVELS):
                packed = jnp.where(group == k, roll(ocean[q, k, rows, :], 8 * k + 4, 1), packed)
            out[q, rows, :] = packed
    level_copy.wait()
    for b in range(BLOCKS):
        rows = pl.ds(8 * b, 8)
        out[4, rows, :] = roll(levels[rows, :].astype(F32), 4, 1)


def low_piece(q, rows, even, swaps):
    return jnp.where(even, swaps[1][q, rows, :], swaps[0][q, rows, :])


def halo_pack(q, rows, even, swaps):
    from_low = lane_index() % 8 < 4
    high = jnp.where(even, swaps[0][q, rows, :], swaps[1][q, rows, :])
    return jnp.where(from_low, low_piece(q, rows, even, swaps), high)


def next_lon(main, halo, step):
    lane = lane_index()
    if step > 0:
        return roll(jnp.where(lane < step, halo, main), -step, 1)
    return roll(jnp.where(lane >= COLS + step, halo, main), -step, 1)


def lon_shifts(main, halo):
    return [main if d == 0 else next_lon(main, halo, d) for d in (-2, -1, 0, 1, 2, 3)]


def west_faces(own, swaps, levels, quantities, halo_quantities, packed, lev_halo, west_flux, blocks):
    lane = lane_index()
    from_low = lane % 8 < 4
    level_of = lane // 8
    even = even_tile("lon")
    for b in blocks:
        rows = pl.ds(8 * b, 8)
        lev = levels[rows, :].astype(F32)
        own_col = lev[:, 0:1]
        west_col = low_piece(4, rows, even, swaps)[:, 3:4]
        both = jnp.minimum(own_col, west_col)
        wet = jnp.where(both > level_of.astype(F32), 1.0, 0.0)
        u = jnp.where(from_low, low_piece(2, rows, even, swaps), own[2, rows, :])
        speed = 0.5 * (u + roll(u, -1, 1)) * wet
        for n, q in enumerate(quantities):
            x = jnp.where(from_low, low_piece(q, rows, even, swaps), own[q, rows, :])
            west_flux[n, rows, :] = upwind_flux(speed, *[roll(x, -d, 1) for d in (-2, -1, 0, 1, 2, 3)])
        for q in halo_quantities:
            packed[q, rows, :] = halo_pack(q, rows, even, swaps)
        lev_halo[rows, :] = roll(halo_pack(4, rows, even, swaps), -4, 1)


def lat_shift(ocean, q, k, b, d):
    start = 8 * b + d
    if 0 <= start and start + 8 <= ROWS:
        return ocean[q, k, start : start + 8, :]
    return roll(ocean[q, k, pl.ds(8 * b, 8), :], -d, 0)


def level_map_shift(levels, b, d):
    start = 8 * b + d
    if 0 <= start and start + 8 <= ROWS:
        return levels[start : start + 8, :].astype(F32)
    return roll(levels[pl.ds(8 * b, 8), :].astype(F32), -d, 0)


def tile_divergence(ocean, levels, k, halo_of, lev_halo, quantities, west_flux, blocks, last):
    lane = lane_index()
    sub = row_index()
    unplace = 124 - 8 * k
    result = {}
    for b in blocks:
        rows = pl.ds(8 * b, 8)
        lev = levels[rows, :].astype(F32)
        wet = wet_of(lev, k)
        u = ocean[2, k, rows, :]
        wet_east = wet_of(next_lon(lev, lev_halo[rows, :], 1), k)
        speed_lon = 0.5 * (u + next_lon(u, halo_of(2, rows), 1)) * (wet * wet_east)
        wet_north = wet_of(level_map_shift(levels, b, 1), k)
        speed_lat = 0.5 * (ocean[3, k, rows, :] + lat_shift(ocean, 3, k, b, 1)) * (wet * wet_north)
        for n, q in enumerate(quantities):
            main = ocean[q, k, rows, :]
            east = upwind_flux(speed_lon, *lon_shifts(main, halo_of(q, rows)))
            west = pltpu.roll(west_flux[n, rows, :], unplace, 1)
            west = roll(jnp.where(lane == COLS - 1, west, east), 1, 1)
            north = upwind_flux(speed_lat, *[lat_shift(ocean, q, k, b, d) for d in (-2, -1, 0, 1, 2, 3)])
            if b == 0:
                north = jnp.where(sub >= 2, north, 0.0)
            if b == BLOCKS - 1:
                north = jnp.where(sub <= 4, north, 0.0)
            last[n, b] = roll(north, 1, 0)
            south = jnp.where(sub == 0, last.get((n, b - 1), 0.0), last[n, b])
            result[n, b] = (east - west) + (north - south)
    return result


def halo_reader(packed, k):
    halo = {}

    def halo_of(q, rows):
        key = (q, rows.start)
        if key not in halo:
            halo[key] = pltpu.roll(packed[q, rows, :], 124 - 8 * k, 1)
        return halo[key]

    return halo_of


def momentum_level(ocean, levels, coriolis, k, packed, lev_halo, west_flux, cum, cum_halo, blocks, last):
    sub = row_index()
    halo_of = halo_reader(packed, k)
    advection = tile_divergence(ocean, levels, k, halo_of, lev_halo, (2, 3), west_flux, blocks, last)
    pressure, pressure_halo = [], {}
    for b in range(BLOCKS):
        rows = pl.ds(8 * b, 8)
        here = density(ocean[0, k, rows, :], ocean[1, k, rows, :], wet_of(levels[rows, :].astype(F32), k))
        total = cum[rows, :] + here
        cum[rows, :] = total
        pressure.append(THICKNESS * (total - 0.5 * here))
    for b in blocks:
        rows = pl.ds(8 * b, 8)
        here = density(halo_of(0, rows), halo_of(1, rows), wet_of(lev_halo[rows, :], k))
        total = cum_halo[rows, :] + here
        cum_halo[rows, :] = total
        pressure_halo[b] = THICKNESS * (total - 0.5 * here)
    result = {}
    for b in blocks:
        rows = pl.ds(8 * b, 8)
        wet = wet_of(levels[rows, :].astype(F32), k)
        grad_lon = 0.5 * (
            next_lon(pressure[b], pressure_halo[b], 1) - next_lon(pressure[b], pressure_halo[b], -1)
        )
        ahead = pressure[b] if b == BLOCKS - 1 else jnp.where(sub == 0, pressure[b + 1], pressure[b])
        behind = pressure[b] if b == 0 else jnp.where(sub == 7, pressure[b - 1], pressure[b])
        grad_lat = 0.5 * (roll(ahead, -1, 0) - roll(behind, 1, 0))
        if b == 0:
            grad_lat = jnp.where(sub >= 1, grad_lat, 0.0)
        if b == BLOCKS - 1:
            grad_lat = jnp.where(sub <= 6, grad_lat, 0.0)
        u, v, turn = ocean[2, k, rows, :], ocean[3, k, rows, :], coriolis[rows, :]
        accel_u = wet * (turn * v - grad_lon - advection[0, b])
        accel_v = wet * (-turn * u - grad_lat - advection[1, b])
        result[b] = (accel_u, accel_v, wet * u, wet * v)
    return result


OUTER = (0, BLOCKS - 1)
INNER = tuple(range(1, BLOCKS - 1))


def outer_kernel(
    ocean, levels, surface, coriolis, own, swap_0, swap_1,
    accel, faces, even_out, odd_out, sums, west_flux, packed, cum, cum_halo, lev_halo,
):
    sub = row_index()
    even_lat = even_tile("lat")
    west_faces(
        own, (swap_0, swap_1), levels, (2, 3), (0, 1, 2, 3), packed, lev_halo, west_flux, OUTER
    )
    cum[...] = jnp.zeros_like(cum)
    cum_halo[...] = jnp.zeros_like(cum_halo)
    sums[...] = jnp.zeros_like(sums)

    def send(index, south, north):
        even_out[index] = jnp.where(even_lat, north, south)
        odd_out[index] = jnp.where(even_lat, south, north)

    first, last_rows = pl.ds(0, 8), pl.ds(ROWS - 8, 8)

    def level(k, carry):
        for pair in range(2):
            t0, t3 = ocean[pair, k, first, :], ocean[pair, k, last_rows, :]
            u0, u3 = ocean[pair + 2, k, first, :], ocean[pair + 2, k, last_rows, :]
            send(
                pair * LEVELS + k,
                jnp.where(sub < 5, u0, roll(t0, 5, 0)),
                jnp.where(sub < 3, roll(t3, 3, 0), u3),
            )
        last = {}
        terms = momentum_level(
            ocean, levels, coriolis, k, packed, lev_halo, west_flux, cum, cum_halo, OUTER, last
        )
        for side, b in enumerate(OUTER):
            for n in range(2):
                accel[n, k, side] = terms[b][n]
            for n in range(4):
                sums[n, pl.ds(8 * b, 8), :] += terms[b][n]
        for n in range(2):
            faces[n, k] = last[n, 0]
        return carry

    lax.fori_loop(0, LEVELS, level, 0)
    flat = [sums.at[0], sums.at[1], surface.at[0], surface.at[1], surface.at[2], levels]
    for n, field in enumerate(flat):
        send(2 * LEVELS + n, field[first, :].astype(F32), field[last_rows, :].astype(F32))


def inner_kernel(
    ocean, levels, coriolis, own, swap_0, swap_1, outer_accel, faces, outer_sums,
    accel, sums, west_flux, packed, cum, cum_halo, lev_halo,
):
    sub = row_index()
    west_faces(
        own, (swap_0, swap_1), levels, (2, 3), (0, 1, 2, 3), packed, lev_halo, west_flux, INNER
    )
    cum[...] = jnp.zeros_like(cum)
    cum_halo[...] = jnp.zeros_like(cum_halo)
    sums[...] = outer_sums[...]
    top_rows = pl.ds(ROWS - 8, 8)

    def level(k, carry):
        last = {(n, 0): faces[n, k] for n in range(2)}
        terms = momentum_level(
            ocean, levels, coriolis, k, packed, lev_halo, west_flux, cum, cum_halo, INNER, last
        )
        for b in INNER:
            rows = pl.ds(8 * b, 8)
            for n in range(4):
                if n < 2:
                    accel[n, k, rows, :] = terms[b][n]
                sums[n, rows, :] += terms[b][n]
        wet = wet_of(levels[top_rows, :].astype(F32), k)
        for n in range(2):
            south_face = wet * jnp.where(sub == 0, last[n, BLOCKS - 2], 0.0)
            accel[n, k, pl.ds(0, 8), :] = outer_accel[n, k, 0]
            accel[n, k, top_rows, :] = outer_accel[n, k, 1] + south_face
            sums[n, top_rows, :] += south_face
        return carry

    lax.fori_loop(0, LEVELS, level, 0)


def tracer_kernel(ocean, levels, own, swap_0, swap_1, after, tracers, west_flux, packed, lev_halo):
    del after
    blocks = range(BLOCKS)
    west_faces(own, (swap_0, swap_1), levels, (0, 1), (0, 1, 2), packed, lev_halo, west_flux, blocks)

    def level(k, carry):
        advection = tile_divergence(
            ocean, levels, k, halo_reader(packed, k), lev_halo, (0, 1), west_flux, blocks, {}
        )
        for b in blocks:
            rows = pl.ds(8 * b, 8)
            wet = wet_of(levels[rows, :].astype(F32), k)
            for n in range(2):
                tracers[n, k, rows, :] = wet * (ocean[n, k, rows, :] - TRACER_STEP * advection[n, b])
        return carry

    lax.fori_loop(0, LEVELS, level, 0)


def window(low_block, high_block, d):
    if d == 8:
        return high_block
    return roll(jnp.where(row_index() >= d, low_block, high_block), -d, 0)


def edge_blocks(ocean, arrived, q, k, side):
    own = ocean[q, k, pl.ds(0 if side == 0 else ROWS - 8, 8), :]
    piece = arrived[(q % 2) * LEVELS + k]
    if side == 0:
        return (roll(piece, 5, 0) if q < 2 else piece), own
    return own, (roll(piece, 3, 0) if q < 2 else piece)


def edge_levels(levels, arrived, side):
    own = levels[pl.ds(0 if side == 0 else ROWS - 8, 8), :].astype(F32)
    return (arrived[PIECES - 1], own) if side == 0 else (own, arrived[PIECES - 1])


def edge_terms(ocean, k, arrived, side, lev5, lev6, quantities):
    sub = row_index()
    v = edge_blocks(ocean, arrived, 3, k, side)
    speed = 0.5 * (window(*v, 5) + window(*v, 6)) * wet_of(jnp.minimum(lev5, lev6), k)
    terms = []
    for q in quantities:
        x = v if q == 3 else edge_blocks(ocean, arrived, q, k, side)
        flux = upwind_flux(speed, *[window(*x, d) for d in (3, 4, 5, 6, 7, 8)])
        flux = jnp.where(sub < 5, flux, 0.0)
        terms.append(flux - jnp.where(sub == 0, 0.0, roll(flux, 1, 0)))
    return terms


def own_rows(term, side):
    sub = row_index()
    if side == 0:
        return jnp.where(sub < 3, roll(term, -3, 0), 0.0)
    return jnp.where(sub >= 5, roll(term, 5, 0), 0.0)


def halo_rows(term, side):
    sub = row_index()
    if side == 0:
        return jnp.where(sub >= 5, roll(term, 5, 0), 0.0)
    return jnp.where(sub < 3, roll(term, -3, 0), 0.0)


def place_arrivals(up, down, south, north):
    even_lat = even_tile("lat")
    at_south = lax.axis_index("lat") == 0
    at_fold = lax.axis_index("lat") == lax.axis_size("lat") - 1
    turned_row, turned_lane = 7 - row_index(), COLS - 1 - lane_index()
    pair_sign = jnp.where(row_index() < 5, -1.0, 1.0)

    def piece(n, sign):
        south[n] = jnp.where(at_south, 0.0, jnp.where(even_lat, down[n], up[n]))
        here = jnp.where(even_lat, up[n], down[n])
        turned = jnp.take_along_axis(jnp.take_along_axis(here, turned_lane, axis=1), turned_row, axis=0)
        north[n] = jnp.where(at_fold, turned * sign, here)

    def pairs(first, carry):
        for n in range(8):
            piece(8 * first + n, pair_sign)
        return carry

    lax.fori_loop(0, 2 * LEVELS // 8, pairs, 0)
    for n, sign in enumerate((-1.0, -1.0, 1.0, -1.0, -1.0, 1.0)):
        piece(2 * LEVELS + n, sign)


def edge_kernel(
    ocean, levels, surface, sums, up, down, after,
    edges, fields, packed, means, south, north, cum, total,
):
    del after
    place_arrivals(up, down, south, north)
    sub = row_index()
    cum[...] = jnp.zeros_like(cum)
    total[...] = jnp.zeros_like(total)
    arrived = (south, north)

    def level(k, carry):
        for side in range(2):
            lev = edge_levels(levels, arrived[side], side)
            lev5, lev6 = window(*lev, 5), window(*lev, 6)
            terms = edge_terms(ocean, k, arrived[side], side, lev5, lev6, (2, 3))
            t = edge_blocks(ocean, arrived[side], 0, k, side)
            s = edge_blocks(ocean, arrived[side], 1, k, side)
            pressure = []
            for half in range(2):
                here = density(t[half], s[half], wet_of(lev[half], k))
                column = cum[side, half] + here
                cum[side, half] = column
                pressure.append(THICKNESS * (column - 0.5 * here))
            grad = 0.5 * (window(*pressure, 6) - window(*pressure, 4))
            grad = jnp.where((sub == 2) | (sub == 3), grad, 0.0)
            wet = wet_of(lev5, k)
            for n, term in enumerate((-wet * terms[0], -wet * (terms[1] + grad))):
                total[side, n] += term
                edges[side, n, k] = own_rows(term, side)
        return carry

    lax.fori_loop(0, LEVELS, level, 0)
    rim = ROWS + 16
    own = pl.ds(8, ROWS)
    for n in range(3):
        fields[n, pl.ds(0, 8), :] = south[2 * LEVELS + 2 + n]
        fields[n, own, :] = surface[n]
        fields[n, pl.ds(rim - 8, 8), :] = north[2 * LEVELS + 2 + n]
    fields[3, pl.ds(0, 8), :] = south[PIECES - 1]
    fields[3, own, :] = levels[...].astype(F32)
    fields[3, pl.ds(rim - 8, 8), :] = north[PIECES - 1]
    for n in range(2):
        fields[4 + n, pl.ds(0, 8), :] = south[2 * LEVELS + n] + halo_rows(total[0, n], 0)
        fields[4 + n, own, :] = sums[n]
        fields[4 + n, pl.ds(8, 8), :] += own_rows(total[0, n], 0)
        fields[4 + n, pl.ds(ROWS, 8), :] += own_rows(total[1, n], 1)
        fields[4 + n, pl.ds(rim - 8, 8), :] = north[2 * LEVELS + n] + halo_rows(total[1, n], 1)
    for n in range(2):
        safe = jnp.maximum(THICKNESS * levels[...].astype(F32), THICKNESS)
        means[n] = THICKNESS * (sums[2 + n] + TRACER_STEP * fields[4 + n, own, :]) / safe
    for b in range(rim // 8):
        rows = pl.ds(8 * b, 8)
        safe = jnp.maximum(THICKNESS * fields[3, rows, :], THICKNESS)
        group = lane_index() // 16
        out = jnp.zeros((8, COLS), F32)
        for n in range(6):
            if n >= 4:
                fields[n, rows, :] = THICKNESS * fields[n, rows, :] / safe
            out = jnp.where(group == n, roll(fields[n, rows, :], 16 * n + 8, 1), out)
        packed[rows, :] = out


def tracer_edge_kernel(ocean, levels, south, north, edges):
    arrived = (south, north)

    def level(k, carry):
        for side in range(2):
            lev = edge_levels(levels, arrived[side], side)
            lev5, lev6 = window(*lev, 5), window(*lev, 6)
            wet = wet_of(lev5, k)
            terms = edge_terms(ocean, k, arrived[side], side, lev5, lev6, (0, 1))
            for n in range(2):
                edges[side, n, k] = own_rows(-wet * terms[n], side)
        return carry

    lax.fori_loop(0, LEVELS, level, 0)


def final_kernel(
    ocean, levels, accel, tracers, edges, tracer_edges, fields, means, swap_0, swap_1,
    ocean_out, surface_out, shift,
):
    rim = ROWS + 16
    lane = lane_index(rim)
    even = even_tile("lon")
    low = jnp.where(even, swap_1[...], swap_0[...])
    high = jnp.where(even, swap_0[...], swap_1[...])
    halos = jnp.where(lane % 16 < 8, low, high)
    both = []
    for n in range(6):
        both.append((fields[n], roll(halos, -(16 * n + 8), 1)))
    height, mean_u, mean_v, level_map, force_lon, force_lat = both
    depth = tuple(THICKNESS * x for x in level_map)
    sea = tuple(jnp.where(x > 0.0, 1.0, 0.0) for x in level_map)

    def d_lon(x):
        main, halo = x
        result = []
        for here, other in ((main, halo), (halo, main)):
            ahead = roll(jnp.where(lane == 0, other, here), -1, 1)
            behind = roll(jnp.where(lane == COLS - 1, other, here), 1, 1)
            result.append(0.5 * (ahead - behind))
        return result

    def d_lat(x):
        return [0.5 * (roll(part, -1, 0) - roll(part, 1, 0)) for part in x]

    def times(x, y):
        return [p * q for p, q in zip(x, y)]

    for _ in range(NSUB):
        along, across = d_lon(times(depth, mean_u)), d_lat(times(depth, mean_v))
        height = [s * (h - SURFACE_STEP * (p + q)) for s, h, p, q in zip(sea, height, along, across)]
        mean_u = [
            s * (m + SURFACE_STEP * (f - d)) for s, m, f, d in zip(sea, mean_u, force_lon, d_lon(height))
        ]
        mean_v = [
            s * (m + SURFACE_STEP * (f - d)) for s, m, f, d in zip(sea, mean_v, force_lat, d_lat(height))
        ]
    for n, field in enumerate((height, mean_u, mean_v)):
        surface_out[n] = field[0][8 : 8 + ROWS]
    shift[0] = mean_u[0][8 : 8 + ROWS] - means[0]
    shift[1] = mean_v[0][8 : 8 + ROWS] - means[1]

    def level(k, carry):
        for b in range(BLOCKS):
            rows = pl.ds(8 * b, 8)
            wet = wet_of(levels[rows, :].astype(F32), k)
            for n in range(2):
                tracer, force = tracers[n, k, rows, :], accel[n, k, rows, :]
                if b in (0, BLOCKS - 1):
                    side = min(b, 1)
                    tracer = tracer + TRACER_STEP * tracer_edges[side, n, k]
                    force = force + edges[side, n, k]
                ocean_out[n, k, rows, :] = tracer
                ocean_out[2 + n, k, rows, :] = wet * (
                    ocean[2 + n, k, rows, :] + TRACER_STEP * force + shift[n, rows, :]
                )
        return carry

    lax.fori_loop(0, LEVELS, level, 0)


def swapped(pairs):
    return list(pairs) + [(b, a) for a, b in pairs]


def swap_lon(x):
    count = lax.axis_size("lon")
    first = swapped([(i, i + 1) for i in range(0, count, 2)])
    second = swapped([(i, (i + 1) % count) for i in range(1, count, 2)])
    second = lax.ppermute(x, "lon", second)
    return lax.ppermute(x, "lon", first), second


def swap_lat(x, y):
    lon_count, lat_count = lax.axis_size("lon"), lax.axis_size("lat")
    first, second = [], []
    for p in range(lon_count):
        base = p * lat_count
        first += [(base + r, base + r + 1) for r in range(0, lat_count, 2)]
        second += [(base + r, base + r + 1) for r in range(1, lat_count - 1, 2)]
        if p < lon_count // 2:
            second.append((base + lat_count - 1, (lon_count - p) * lat_count - 1))
    y = lax.ppermute(y, ("lon", "lat"), swapped(second))
    x = lax.ppermute(x, ("lon", "lat"), swapped(first))
    return x, y


def call(kernel, outs, scratch=(), operands=1, unread=0, cost=1000000, limit=16):
    def vmem():
        return pl.BlockSpec(memory_space=pltpu.VMEM)

    specs = [vmem()] * operands
    specs += [pl.BlockSpec(memory_space=pl.ANY)] * unread
    single = len(outs) == 1
    shapes = [jax.ShapeDtypeStruct(shape, F32) for shape in outs]
    return pl.pallas_call(
        kernel,
        out_shape=shapes[0] if single else shapes,
        in_specs=specs,
        out_specs=vmem() if single else [vmem() for _ in outs],
        scratch_shapes=[pltpu.VMEM(shape, F32) for shape in scratch],
        cost_estimate=pl.CostEstimate(flops=cost, bytes_accessed=cost, transcendentals=0),
        compiler_params=pltpu.CompilerParams(vmem_limit_bytes=limit << 20),
    )


def on_device(ocean, surface, levels):
    tile = (ROWS, COLS)
    rim = (ROWS + 16, COLS)
    own = pl.pallas_call(
        pack_kernel,
        out_shape=jax.ShapeDtypeStruct((5, *tile), F32),
        in_specs=[pl.BlockSpec(memory_space=pl.ANY)] * 2,
        out_specs=pl.BlockSpec(memory_space=pltpu.VMEM),
        scratch_shapes=[
            pltpu.VMEM(ocean.shape, F32),
            pltpu.VMEM(tile, jnp.int32),
            pltpu.SemaphoreType.DMA((4,)),
            pltpu.SemaphoreType.DMA(()),
        ],
    )(ocean, levels)
    lon_0, lon_1 = swap_lon(own)
    lat_index, lat_count = lax.axis_index("lat"), lax.axis_size("lat")
    own = jnp.where(lat_index < 0, 0.0, own)
    row = lat_index * ROWS + lax.broadcasted_iota(jnp.int32, tile, 0)
    latitude = (row.astype(F32) + 0.5) / float(lat_count * ROWS)
    coriolis = jnp.sin(math.pi * latitude - 0.5 * math.pi)
    momentum_scratch = [(2, *tile), (4, *tile), tile, tile, tile]
    outer_accel, faces, lat_0, lat_1, outer_sums = call(
        outer_kernel,
        [(2, LEVELS, 2, 8, COLS), (2, LEVELS, 8, COLS), (PIECES, 8, COLS), (PIECES, 8, COLS), (4, *tile)],
        scratch=momentum_scratch,
        operands=7,
    )(ocean, levels, surface, coriolis, own, lon_0, lon_1)
    lat_0, lat_1 = swap_lat(lat_0, lat_1)
    accel, sums = call(
        inner_kernel,
        [(2, LEVELS, *tile), (4, *tile)],
        scratch=momentum_scratch,
        operands=9,
        cost=100000000,
    )(ocean, levels, coriolis, own, lon_0, lon_1, outer_accel, faces, outer_sums)
    tracers = call(
        tracer_kernel,
        [(2, LEVELS, *tile)],
        scratch=[(2, *tile), (3, *tile), tile],
        operands=5,
        unread=1,
        cost=100000000,
    )(ocean, levels, own, lon_0, lon_1, sums)
    edges, fields, packed, means, south, north = call(
        edge_kernel,
        [(2, 2, LEVELS, 8, COLS), (6, *rim), rim, (2, *tile), (PIECES, 8, COLS), (PIECES, 8, COLS)],
        scratch=[(2, 2, 8, COLS), (2, 2, 8, COLS)],
        operands=6,
        unread=1,
    )(ocean, levels, surface, sums, lat_0, lat_1, tracers)
    rim_0, rim_1 = swap_lon(packed)
    tracer_edges = call(tracer_edge_kernel, [(2, 2, LEVELS, 8, COLS)], operands=4)(ocean, levels, south, north)
    return call(final_kernel, [(4, LEVELS, *tile), (3, *tile)], scratch=[(2, *tile)], operands=10)(
        ocean, levels, accel, tracers, edges, tracer_edges, fields, means, rim_0, rim_1
    )


def solution(mesh):
    return jax.shard_map(
        on_device,
        mesh=mesh,
        in_specs=(P(None, None, "lat", "lon"), P(None, "lat", "lon"), P("lat", "lon")),
        out_specs=(P(None, None, "lat", "lon"), P(None, "lat", "lon")),
        check_vma=False,
    )
```

```python
import functools
import math

import jax
import jax.numpy as jnp
from jax import lax
from jax.experimental import pallas as pl
from jax.experimental.pallas import tpu as pltpu
from jax.sharding import PartitionSpec as P


NSUB = 4
LEVELS = 16
ROWS = 32
COLS = 128
BLOCKS = ROWS // 8
THICKNESS = 1.0 / LEVELS
TRACER_STEP = 0.1
SURFACE_STEP = 1.2
PIECES = 2 * LEVELS + 6

F32 = jnp.float32


def even_tile(axis):
    return lax.rem(lax.axis_index(axis), 2) == 0


def lane_index(rows=8):
    return lax.broadcasted_iota(jnp.int32, (rows, COLS), 1)


def row_index(rows=8):
    return lax.broadcasted_iota(jnp.int32, (rows, COLS), 0)


def roll(x, shift, axis):
    if isinstance(shift, int):
        shift %= x.shape[axis]
        if shift == 0:
            return x
    return pltpu.roll(x, shift, axis)


def upwind_flux(speed, qm2, qm1, q0, q1, q2, q3):
    ahead = speed >= 0.0
    a = jnp.where(ahead, qm2, q3)
    b = jnp.where(ahead, qm1, q2)
    c = jnp.where(ahead, q0, q1)
    d = jnp.where(ahead, q1, q0)
    e = jnp.where(ahead, q2, qm1)
    ab = a - b
    bc = b - c
    cd = c - d
    de = d - e
    x1 = ab - bc
    y1 = ab - 3.0 * bc
    x2 = bc - cd
    y2 = bc + cd
    x3 = cd - de
    y3 = 3.0 * cd - de
    third = 13.0 / 3.0
    s1 = third * (x1 * x1) + (y1 * y1 + 4e-6)
    s2 = third * (x2 * x2) + (y2 * y2 + 4e-6)
    s3 = third * (x3 * x3) + (y3 * y3 + 4e-6)
    r1 = s2 * s3
    r2 = s1 * s3
    r3 = s1 * s2
    w1 = r1 * r1
    w2 = 6.0 * (r2 * r2)
    w3 = 3.0 * (r3 * r3)
    top = w1 * (2.0 * ab - 5.0 * bc) - w2 * (bc + 2.0 * cd) + w3 * (de - 4.0 * cd)
    low = 6.0 * (w1 + w2 + w3)
    return speed * (c + top / low)


def density(t, s, wet):
    return wet * (t * (0.03 * s - 0.2 - 0.05 * t) + 0.8 * s)


def wet_of(level_map, k):
    return jnp.where(level_map > k, 1.0, 0.0).astype(F32)


def pack_kernel(ocean_hbm, levels_hbm, out, ocean, levels, sems, level_sem):
    copies = [pltpu.make_async_copy(ocean_hbm.at[q], ocean.at[q], sems.at[q]) for q in range(4)]
    level_copy = pltpu.make_async_copy(levels_hbm, levels, level_sem)
    for copy in copies:
        copy.start()
    level_copy.start()
    group = lane_index() // 8
    for q in range(4):
        copies[q].wait()
        for b in range(BLOCKS):
            rows = pl.ds(8 * b, 8)
            packed = jnp.zeros((8, COLS), F32)
            for k in range(LEVELS):
                packed = jnp.where(group == k, roll(ocean[q, k, rows, :], 8 * k + 4, 1), packed)
            out[q, rows, :] = packed
    level_copy.wait()
    for b in range(BLOCKS):
        rows = pl.ds(8 * b, 8)
        out[4, rows, :] = roll(levels[rows, :].astype(F32), 4, 1)


def low_piece(q, rows, even, swaps):
    return jnp.where(even, swaps[1][q, rows, :], swaps[0][q, rows, :])


def halo_pack(q, rows, even, swaps):
    from_low = lane_index() % 8 < 4
    high = jnp.where(even, swaps[0][q, rows, :], swaps[1][q, rows, :])
    return jnp.where(from_low, low_piece(q, rows, even, swaps), high)


def next_lon(main, halo, step):
    lane = lane_index()
    if step > 0:
        return roll(jnp.where(lane < step, halo, main), -step, 1)
    return roll(jnp.where(lane >= COLS + step, halo, main), -step, 1)


def lon_shifts(main, halo):
    return [main if d == 0 else next_lon(main, halo, d) for d in (-2, -1, 0, 1, 2, 3)]


def west_faces(own, swaps, levels, quantities, halo_quantities, packed, lev_halo, west_flux, blocks):
    lane = lane_index()
    from_low = lane % 8 < 4
    level_of = lane // 8
    even = even_tile("lon")
    for b in blocks:
        rows = pl.ds(8 * b, 8)
        lev = levels[rows, :].astype(F32)
        own_col = lev[:, 0:1]
        west_col = low_piece(4, rows, even, swaps)[:, 3:4]
        both = jnp.minimum(own_col, west_col)
        wet = jnp.where(both > level_of.astype(F32), 1.0, 0.0)
        u = jnp.where(from_low, low_piece(2, rows, even, swaps), own[2, rows, :])
        speed = 0.5 * (u + roll(u, -1, 1)) * wet
        for n, q in enumerate(quantities):
            x = jnp.where(from_low, low_piece(q, rows, even, swaps), own[q, rows, :])
            west_flux[n, rows, :] = upwind_flux(speed, *[roll(x, -d, 1) for d in (-2, -1, 0, 1, 2, 3)])
        for q in halo_quantities:
            packed[q, rows, :] = halo_pack(q, rows, even, swaps)
        lev_halo[rows, :] = roll(halo_pack(4, rows, even, swaps), -4, 1)


def lat_shift(ocean, q, k, b, d):
    start = 8 * b + d
    if 0 <= start and start + 8 <= ROWS:
        return ocean[q, k, start : start + 8, :]
    return roll(ocean[q, k, pl.ds(8 * b, 8), :], -d, 0)


def level_map_shift(levels, b, d):
    start = 8 * b + d
    if 0 <= start and start + 8 <= ROWS:
        return levels[start : start + 8, :].astype(F32)
    return roll(levels[pl.ds(8 * b, 8), :].astype(F32), -d, 0)


def lat_terms(ocean, levels, k, quantities, blocks, last):
    sub = row_index()
    result = {}
    for b in blocks:
        rows = pl.ds(8 * b, 8)
        wet = wet_of(levels[rows, :].astype(F32), k)
        wet_north = wet_of(level_map_shift(levels, b, 1), k)
        speed = 0.5 * (ocean[3, k, rows, :] + lat_shift(ocean, 3, k, b, 1)) * (wet * wet_north)
        for n, q in enumerate(quantities):
            north = upwind_flux(speed, *[lat_shift(ocean, q, k, b, d) for d in (-2, -1, 0, 1, 2, 3)])
            if b == 0:
                north = jnp.where(sub >= 2, north, 0.0)
            if b == BLOCKS - 1:
                north = jnp.where(sub <= 4, north, 0.0)
            last[n, b] = roll(north, 1, 0)
            south = jnp.where(sub == 0, last.get((n, b - 1), 0.0), last[n, b])
            result[n, b] = north - south
    return result


def lon_terms(ocean, levels, k, halo_of, lev_halo, quantities, west_flux, blocks):
    lane = lane_index()
    unplace = 124 - 8 * k
    result = {}
    for b in blocks:
        rows = pl.ds(8 * b, 8)
        lev = levels[rows, :].astype(F32)
        wet = wet_of(lev, k)
        u = ocean[2, k, rows, :]
        wet_east = wet_of(next_lon(lev, lev_halo[rows, :], 1), k)
        speed = 0.5 * (u + next_lon(u, halo_of(2, rows), 1)) * (wet * wet_east)
        for n, q in enumerate(quantities):
            main = ocean[q, k, rows, :]
            east = upwind_flux(speed, *lon_shifts(main, halo_of(q, rows)))
            west = pltpu.roll(west_flux[n, rows, :], unplace, 1)
            west = roll(jnp.where(lane == COLS - 1, west, east), 1, 1)
            result[n, b] = east - west
    return result


def halo_reader(packed, k):
    halo = {}

    def halo_of(q, rows):
        key = (q, rows.start)
        if key not in halo:
            halo[key] = pltpu.roll(packed[q, rows, :], 124 - 8 * k, 1)
        return halo[key]

    return halo_of


def momentum_level(ocean, levels, coriolis, k, packed, lev_halo, west_flux, cum, cum_halo, blocks, lat):
    sub = row_index()
    halo_of = halo_reader(packed, k)
    lon = lon_terms(ocean, levels, k, halo_of, lev_halo, (2, 3), west_flux, blocks)
    pressure, pressure_halo = [], {}
    for b in range(BLOCKS):
        rows = pl.ds(8 * b, 8)
        here = density(ocean[0, k, rows, :], ocean[1, k, rows, :], wet_of(levels[rows, :].astype(F32), k))
        total = cum[rows, :] + here
        cum[rows, :] = total
        pressure.append(THICKNESS * (total - 0.5 * here))
    for b in blocks:
        rows = pl.ds(8 * b, 8)
        here = density(halo_of(0, rows), halo_of(1, rows), wet_of(lev_halo[rows, :], k))
        total = cum_halo[rows, :] + here
        cum_halo[rows, :] = total
        pressure_halo[b] = THICKNESS * (total - 0.5 * here)
    result = {}
    for b in blocks:
        rows = pl.ds(8 * b, 8)
        wet = wet_of(levels[rows, :].astype(F32), k)
        grad_lon = 0.5 * (
            next_lon(pressure[b], pressure_halo[b], 1) - next_lon(pressure[b], pressure_halo[b], -1)
        )
        ahead = pressure[b] if b == BLOCKS - 1 else jnp.where(sub == 0, pressure[b + 1], pressure[b])
        behind = pressure[b] if b == 0 else jnp.where(sub == 7, pressure[b - 1], pressure[b])
        grad_lat = 0.5 * (roll(ahead, -1, 0) - roll(behind, 1, 0))
        if b == 0:
            grad_lat = jnp.where(sub >= 1, grad_lat, 0.0)
        if b == BLOCKS - 1:
            grad_lat = jnp.where(sub <= 6, grad_lat, 0.0)
        u, v, turn = ocean[2, k, rows, :], ocean[3, k, rows, :], coriolis[rows, :]
        accel_u = wet * (turn * v - grad_lon - (lon[0, b] + lat[0, b]))
        accel_v = wet * (-turn * u - grad_lat - (lon[1, b] + lat[1, b]))
        result[b] = (accel_u, accel_v, wet * u, wet * v)
    return result


OUTER = (0, BLOCKS - 1)
INNER = tuple(range(1, BLOCKS - 1))


def early_kernel(ocean, levels, lat, faces):
    def level(k, carry):
        last = {}
        terms = lat_terms(ocean, levels, k, (2, 3), OUTER, last)
        for n in range(2):
            for side, b in enumerate(OUTER):
                lat[n, k, side] = terms[n, b]
            faces[n, k] = last[n, 0]
        return carry

    lax.fori_loop(0, LEVELS, level, 0)


def outer_kernel(
    ocean, levels, surface, coriolis, own, swap_0, swap_1, lat,
    accel, even_out, odd_out, sums, west_flux, packed, cum, cum_halo, lev_halo,
):
    sub = row_index()
    even_lat = even_tile("lat")
    west_faces(
        own, (swap_0, swap_1), levels, (2, 3), (0, 1, 2, 3), packed, lev_halo, west_flux, OUTER
    )
    cum[...] = jnp.zeros_like(cum)
    cum_halo[...] = jnp.zeros_like(cum_halo)
    sums[...] = jnp.zeros_like(sums)

    def send(index, south, north):
        even_out[index] = jnp.where(even_lat, north, south)
        odd_out[index] = jnp.where(even_lat, south, north)

    first, last_rows = pl.ds(0, 8), pl.ds(ROWS - 8, 8)

    def level(k, carry):
        for pair in range(2):
            t0, t3 = ocean[pair, k, first, :], ocean[pair, k, last_rows, :]
            u0, u3 = ocean[pair + 2, k, first, :], ocean[pair + 2, k, last_rows, :]
            send(
                pair * LEVELS + k,
                jnp.where(sub < 5, u0, roll(t0, 5, 0)),
                jnp.where(sub < 3, roll(t3, 3, 0), u3),
            )
        given = {(n, b): lat[n, k, side] for n in range(2) for side, b in enumerate(OUTER)}
        terms = momentum_level(
            ocean, levels, coriolis, k, packed, lev_halo, west_flux, cum, cum_halo, OUTER, given
        )
        for side, b in enumerate(OUTER):
            for n in range(2):
                accel[n, k, side] = terms[b][n]
            for n in range(4):
                sums[n, pl.ds(8 * b, 8), :] += terms[b][n]
        return carry

    lax.fori_loop(0, LEVELS, level, 0)
    flat = [sums.at[0], sums.at[1], surface.at[0], surface.at[1], surface.at[2], levels]
    for n, field in enumerate(flat):
        send(2 * LEVELS + n, field[first, :].astype(F32), field[last_rows, :].astype(F32))


def inner_kernel(
    ocean, levels, coriolis, own, swap_0, swap_1, outer_accel, faces, outer_sums,
    accel, sums, west_flux, packed, cum, cum_halo, lev_halo,
):
    sub = row_index()
    west_faces(
        own, (swap_0, swap_1), levels, (2, 3), (0, 1, 2, 3), packed, lev_halo, west_flux, INNER
    )
    cum[...] = jnp.zeros_like(cum)
    cum_halo[...] = jnp.zeros_like(cum_halo)
    sums[...] = outer_sums[...]
    top_rows = pl.ds(ROWS - 8, 8)

    def level(k, carry):
        last = {(n, 0): faces[n, k] for n in range(2)}
        lat = lat_terms(ocean, levels, k, (2, 3), INNER, last)
        terms = momentum_level(
            ocean, levels, coriolis, k, packed, lev_halo, west_flux, cum, cum_halo, INNER, lat
        )
        for b in INNER:
            rows = pl.ds(8 * b, 8)
            for n in range(4):
                if n < 2:
                    accel[n, k, rows, :] = terms[b][n]
                sums[n, rows, :] += terms[b][n]
        wet = wet_of(levels[top_rows, :].astype(F32), k)
        for n in range(2):
            south_face = wet * jnp.where(sub == 0, last[n, BLOCKS - 2], 0.0)
            accel[n, k, pl.ds(0, 8), :] = outer_accel[n, k, 0]
            accel[n, k, top_rows, :] = outer_accel[n, k, 1] + south_face
            sums[n, top_rows, :] += south_face
        return carry

    lax.fori_loop(0, LEVELS, level, 0)


def tracer_kernel(q, ocean, levels, own, swap_0, swap_1, after, tracer, west_flux, packed, lev_halo):
    del after
    blocks = range(BLOCKS)
    west_faces(own, (swap_0, swap_1), levels, (q,), (q, 2), packed, lev_halo, west_flux, blocks)

    def level(k, carry):
        halo_of = halo_reader(packed, k)
        lon = lon_terms(ocean, levels, k, halo_of, lev_halo, (q,), west_flux, blocks)
        lat = lat_terms(ocean, levels, k, (q,), blocks, {})
        for b in blocks:
            rows = pl.ds(8 * b, 8)
            wet = wet_of(levels[rows, :].astype(F32), k)
            tracer[k, rows, :] = wet * (ocean[q, k, rows, :] - TRACER_STEP * (lon[0, b] + lat[0, b]))
        return carry

    lax.fori_loop(0, LEVELS, level, 0)


def window(low_block, high_block, d):
    if d == 8:
        return high_block
    return roll(jnp.where(row_index() >= d, low_block, high_block), -d, 0)


def edge_blocks(ocean, arrived, q, k, side):
    own = ocean[q, k, pl.ds(0 if side == 0 else ROWS - 8, 8), :]
    piece = arrived[(q % 2) * LEVELS + k]
    if side == 0:
        return (roll(piece, 5, 0) if q < 2 else piece), own
    return own, (roll(piece, 3, 0) if q < 2 else piece)


def edge_levels(levels, arrived, side):
    own = levels[pl.ds(0 if side == 0 else ROWS - 8, 8), :].astype(F32)
    return (arrived[PIECES - 1], own) if side == 0 else (own, arrived[PIECES - 1])


def edge_terms(ocean, k, arrived, side, lev5, lev6, quantities):
    sub = row_index()
    v = edge_blocks(ocean, arrived, 3, k, side)
    speed = 0.5 * (window(*v, 5) + window(*v, 6)) * wet_of(jnp.minimum(lev5, lev6), k)
    terms = []
    for q in quantities:
        x = v if q == 3 else edge_blocks(ocean, arrived, q, k, side)
        flux = upwind_flux(speed, *[window(*x, d) for d in (3, 4, 5, 6, 7, 8)])
        flux = jnp.where(sub < 5, flux, 0.0)
        terms.append(flux - jnp.where(sub == 0, 0.0, roll(flux, 1, 0)))
    return terms


def own_rows(term, side):
    sub = row_index()
    if side == 0:
        return jnp.where(sub < 3, roll(term, -3, 0), 0.0)
    return jnp.where(sub >= 5, roll(term, 5, 0), 0.0)


def halo_rows(term, side):
    sub = row_index()
    if side == 0:
        return jnp.where(sub >= 5, roll(term, 5, 0), 0.0)
    return jnp.where(sub < 3, roll(term, -3, 0), 0.0)


def place_arrivals(up, down, south, north):
    even_lat = even_tile("lat")
    at_south = lax.axis_index("lat") == 0
    at_fold = lax.axis_index("lat") == lax.axis_size("lat") - 1
    turned_row, turned_lane = 7 - row_index(), COLS - 1 - lane_index()
    pair_sign = jnp.where(row_index() < 5, -1.0, 1.0)

    def piece(n, sign):
        south[n] = jnp.where(at_south, 0.0, jnp.where(even_lat, down[n], up[n]))
        here = jnp.where(even_lat, up[n], down[n])
        turned = jnp.take_along_axis(jnp.take_along_axis(here, turned_lane, axis=1), turned_row, axis=0)
        north[n] = jnp.where(at_fold, turned * sign, here)

    def pairs(first, carry):
        for n in range(8):
            piece(8 * first + n, pair_sign)
        return carry

    lax.fori_loop(0, 2 * LEVELS // 8, pairs, 0)
    for n, sign in enumerate((-1.0, -1.0, 1.0, -1.0, -1.0, 1.0)):
        piece(2 * LEVELS + n, sign)


def edge_kernel(
    ocean, levels, surface, sums, up, down, after,
    edges, fields, packed, means, south, north, cum, total,
):
    del after
    place_arrivals(up, down, south, north)
    sub = row_index()
    cum[...] = jnp.zeros_like(cum)
    total[...] = jnp.zeros_like(total)
    arrived = (south, north)

    def level(k, carry):
        for side in range(2):
            lev = edge_levels(levels, arrived[side], side)
            lev5, lev6 = window(*lev, 5), window(*lev, 6)
            terms = edge_terms(ocean, k, arrived[side], side, lev5, lev6, (2, 3))
            t = edge_blocks(ocean, arrived[side], 0, k, side)
            s = edge_blocks(ocean, arrived[side], 1, k, side)
            pressure = []
            for half in range(2):
                here = density(t[half], s[half], wet_of(lev[half], k))
                column = cum[side, half] + here
                cum[side, half] = column
                pressure.append(THICKNESS * (column - 0.5 * here))
            grad = 0.5 * (window(*pressure, 6) - window(*pressure, 4))
            grad = jnp.where((sub == 2) | (sub == 3), grad, 0.0)
            wet = wet_of(lev5, k)
            for n, term in enumerate((-wet * terms[0], -wet * (terms[1] + grad))):
                total[side, n] += term
                edges[side, n, k] = own_rows(term, side)
        return carry

    lax.fori_loop(0, LEVELS, level, 0)
    rim = ROWS + 16
    own = pl.ds(8, ROWS)
    for n in range(3):
        fields[n, pl.ds(0, 8), :] = south[2 * LEVELS + 2 + n]
        fields[n, own, :] = surface[n]
        fields[n, pl.ds(rim - 8, 8), :] = north[2 * LEVELS + 2 + n]
    fields[3, pl.ds(0, 8), :] = south[PIECES - 1]
    fields[3, own, :] = levels[...].astype(F32)
    fields[3, pl.ds(rim - 8, 8), :] = north[PIECES - 1]
    for n in range(2):
        fields[4 + n, pl.ds(0, 8), :] = south[2 * LEVELS + n] + halo_rows(total[0, n], 0)
        fields[4 + n, own, :] = sums[n]
        fields[4 + n, pl.ds(8, 8), :] += own_rows(total[0, n], 0)
        fields[4 + n, pl.ds(ROWS, 8), :] += own_rows(total[1, n], 1)
        fields[4 + n, pl.ds(rim - 8, 8), :] = north[2 * LEVELS + n] + halo_rows(total[1, n], 1)
    for n in range(2):
        safe = jnp.maximum(THICKNESS * levels[...].astype(F32), THICKNESS)
        means[n] = THICKNESS * (sums[2 + n] + TRACER_STEP * fields[4 + n, own, :]) / safe
    for b in range(rim // 8):
        rows = pl.ds(8 * b, 8)
        safe = jnp.maximum(THICKNESS * fields[3, rows, :], THICKNESS)
        group = lane_index() // 16
        out = jnp.zeros((8, COLS), F32)
        for n in range(6):
            if n >= 4:
                fields[n, rows, :] = THICKNESS * fields[n, rows, :] / safe
            out = jnp.where(group == n, roll(fields[n, rows, :], 16 * n + 8, 1), out)
        packed[rows, :] = out


def tracer_edge_kernel(ocean, levels, south, north, edges):
    arrived = (south, north)

    def level(k, carry):
        for side in range(2):
            lev = edge_levels(levels, arrived[side], side)
            lev5, lev6 = window(*lev, 5), window(*lev, 6)
            wet = wet_of(lev5, k)
            terms = edge_terms(ocean, k, arrived[side], side, lev5, lev6, (0, 1))
            for n in range(2):
                edges[side, n, k] = own_rows(-wet * terms[n], side)
        return carry

    lax.fori_loop(0, LEVELS, level, 0)


def final_kernel(
    ocean, levels, accel, temperature, salinity, edges, tracer_edges, fields, means, swap_0, swap_1,
    ocean_out, surface_out, shift,
):
    rim = ROWS + 16
    lane = lane_index(rim)
    even = even_tile("lon")
    low = jnp.where(even, swap_1[...], swap_0[...])
    high = jnp.where(even, swap_0[...], swap_1[...])
    halos = jnp.where(lane % 16 < 8, low, high)
    both = []
    for n in range(6):
        both.append((fields[n], roll(halos, -(16 * n + 8), 1)))
    height, mean_u, mean_v, level_map, force_lon, force_lat = both
    depth = tuple(THICKNESS * x for x in level_map)
    sea = tuple(jnp.where(x > 0.0, 1.0, 0.0) for x in level_map)

    def d_lon(x):
        main, halo = x
        result = []
        for here, other in ((main, halo), (halo, main)):
            ahead = roll(jnp.where(lane == 0, other, here), -1, 1)
            behind = roll(jnp.where(lane == COLS - 1, other, here), 1, 1)
            result.append(0.5 * (ahead - behind))
        return result

    def d_lat(x):
        return [0.5 * (roll(part, -1, 0) - roll(part, 1, 0)) for part in x]

    def times(x, y):
        return [p * q for p, q in zip(x, y)]

    for _ in range(NSUB):
        along, across = d_lon(times(depth, mean_u)), d_lat(times(depth, mean_v))
        height = [s * (h - SURFACE_STEP * (p + q)) for s, h, p, q in zip(sea, height, along, across)]
        mean_u = [
            s * (m + SURFACE_STEP * (f - d)) for s, m, f, d in zip(sea, mean_u, force_lon, d_lon(height))
        ]
        mean_v = [
            s * (m + SURFACE_STEP * (f - d)) for s, m, f, d in zip(sea, mean_v, force_lat, d_lat(height))
        ]
    for n, field in enumerate((height, mean_u, mean_v)):
        surface_out[n] = field[0][8 : 8 + ROWS]
    shift[0] = mean_u[0][8 : 8 + ROWS] - means[0]
    shift[1] = mean_v[0][8 : 8 + ROWS] - means[1]

    def level(k, carry):
        for b in range(BLOCKS):
            rows = pl.ds(8 * b, 8)
            wet = wet_of(levels[rows, :].astype(F32), k)
            for n in range(2):
                tracer, force = (temperature, salinity)[n][k, rows, :], accel[n, k, rows, :]
                if b in (0, BLOCKS - 1):
                    side = min(b, 1)
                    tracer = tracer + TRACER_STEP * tracer_edges[side, n, k]
                    force = force + edges[side, n, k]
                ocean_out[n, k, rows, :] = tracer
                ocean_out[2 + n, k, rows, :] = wet * (
                    ocean[2 + n, k, rows, :] + TRACER_STEP * force + shift[n, rows, :]
                )
        return carry

    lax.fori_loop(0, LEVELS, level, 0)


def swapped(pairs):
    return list(pairs) + [(b, a) for a, b in pairs]


def swap_lon(x):
    count = lax.axis_size("lon")
    first = swapped([(i, i + 1) for i in range(0, count, 2)])
    second = swapped([(i, (i + 1) % count) for i in range(1, count, 2)])
    second = lax.ppermute(x, "lon", second)
    return lax.ppermute(x, "lon", first), second


def swap_lat(x, y):
    lon_count, lat_count = lax.axis_size("lon"), lax.axis_size("lat")
    first, second = [], []
    for p in range(lon_count):
        base = p * lat_count
        first += [(base + r, base + r + 1) for r in range(0, lat_count, 2)]
        second += [(base + r, base + r + 1) for r in range(1, lat_count - 1, 2)]
        if p < lon_count // 2:
            second.append((base + lat_count - 1, (lon_count - p) * lat_count - 1))
    y = lax.ppermute(y, ("lon", "lat"), swapped(second))
    x = lax.ppermute(x, ("lon", "lat"), swapped(first))
    return x, y


def call(kernel, outs, scratch=(), operands=1, unread=0, cost=1000000, limit=16):
    def vmem():
        return pl.BlockSpec(memory_space=pltpu.VMEM)

    specs = [vmem()] * operands
    specs += [pl.BlockSpec(memory_space=pl.ANY)] * unread
    single = len(outs) == 1
    shapes = [jax.ShapeDtypeStruct(shape, F32) for shape in outs]
    return pl.pallas_call(
        kernel,
        out_shape=shapes[0] if single else shapes,
        in_specs=specs,
        out_specs=vmem() if single else [vmem() for _ in outs],
        scratch_shapes=[pltpu.VMEM(shape, F32) for shape in scratch],
        cost_estimate=pl.CostEstimate(flops=cost, bytes_accessed=cost, transcendentals=0),
        compiler_params=pltpu.CompilerParams(vmem_limit_bytes=limit << 20),
    )


def on_device(ocean, surface, levels):
    tile = (ROWS, COLS)
    rim = (ROWS + 16, COLS)
    own = pl.pallas_call(
        pack_kernel,
        out_shape=jax.ShapeDtypeStruct((5, *tile), F32),
        in_specs=[pl.BlockSpec(memory_space=pl.ANY)] * 2,
        out_specs=pl.BlockSpec(memory_space=pltpu.VMEM),
        scratch_shapes=[
            pltpu.VMEM(ocean.shape, F32),
            pltpu.VMEM(tile, jnp.int32),
            pltpu.SemaphoreType.DMA((4,)),
            pltpu.SemaphoreType.DMA(()),
        ],
    )(ocean, levels)
    lon_0, lon_1 = swap_lon(own)
    lat_index, lat_count = lax.axis_index("lat"), lax.axis_size("lat")
    own = jnp.where(lat_index < 0, 0.0, own)
    row = lat_index * ROWS + lax.broadcasted_iota(jnp.int32, tile, 0)
    latitude = (row.astype(F32) + 0.5) / float(lat_count * ROWS)
    coriolis = jnp.sin(math.pi * latitude - 0.5 * math.pi)
    momentum_scratch = [(2, *tile), (4, *tile), tile, tile, tile]
    half = (2, LEVELS, 2, 8, COLS)
    arrivals = [(PIECES, 8, COLS)] * 2
    lat_part, faces = call(early_kernel, [half, (2, LEVELS, 8, COLS)], operands=2, cost=100000000)(ocean, levels)
    outer_accel, lat_0, lat_1, outer_sums = call(
        outer_kernel,
        [half, *arrivals, (4, *tile)],
        scratch=momentum_scratch,
        operands=8,
    )(ocean, levels, surface, coriolis, own, lon_0, lon_1, lat_part)
    lat_0, lat_1 = swap_lat(lat_0, lat_1)
    accel, sums = call(
        inner_kernel,
        [(2, LEVELS, *tile), (4, *tile)],
        scratch=momentum_scratch,
        operands=9,
        cost=100000000,
    )(ocean, levels, coriolis, own, lon_0, lon_1, outer_accel, faces, outer_sums)

    def tracer(q, after):
        return call(
            functools.partial(tracer_kernel, q),
            [(LEVELS, *tile)],
            scratch=[(1, *tile), (3, *tile), tile],
            operands=5,
            unread=1,
            cost=100000000,
        )(ocean, levels, own, lon_0, lon_1, after)

    temperature = tracer(0, sums)
    edges, fields, packed, means, south, north = call(
        edge_kernel,
        [(2, 2, LEVELS, 8, COLS), (6, *rim), rim, (2, *tile), *arrivals],
        scratch=[(2, 2, 8, COLS), (2, 2, 8, COLS)],
        operands=6,
        unread=1,
    )(ocean, levels, surface, sums, lat_0, lat_1, temperature)
    rim_0, rim_1 = swap_lon(packed)
    tracer_edges = call(
        tracer_edge_kernel, [(2, 2, LEVELS, 8, COLS)], operands=4, cost=100000000
    )(ocean, levels, south, north)
    salinity = tracer(1, means)
    return call(final_kernel, [(4, LEVELS, *tile), (3, *tile)], scratch=[(2, *tile)], operands=11)(
        ocean, levels, accel, temperature, salinity, edges, tracer_edges, fields, means, rim_0, rim_1
    )


def solution(mesh):
    return jax.shard_map(
        on_device,
        mesh=mesh,
        in_specs=(P(None, None, "lat", "lon"), P(None, "lat", "lon"), P("lat", "lon")),
        out_specs=(P(None, None, "lat", "lon"), P(None, "lat", "lon")),
        check_vma=False,
    )
```

```python
import functools
import math

import jax
import jax.numpy as jnp
from jax import lax
from jax.experimental import pallas as pl
from jax.experimental.pallas import tpu as pltpu
from jax.sharding import PartitionSpec as P


NSUB = 4
LEVELS = 16
ROWS = 32
COLS = 128
PER_STEP = 4
BLOCKS = ROWS // 8
THICKNESS = 1.0 / LEVELS
TRACER_STEP = 0.1
SURFACE_STEP = 1.2
PIECES = 2 * LEVELS + 6

F32 = jnp.float32


def over_levels(level):
    def step(i, carry):
        for j in range(PER_STEP):
            level(PER_STEP * i + j, carry)
        return carry

    lax.fori_loop(0, LEVELS // PER_STEP, step, 0)


def even_tile(axis):
    return lax.rem(lax.axis_index(axis), 2) == 0


def lane_index(rows=8):
    return lax.broadcasted_iota(jnp.int32, (rows, COLS), 1)


def row_index(rows=8):
    return lax.broadcasted_iota(jnp.int32, (rows, COLS), 0)


def roll(x, shift, axis):
    if isinstance(shift, int):
        shift %= x.shape[axis]
        if shift == 0:
            return x
    return pltpu.roll(x, shift, axis)


def upwind_flux(speed, qm2, qm1, q0, q1, q2, q3):
    ahead = speed >= 0.0
    a = jnp.where(ahead, qm2, q3)
    b = jnp.where(ahead, qm1, q2)
    c = jnp.where(ahead, q0, q1)
    d = jnp.where(ahead, q1, q0)
    e = jnp.where(ahead, q2, qm1)
    ab = a - b
    bc = b - c
    cd = c - d
    de = d - e
    x1 = ab - bc
    y1 = ab - 3.0 * bc
    x2 = bc - cd
    y2 = bc + cd
    x3 = cd - de
    y3 = 3.0 * cd - de
    third = 13.0 / 3.0
    s1 = third * (x1 * x1) + (y1 * y1 + 4e-6)
    s2 = third * (x2 * x2) + (y2 * y2 + 4e-6)
    s3 = third * (x3 * x3) + (y3 * y3 + 4e-6)
    r1 = s2 * s3
    r2 = s1 * s3
    r3 = s1 * s2
    w1 = r1 * r1
    w2 = 6.0 * (r2 * r2)
    w3 = 3.0 * (r3 * r3)
    top = w1 * (2.0 * ab - 5.0 * bc) - w2 * (bc + 2.0 * cd) + w3 * (de - 4.0 * cd)
    low = 6.0 * (w1 + w2 + w3)
    return speed * (c + top / low)


def density(t, s, wet):
    return wet * (t * (0.03 * s - 0.2 - 0.05 * t) + 0.8 * s)


def wet_of(level_map, k):
    return jnp.where(level_map > k, 1.0, 0.0).astype(F32)


def pack_kernel(ocean_hbm, levels_hbm, out, ocean, levels, sems, level_sem):
    copies = [pltpu.make_async_copy(ocean_hbm.at[q], ocean.at[q], sems.at[q]) for q in range(4)]
    level_copy = pltpu.make_async_copy(levels_hbm, levels, level_sem)
    for copy in copies:
        copy.start()
    level_copy.start()
    group = lane_index() // 8
    for q in range(4):
        copies[q].wait()
        for b in range(BLOCKS):
            rows = pl.ds(8 * b, 8)
            packed = jnp.zeros((8, COLS), F32)
            for k in range(LEVELS):
                packed = jnp.where(group == k, roll(ocean[q, k, rows, :], 8 * k + 4, 1), packed)
            out[q, rows, :] = packed
    level_copy.wait()
    for b in range(BLOCKS):
        rows = pl.ds(8 * b, 8)
        out[4, rows, :] = roll(levels[rows, :].astype(F32), 4, 1)


def low_piece(q, rows, even, swaps):
    return jnp.where(even, swaps[1][q, rows, :], swaps[0][q, rows, :])


def halo_pack(q, rows, even, swaps):
    from_low = lane_index() % 8 < 4
    high = jnp.where(even, swaps[0][q, rows, :], swaps[1][q, rows, :])
    return jnp.where(from_low, low_piece(q, rows, even, swaps), high)


def next_lon(main, halo, step):
    lane = lane_index()
    if step > 0:
        return roll(jnp.where(lane < step, halo, main), -step, 1)
    return roll(jnp.where(lane >= COLS + step, halo, main), -step, 1)


def lon_shifts(main, halo):
    return [main if d == 0 else next_lon(main, halo, d) for d in (-2, -1, 0, 1, 2, 3)]


def west_faces(own, swaps, levels, quantities, halo_quantities, packed, lev_halo, west_flux, blocks):
    lane = lane_index()
    from_low = lane % 8 < 4
    level_of = lane // 8
    even = even_tile("lon")
    for b in blocks:
        rows = pl.ds(8 * b, 8)
        lev = levels[rows, :].astype(F32)
        own_col = lev[:, 0:1]
        west_col = low_piece(4, rows, even, swaps)[:, 3:4]
        both = jnp.minimum(own_col, west_col)
        wet = jnp.where(both > level_of.astype(F32), 1.0, 0.0)
        u = jnp.where(from_low, low_piece(2, rows, even, swaps), own[2, rows, :])
        speed = 0.5 * (u + roll(u, -1, 1)) * wet
        for n, q in enumerate(quantities):
            x = jnp.where(from_low, low_piece(q, rows, even, swaps), own[q, rows, :])
            west_flux[n, rows, :] = upwind_flux(speed, *[roll(x, -d, 1) for d in (-2, -1, 0, 1, 2, 3)])
        for q in halo_quantities:
            packed[q, rows, :] = halo_pack(q, rows, even, swaps)
        lev_halo[rows, :] = roll(halo_pack(4, rows, even, swaps), -4, 1)


def lat_shift(ocean, q, k, b, d):
    start = 8 * b + d
    if 0 <= start and start + 8 <= ROWS:
        return ocean[q, k, start : start + 8, :]
    return roll(ocean[q, k, pl.ds(8 * b, 8), :], -d, 0)


def level_map_shift(levels, b, d):
    start = 8 * b + d
    if 0 <= start and start + 8 <= ROWS:
        return levels[start : start + 8, :].astype(F32)
    return roll(levels[pl.ds(8 * b, 8), :].astype(F32), -d, 0)


def lat_terms(ocean, levels, k, quantities, blocks):
    sub = row_index()
    result, last = {}, {}
    for b in blocks:
        rows = pl.ds(8 * b, 8)
        wet = wet_of(levels[rows, :].astype(F32), k)
        wet_north = wet_of(level_map_shift(levels, b, 1), k)
        speed = 0.5 * (ocean[3, k, rows, :] + lat_shift(ocean, 3, k, b, 1)) * (wet * wet_north)
        for n, q in enumerate(quantities):
            north = upwind_flux(speed, *[lat_shift(ocean, q, k, b, d) for d in (-2, -1, 0, 1, 2, 3)])
            if b == 0:
                north = jnp.where(sub >= 2, north, 0.0)
            if b == BLOCKS - 1:
                north = jnp.where(sub <= 4, north, 0.0)
            last[n, b] = roll(north, 1, 0)
            south = jnp.where(sub == 0, last.get((n, b - 1), 0.0), last[n, b])
            result[n, b] = north - south
    return result


def lon_terms(ocean, levels, k, halo_of, lev_halo, quantities, west_flux, blocks):
    lane = lane_index()
    unplace = 124 - 8 * k
    result = {}
    for b in blocks:
        rows = pl.ds(8 * b, 8)
        lev = levels[rows, :].astype(F32)
        wet = wet_of(lev, k)
        u = ocean[2, k, rows, :]
        wet_east = wet_of(next_lon(lev, lev_halo[rows, :], 1), k)
        speed = 0.5 * (u + next_lon(u, halo_of(2, rows), 1)) * (wet * wet_east)
        for n, q in enumerate(quantities):
            main = ocean[q, k, rows, :]
            east = upwind_flux(speed, *lon_shifts(main, halo_of(q, rows)))
            west = pltpu.roll(west_flux[n, rows, :], unplace, 1)
            west = roll(jnp.where(lane == COLS - 1, west, east), 1, 1)
            result[n, b] = east - west
    return result


def halo_reader(packed, k):
    halo = {}

    def halo_of(q, rows):
        key = (q, rows.start)
        if key not in halo:
            halo[key] = pltpu.roll(packed[q, rows, :], 124 - 8 * k, 1)
        return halo[key]

    return halo_of


def momentum_level(ocean, levels, coriolis, k, packed, lev_halo, west_flux, cum, cum_halo, blocks, lat):
    sub = row_index()
    halo_of = halo_reader(packed, k)
    lon = lon_terms(ocean, levels, k, halo_of, lev_halo, (2, 3), west_flux, blocks)
    pressure, pressure_halo = [], {}
    for b in range(BLOCKS):
        rows = pl.ds(8 * b, 8)
        here = density(ocean[0, k, rows, :], ocean[1, k, rows, :], wet_of(levels[rows, :].astype(F32), k))
        total = cum[rows, :] + here
        cum[rows, :] = total
        pressure.append(THICKNESS * (total - 0.5 * here))
    for b in blocks:
        rows = pl.ds(8 * b, 8)
        here = density(halo_of(0, rows), halo_of(1, rows), wet_of(lev_halo[rows, :], k))
        total = cum_halo[rows, :] + here
        cum_halo[rows, :] = total
        pressure_halo[b] = THICKNESS * (total - 0.5 * here)
    result = {}
    for b in blocks:
        rows = pl.ds(8 * b, 8)
        wet = wet_of(levels[rows, :].astype(F32), k)
        grad_lon = 0.5 * (
            next_lon(pressure[b], pressure_halo[b], 1) - next_lon(pressure[b], pressure_halo[b], -1)
        )
        ahead = pressure[b] if b == BLOCKS - 1 else jnp.where(sub == 0, pressure[b + 1], pressure[b])
        behind = pressure[b] if b == 0 else jnp.where(sub == 7, pressure[b - 1], pressure[b])
        grad_lat = 0.5 * (roll(ahead, -1, 0) - roll(behind, 1, 0))
        if b == 0:
            grad_lat = jnp.where(sub >= 1, grad_lat, 0.0)
        if b == BLOCKS - 1:
            grad_lat = jnp.where(sub <= 6, grad_lat, 0.0)
        u, v, turn = ocean[2, k, rows, :], ocean[3, k, rows, :], coriolis[rows, :]
        accel_u = wet * (turn * v - grad_lon - (lon[0, b] + lat[0, b]))
        accel_v = wet * (-turn * u - grad_lat - (lon[1, b] + lat[1, b]))
        result[b] = (accel_u, accel_v, wet * u, wet * v)
    return result


EARLY = (2, 3, 0)
OUTER = (0, BLOCKS - 1)
INNER = tuple(range(1, BLOCKS - 1))


def early_kernel(ocean, levels, lat):
    def level(k, carry):
        terms = lat_terms(ocean, levels, k, EARLY, range(BLOCKS))
        for n in range(len(EARLY)):
            for b in range(BLOCKS):
                lat[n, k, pl.ds(8 * b, 8), :] = terms[n, b]
        return carry

    over_levels(level)


def outer_kernel(
    ocean, levels, surface, coriolis, own, swap_0, swap_1, lat,
    accel, even_out, odd_out, sums, west_flux, packed, cum, cum_halo, lev_halo,
):
    sub = row_index()
    even_lat = even_tile("lat")
    west_faces(
        own, (swap_0, swap_1), levels, (2, 3), (0, 1, 2, 3), packed, lev_halo, west_flux, OUTER
    )
    cum[...] = jnp.zeros_like(cum)
    cum_halo[...] = jnp.zeros_like(cum_halo)
    sums[...] = jnp.zeros_like(sums)

    def send(index, south, north):
        even_out[index] = jnp.where(even_lat, north, south)
        odd_out[index] = jnp.where(even_lat, south, north)

    first, last_rows = pl.ds(0, 8), pl.ds(ROWS - 8, 8)

    def level(k, carry):
        for pair in range(2):
            t0, t3 = ocean[pair, k, first, :], ocean[pair, k, last_rows, :]
            u0, u3 = ocean[pair + 2, k, first, :], ocean[pair + 2, k, last_rows, :]
            send(
                pair * LEVELS + k,
                jnp.where(sub < 5, u0, roll(t0, 5, 0)),
                jnp.where(sub < 3, roll(t3, 3, 0), u3),
            )
        given = {(n, b): lat[n, k, pl.ds(8 * b, 8), :] for n in range(2) for b in OUTER}
        terms = momentum_level(
            ocean, levels, coriolis, k, packed, lev_halo, west_flux, cum, cum_halo, OUTER, given
        )
        for side, b in enumerate(OUTER):
            for n in range(2):
                accel[n, k, side] = terms[b][n]
            for n in range(4):
                sums[n, pl.ds(8 * b, 8), :] += terms[b][n]
        return carry

    over_levels(level)
    flat = [sums.at[0], sums.at[1], surface.at[0], surface.at[1], surface.at[2], levels]
    for n, field in enumerate(flat):
        send(2 * LEVELS + n, field[first, :].astype(F32), field[last_rows, :].astype(F32))


def inner_kernel(
    ocean, levels, coriolis, own, swap_0, swap_1, lat, outer_accel, outer_sums,
    accel, sums, west_flux, packed, cum, cum_halo, lev_halo,
):
    west_faces(
        own, (swap_0, swap_1), levels, (2, 3), (0, 1, 2, 3), packed, lev_halo, west_flux, INNER
    )
    cum[...] = jnp.zeros_like(cum)
    cum_halo[...] = jnp.zeros_like(cum_halo)
    sums[...] = outer_sums[...]

    def level(k, carry):
        given = {(n, b): lat[n, k, pl.ds(8 * b, 8), :] for n in range(2) for b in INNER}
        terms = momentum_level(
            ocean, levels, coriolis, k, packed, lev_halo, west_flux, cum, cum_halo, INNER, given
        )
        for b in INNER:
            rows = pl.ds(8 * b, 8)
            for n in range(4):
                if n < 2:
                    accel[n, k, rows, :] = terms[b][n]
                sums[n, rows, :] += terms[b][n]
        for n in range(2):
            for side, b in enumerate(OUTER):
                accel[n, k, pl.ds(8 * b, 8), :] = outer_accel[n, k, side]
        return carry

    over_levels(level)


def tracer_kernel(q, ocean, levels, own, swap_0, swap_1, *rest):
    early = EARLY.index(q) if q in EARLY else None
    lat_part = rest[0]
    tracer, west_flux, packed, lev_halo = rest[-4:]
    blocks = range(BLOCKS)
    west_faces(own, (swap_0, swap_1), levels, (q,), (q, 2), packed, lev_halo, west_flux, blocks)

    def level(k, carry):
        halo_of = halo_reader(packed, k)
        lon = lon_terms(ocean, levels, k, halo_of, lev_halo, (q,), west_flux, blocks)
        if early is None:
            lat = lat_terms(ocean, levels, k, (q,), blocks)
        else:
            lat = {(0, b): lat_part[early, k, pl.ds(8 * b, 8), :] for b in blocks}
        for b in blocks:
            rows = pl.ds(8 * b, 8)
            wet = wet_of(levels[rows, :].astype(F32), k)
            tracer[k, rows, :] = wet * (ocean[q, k, rows, :] - TRACER_STEP * (lon[0, b] + lat[0, b]))
        return carry

    over_levels(level)


def window(low_block, high_block, d):
    if d == 8:
        return high_block
    return roll(jnp.where(row_index() >= d, low_block, high_block), -d, 0)


def edge_blocks(ocean, arrived, q, k, side):
    own = ocean[q, k, pl.ds(0 if side == 0 else ROWS - 8, 8), :]
    piece = arrived[(q % 2) * LEVELS + k]
    if side == 0:
        return (roll(piece, 5, 0) if q < 2 else piece), own
    return own, (roll(piece, 3, 0) if q < 2 else piece)


def edge_levels(levels, arrived, side):
    own = levels[pl.ds(0 if side == 0 else ROWS - 8, 8), :].astype(F32)
    return (arrived[PIECES - 1], own) if side == 0 else (own, arrived[PIECES - 1])


def edge_terms(ocean, k, arrived, side, lev5, lev6, quantities):
    sub = row_index()
    v = edge_blocks(ocean, arrived, 3, k, side)
    speed = 0.5 * (window(*v, 5) + window(*v, 6)) * wet_of(jnp.minimum(lev5, lev6), k)
    terms = []
    for q in quantities:
        x = v if q == 3 else edge_blocks(ocean, arrived, q, k, side)
        flux = upwind_flux(speed, *[window(*x, d) for d in (3, 4, 5, 6, 7, 8)])
        flux = jnp.where(sub < 5, flux, 0.0)
        terms.append(flux - jnp.where(sub == 0, 0.0, roll(flux, 1, 0)))
    return terms


def own_rows(term, side):
    sub = row_index()
    if side == 0:
        return jnp.where(sub < 3, roll(term, -3, 0), 0.0)
    return jnp.where(sub >= 5, roll(term, 5, 0), 0.0)


def halo_rows(term, side):
    sub = row_index()
    if side == 0:
        return jnp.where(sub >= 5, roll(term, 5, 0), 0.0)
    return jnp.where(sub < 3, roll(term, -3, 0), 0.0)


def place_arrivals(up, down, south, north):
    even_lat = even_tile("lat")
    at_south = lax.axis_index("lat") == 0
    at_fold = lax.axis_index("lat") == lax.axis_size("lat") - 1
    turned_row, turned_lane = 7 - row_index(), COLS - 1 - lane_index()
    pair_sign = jnp.where(row_index() < 5, -1.0, 1.0)

    def piece(n, sign):
        south[n] = jnp.where(at_south, 0.0, jnp.where(even_lat, down[n], up[n]))
        here = jnp.where(even_lat, up[n], down[n])
        turned = jnp.take_along_axis(jnp.take_along_axis(here, turned_lane, axis=1), turned_row, axis=0)
        north[n] = jnp.where(at_fold, turned * sign, here)

    def pairs(first, carry):
        for n in range(8):
            piece(8 * first + n, pair_sign)
        return carry

    lax.fori_loop(0, 2 * LEVELS // 8, pairs, 0)
    for n, sign in enumerate((-1.0, -1.0, 1.0, -1.0, -1.0, 1.0)):
        piece(2 * LEVELS + n, sign)


def edge_kernel(
    ocean, levels, surface, sums, up, down, after,
    edges, fields, packed, means, south, north, cum, total,
):
    del after
    place_arrivals(up, down, south, north)
    sub = row_index()
    cum[...] = jnp.zeros_like(cum)
    total[...] = jnp.zeros_like(total)
    arrived = (south, north)

    def level(k, carry):
        for side in range(2):
            lev = edge_levels(levels, arrived[side], side)
            lev5, lev6 = window(*lev, 5), window(*lev, 6)
            terms = edge_terms(ocean, k, arrived[side], side, lev5, lev6, (2, 3))
            t = edge_blocks(ocean, arrived[side], 0, k, side)
            s = edge_blocks(ocean, arrived[side], 1, k, side)
            pressure = []
            for half in range(2):
                here = density(t[half], s[half], wet_of(lev[half], k))
                column = cum[side, half] + here
                cum[side, half] = column
                pressure.append(THICKNESS * (column - 0.5 * here))
            grad = 0.5 * (window(*pressure, 6) - window(*pressure, 4))
            grad = jnp.where((sub == 2) | (sub == 3), grad, 0.0)
            wet = wet_of(lev5, k)
            for n, term in enumerate((-wet * terms[0], -wet * (terms[1] + grad))):
                total[side, n] += term
                edges[side, n, k] = own_rows(term, side)
        return carry

    over_levels(level)
    rim = ROWS + 16
    own = pl.ds(8, ROWS)
    for n in range(3):
        fields[n, pl.ds(0, 8), :] = south[2 * LEVELS + 2 + n]
        fields[n, own, :] = surface[n]
        fields[n, pl.ds(rim - 8, 8), :] = north[2 * LEVELS + 2 + n]
    fields[3, pl.ds(0, 8), :] = south[PIECES - 1]
    fields[3, own, :] = levels[...].astype(F32)
    fields[3, pl.ds(rim - 8, 8), :] = north[PIECES - 1]
    for n in range(2):
        fields[4 + n, pl.ds(0, 8), :] = south[2 * LEVELS + n] + halo_rows(total[0, n], 0)
        fields[4 + n, own, :] = sums[n]
        fields[4 + n, pl.ds(8, 8), :] += own_rows(total[0, n], 0)
        fields[4 + n, pl.ds(ROWS, 8), :] += own_rows(total[1, n], 1)
        fields[4 + n, pl.ds(rim - 8, 8), :] = north[2 * LEVELS + n] + halo_rows(total[1, n], 1)
    for n in range(2):
        safe = jnp.maximum(THICKNESS * levels[...].astype(F32), THICKNESS)
        means[n] = THICKNESS * (sums[2 + n] + TRACER_STEP * fields[4 + n, own, :]) / safe
    for b in range(rim // 8):
        rows = pl.ds(8 * b, 8)
        safe = jnp.maximum(THICKNESS * fields[3, rows, :], THICKNESS)
        group = lane_index() // 16
        out = jnp.zeros((8, COLS), F32)
        for n in range(6):
            if n >= 4:
                fields[n, rows, :] = THICKNESS * fields[n, rows, :] / safe
            out = jnp.where(group == n, roll(fields[n, rows, :], 16 * n + 8, 1), out)
        packed[rows, :] = out


def tracer_edge_kernel(ocean, levels, south, north, edges):
    arrived = (south, north)

    def level(k, carry):
        for side in range(2):
            lev = edge_levels(levels, arrived[side], side)
            lev5, lev6 = window(*lev, 5), window(*lev, 6)
            wet = wet_of(lev5, k)
            terms = edge_terms(ocean, k, arrived[side], side, lev5, lev6, (0, 1))
            for n in range(2):
                edges[side, n, k] = own_rows(-wet * terms[n], side)
        return carry

    over_levels(level)


def final_kernel(
    ocean, levels, accel, temperature, salinity, edges, tracer_edges, fields, means, swap_0, swap_1,
    ocean_out, surface_out, shift,
):
    rim = ROWS + 16
    lane = lane_index(rim)
    even = even_tile("lon")
    low = jnp.where(even, swap_1[...], swap_0[...])
    high = jnp.where(even, swap_0[...], swap_1[...])
    halos = jnp.where(lane % 16 < 8, low, high)
    both = []
    for n in range(6):
        both.append((fields[n], roll(halos, -(16 * n + 8), 1)))
    height, mean_u, mean_v, level_map, force_lon, force_lat = both
    depth = tuple(THICKNESS * x for x in level_map)
    sea = tuple(jnp.where(x > 0.0, 1.0, 0.0) for x in level_map)

    def d_lon(x):
        main, halo = x
        result = []
        for here, other in ((main, halo), (halo, main)):
            ahead = roll(jnp.where(lane == 0, other, here), -1, 1)
            behind = roll(jnp.where(lane == COLS - 1, other, here), 1, 1)
            result.append(0.5 * (ahead - behind))
        return result

    def d_lat(x):
        return [0.5 * (roll(part, -1, 0) - roll(part, 1, 0)) for part in x]

    def times(x, y):
        return [p * q for p, q in zip(x, y)]

    for _ in range(NSUB):
        along, across = d_lon(times(depth, mean_u)), d_lat(times(depth, mean_v))
        height = [s * (h - SURFACE_STEP * (p + q)) for s, h, p, q in zip(sea, height, along, across)]
        mean_u = [
            s * (m + SURFACE_STEP * (f - d)) for s, m, f, d in zip(sea, mean_u, force_lon, d_lon(height))
        ]
        mean_v = [
            s * (m + SURFACE_STEP * (f - d)) for s, m, f, d in zip(sea, mean_v, force_lat, d_lat(height))
        ]
    for n, field in enumerate((height, mean_u, mean_v)):
        surface_out[n] = field[0][8 : 8 + ROWS]
    shift[0] = mean_u[0][8 : 8 + ROWS] - means[0]
    shift[1] = mean_v[0][8 : 8 + ROWS] - means[1]

    def level(k, carry):
        for b in range(BLOCKS):
            rows = pl.ds(8 * b, 8)
            wet = wet_of(levels[rows, :].astype(F32), k)
            for n in range(2):
                tracer, force = (temperature, salinity)[n][k, rows, :], accel[n, k, rows, :]
                if b in (0, BLOCKS - 1):
                    side = min(b, 1)
                    tracer = tracer + TRACER_STEP * tracer_edges[side, n, k]
                    force = force + edges[side, n, k]
                ocean_out[n, k, rows, :] = tracer
                ocean_out[2 + n, k, rows, :] = wet * (
                    ocean[2 + n, k, rows, :] + TRACER_STEP * force + shift[n, rows, :]
                )
        return carry

    over_levels(level)


def swapped(pairs):
    return list(pairs) + [(b, a) for a, b in pairs]


def swap_lon(x):
    count = lax.axis_size("lon")
    first = swapped([(i, i + 1) for i in range(0, count, 2)])
    second = swapped([(i, (i + 1) % count) for i in range(1, count, 2)])
    second = lax.ppermute(x, "lon", second)
    return lax.ppermute(x, "lon", first), second


def swap_lat(x, y):
    lon_count, lat_count = lax.axis_size("lon"), lax.axis_size("lat")
    first, second = [], []
    for p in range(lon_count):
        base = p * lat_count
        first += [(base + r, base + r + 1) for r in range(0, lat_count, 2)]
        second += [(base + r, base + r + 1) for r in range(1, lat_count - 1, 2)]
        if p < lon_count // 2:
            second.append((base + lat_count - 1, (lon_count - p) * lat_count - 1))
    y = lax.ppermute(y, ("lon", "lat"), swapped(second))
    x = lax.ppermute(x, ("lon", "lat"), swapped(first))
    return x, y


def call(kernel, outs, scratch=(), operands=1, unread=0, cost=1000000, limit=16):
    def vmem():
        return pl.BlockSpec(memory_space=pltpu.VMEM)

    specs = [vmem()] * operands
    specs += [pl.BlockSpec(memory_space=pl.ANY)] * unread
    single = len(outs) == 1
    shapes = [jax.ShapeDtypeStruct(shape, F32) for shape in outs]
    return pl.pallas_call(
        kernel,
        out_shape=shapes[0] if single else shapes,
        in_specs=specs,
        out_specs=vmem() if single else [vmem() for _ in outs],
        scratch_shapes=[pltpu.VMEM(shape, F32) for shape in scratch],
        cost_estimate=pl.CostEstimate(flops=cost, bytes_accessed=cost, transcendentals=0),
        compiler_params=pltpu.CompilerParams(vmem_limit_bytes=limit << 20),
    )


def on_device(ocean, surface, levels):
    tile = (ROWS, COLS)
    rim = (ROWS + 16, COLS)
    own = pl.pallas_call(
        pack_kernel,
        out_shape=jax.ShapeDtypeStruct((5, *tile), F32),
        in_specs=[pl.BlockSpec(memory_space=pl.ANY)] * 2,
        out_specs=pl.BlockSpec(memory_space=pltpu.VMEM),
        scratch_shapes=[
            pltpu.VMEM(ocean.shape, F32),
            pltpu.VMEM(tile, jnp.int32),
            pltpu.SemaphoreType.DMA((4,)),
            pltpu.SemaphoreType.DMA(()),
        ],
    )(ocean, levels)
    lon_0, lon_1 = swap_lon(own)
    lat_index, lat_count = lax.axis_index("lat"), lax.axis_size("lat")
    own = jnp.where(lat_index < 0, 0.0, own)
    row = lat_index * ROWS + lax.broadcasted_iota(jnp.int32, tile, 0)
    latitude = (row.astype(F32) + 0.5) / float(lat_count * ROWS)
    coriolis = jnp.sin(math.pi * latitude - 0.5 * math.pi)
    momentum_scratch = [(2, *tile), (4, *tile), tile, tile, tile]
    half = (2, LEVELS, 2, 8, COLS)
    arrivals = [(PIECES, 8, COLS)] * 2
    lat_part = call(early_kernel, [(len(EARLY), LEVELS, *tile)], operands=2, cost=100000000)(ocean, levels)
    outer_accel, lat_0, lat_1, outer_sums = call(
        outer_kernel,
        [half, *arrivals, (4, *tile)],
        scratch=momentum_scratch,
        operands=8,
    )(ocean, levels, surface, coriolis, own, lon_0, lon_1, lat_part)
    lat_0, lat_1 = swap_lat(lat_0, lat_1)
    accel, sums = call(
        inner_kernel,
        [(2, LEVELS, *tile), (4, *tile)],
        scratch=momentum_scratch,
        operands=9,
        cost=100000000,
    )(ocean, levels, coriolis, own, lon_0, lon_1, lat_part, outer_accel, outer_sums)

    def tracer(q, after):
        return call(
            functools.partial(tracer_kernel, q),
            [(LEVELS, *tile)],
            scratch=[(1, *tile), (3, *tile), tile],
            operands=5 + (q in EARLY),
            unread=1,
            cost=100000000,
        )(ocean, levels, own, lon_0, lon_1, *([lat_part] if q in EARLY else []), after)

    temperature = tracer(0, sums)
    edges, fields, packed, means, south, north = call(
        edge_kernel,
        [(2, 2, LEVELS, 8, COLS), (6, *rim), rim, (2, *tile), *arrivals],
        scratch=[(2, 2, 8, COLS), (2, 2, 8, COLS)],
        operands=6,
        unread=1,
    )(ocean, levels, surface, sums, lat_0, lat_1, temperature)
    rim_0, rim_1 = swap_lon(packed)
    tracer_edges = call(
        tracer_edge_kernel, [(2, 2, LEVELS, 8, COLS)], operands=4, cost=100000000
    )(ocean, levels, south, north)
    salinity = tracer(1, means)
    return call(final_kernel, [(4, LEVELS, *tile), (3, *tile)], scratch=[(2, *tile)], operands=11)(
        ocean, levels, accel, temperature, salinity, edges, tracer_edges, fields, means, rim_0, rim_1
    )


def solution(mesh):
    return jax.shard_map(
        on_device,
        mesh=mesh,
        in_specs=(P(None, None, "lat", "lon"), P(None, "lat", "lon"), P("lat", "lon")),
        out_specs=(P(None, None, "lat", "lon"), P(None, "lat", "lon")),
        check_vma=False,
    )
```

```python
import functools
import math

import jax
import jax.numpy as jnp
from jax import lax
from jax.experimental import pallas as pl
from jax.experimental.pallas import tpu as pltpu
from jax.sharding import PartitionSpec as P


NSUB = 4
LEVELS = 16
ROWS = 32
COLS = 128
PER_STEP = 4
BLOCKS = ROWS // 8
THICKNESS = 1.0 / LEVELS
TRACER_STEP = 0.1
SURFACE_STEP = 1.2
SPARE = LEVELS
PRESSURE = SPARE + LEVELS // 4
FLAT = PRESSURE + LEVELS // 8
PIECES = FLAT + 6
PLACED = 2 * LEVELS + 6

F32 = jnp.float32


def over_levels(level):
    def step(i, carry):
        for j in range(PER_STEP):
            level(PER_STEP * i + j, carry)
        return carry

    lax.fori_loop(0, LEVELS // PER_STEP, step, 0)


def even_tile(axis):
    return lax.rem(lax.axis_index(axis), 2) == 0


def lane_index(rows=8):
    return lax.broadcasted_iota(jnp.int32, (rows, COLS), 1)


def row_index(rows=8):
    return lax.broadcasted_iota(jnp.int32, (rows, COLS), 0)


def roll(x, shift, axis):
    if isinstance(shift, int):
        shift %= x.shape[axis]
        if shift == 0:
            return x
    return pltpu.roll(x, shift, axis)


def upwind_flux(speed, qm2, qm1, q0, q1, q2, q3):
    ahead = speed >= 0.0
    a = jnp.where(ahead, qm2, q3)
    b = jnp.where(ahead, qm1, q2)
    c = jnp.where(ahead, q0, q1)
    d = jnp.where(ahead, q1, q0)
    e = jnp.where(ahead, q2, qm1)
    ab = a - b
    bc = b - c
    cd = c - d
    de = d - e
    x1 = ab - bc
    y1 = ab - 3.0 * bc
    x2 = bc - cd
    y2 = bc + cd
    x3 = cd - de
    y3 = 3.0 * cd - de
    third = 13.0 / 3.0
    s1 = third * (x1 * x1) + (y1 * y1 + 4e-6)
    s2 = third * (x2 * x2) + (y2 * y2 + 4e-6)
    s3 = third * (x3 * x3) + (y3 * y3 + 4e-6)
    r1 = s2 * s3
    r2 = s1 * s3
    r3 = s1 * s2
    w1 = r1 * r1
    w2 = 6.0 * (r2 * r2)
    w3 = 3.0 * (r3 * r3)
    top = w1 * (2.0 * ab - 5.0 * bc) - w2 * (bc + 2.0 * cd) + w3 * (de - 4.0 * cd)
    low = 6.0 * (w1 + w2 + w3)
    return speed * (c + top / low)


def density(t, s, wet):
    return wet * (t * (0.03 * s - 0.2 - 0.05 * t) + 0.8 * s)


def wet_of(level_map, k):
    return jnp.where(level_map > k, 1.0, 0.0).astype(F32)


def pack_kernel(ocean_hbm, levels_hbm, out, ocean, levels, sems, level_sem):
    copies = [pltpu.make_async_copy(ocean_hbm.at[q], ocean.at[q], sems.at[q]) for q in range(4)]
    level_copy = pltpu.make_async_copy(levels_hbm, levels, level_sem)
    for copy in copies:
        copy.start()
    level_copy.start()
    group = lane_index() // 8
    for q in range(4):
        copies[q].wait()
        for b in range(BLOCKS):
            rows = pl.ds(8 * b, 8)
            packed = jnp.zeros((8, COLS), F32)
            for k in range(LEVELS):
                packed = jnp.where(group == k, roll(ocean[q, k, rows, :], 8 * k + 4, 1), packed)
            out[q, rows, :] = packed
    level_copy.wait()
    for b in range(BLOCKS):
        rows = pl.ds(8 * b, 8)
        out[4, rows, :] = roll(levels[rows, :].astype(F32), 4, 1)


def low_piece(q, rows, even, swaps):
    return jnp.where(even, swaps[1][q, rows, :], swaps[0][q, rows, :])


def halo_pack(q, rows, even, swaps):
    from_low = lane_index() % 8 < 4
    high = jnp.where(even, swaps[0][q, rows, :], swaps[1][q, rows, :])
    return jnp.where(from_low, low_piece(q, rows, even, swaps), high)


def next_lon(main, halo, step):
    lane = lane_index()
    if step > 0:
        return roll(jnp.where(lane < step, halo, main), -step, 1)
    return roll(jnp.where(lane >= COLS + step, halo, main), -step, 1)


def lon_shifts(main, halo):
    return [main if d == 0 else next_lon(main, halo, d) for d in (-2, -1, 0, 1, 2, 3)]


def west_faces(own, swaps, levels, quantities, halo_quantities, packed, lev_halo, west_flux, blocks):
    lane = lane_index()
    from_low = lane % 8 < 4
    level_of = lane // 8
    even = even_tile("lon")
    for b in blocks:
        rows = pl.ds(8 * b, 8)
        lev = levels[rows, :].astype(F32)
        own_col = lev[:, 0:1]
        west_col = low_piece(4, rows, even, swaps)[:, 3:4]
        both = jnp.minimum(own_col, west_col)
        wet = jnp.where(both > level_of.astype(F32), 1.0, 0.0)
        u = jnp.where(from_low, low_piece(2, rows, even, swaps), own[2, rows, :])
        speed = 0.5 * (u + roll(u, -1, 1)) * wet
        for n, q in enumerate(quantities):
            x = jnp.where(from_low, low_piece(q, rows, even, swaps), own[q, rows, :])
            west_flux[n, rows, :] = upwind_flux(speed, *[roll(x, -d, 1) for d in (-2, -1, 0, 1, 2, 3)])
        for q in halo_quantities:
            packed[q, rows, :] = halo_pack(q, rows, even, swaps)
        lev_halo[rows, :] = roll(halo_pack(4, rows, even, swaps), -4, 1)


def lat_shift(ocean, q, k, b, d):
    start = 8 * b + d
    if 0 <= start and start + 8 <= ROWS:
        return ocean[q, k, start : start + 8, :]
    return roll(ocean[q, k, pl.ds(8 * b, 8), :], -d, 0)


def level_map_shift(levels, b, d):
    start = 8 * b + d
    if 0 <= start and start + 8 <= ROWS:
        return levels[start : start + 8, :].astype(F32)
    return roll(levels[pl.ds(8 * b, 8), :].astype(F32), -d, 0)


def lat_terms(ocean, levels, k, quantities, blocks):
    sub = row_index()
    result, last = {}, {}
    for b in blocks:
        rows = pl.ds(8 * b, 8)
        wet = wet_of(levels[rows, :].astype(F32), k)
        wet_north = wet_of(level_map_shift(levels, b, 1), k)
        speed = 0.5 * (ocean[3, k, rows, :] + lat_shift(ocean, 3, k, b, 1)) * (wet * wet_north)
        for n, q in enumerate(quantities):
            north = upwind_flux(speed, *[lat_shift(ocean, q, k, b, d) for d in (-2, -1, 0, 1, 2, 3)])
            if b == 0:
                north = jnp.where(sub >= 2, north, 0.0)
            if b == BLOCKS - 1:
                north = jnp.where(sub <= 4, north, 0.0)
            last[n, b] = roll(north, 1, 0)
            south = jnp.where(sub == 0, last.get((n, b - 1), 0.0), last[n, b])
            result[n, b] = north - south
    return result


def lon_terms(ocean, levels, k, halo_of, lev_halo, quantities, west_flux, blocks):
    lane = lane_index()
    unplace = 124 - 8 * k
    result = {}
    for b in blocks:
        rows = pl.ds(8 * b, 8)
        lev = levels[rows, :].astype(F32)
        wet = wet_of(lev, k)
        u = ocean[2, k, rows, :]
        wet_east = wet_of(next_lon(lev, lev_halo[rows, :], 1), k)
        speed = 0.5 * (u + next_lon(u, halo_of(2, rows), 1)) * (wet * wet_east)
        for n, q in enumerate(quantities):
            main = ocean[q, k, rows, :]
            east = upwind_flux(speed, *lon_shifts(main, halo_of(q, rows)))
            west = pltpu.roll(west_flux[n, rows, :], unplace, 1)
            west = roll(jnp.where(lane == COLS - 1, west, east), 1, 1)
            result[n, b] = east - west
    return result


def halo_reader(packed, k):
    halo = {}

    def halo_of(q, rows):
        key = (q, rows.start)
        if key not in halo:
            halo[key] = pltpu.roll(packed[q, rows, :], 124 - 8 * k, 1)
        return halo[key]

    return halo_of


def momentum_level(ocean, levels, coriolis, k, packed, lev_halo, west_flux, cum, cum_halo, blocks, lat):
    sub = row_index()
    halo_of = halo_reader(packed, k)
    lon = lon_terms(ocean, levels, k, halo_of, lev_halo, (2, 3), west_flux, blocks)
    pressure, pressure_halo = [], {}
    for b in range(BLOCKS):
        rows = pl.ds(8 * b, 8)
        here = density(ocean[0, k, rows, :], ocean[1, k, rows, :], wet_of(levels[rows, :].astype(F32), k))
        total = cum[rows, :] + here
        cum[rows, :] = total
        pressure.append(THICKNESS * (total - 0.5 * here))
    for b in blocks:
        rows = pl.ds(8 * b, 8)
        here = density(halo_of(0, rows), halo_of(1, rows), wet_of(lev_halo[rows, :], k))
        total = cum_halo[rows, :] + here
        cum_halo[rows, :] = total
        pressure_halo[b] = THICKNESS * (total - 0.5 * here)
    result = {}
    for b in blocks:
        rows = pl.ds(8 * b, 8)
        wet = wet_of(levels[rows, :].astype(F32), k)
        grad_lon = 0.5 * (
            next_lon(pressure[b], pressure_halo[b], 1) - next_lon(pressure[b], pressure_halo[b], -1)
        )
        ahead = pressure[b] if b == BLOCKS - 1 else jnp.where(sub == 0, pressure[b + 1], pressure[b])
        behind = pressure[b] if b == 0 else jnp.where(sub == 7, pressure[b - 1], pressure[b])
        ahead, behind = roll(ahead, -1, 0), roll(behind, 1, 0)
        if b == 0:
            behind = jnp.where(sub >= 1, behind, 0.0)
        if b == BLOCKS - 1:
            ahead = jnp.where(sub <= 6, ahead, 0.0)
        grad_lat = 0.5 * (ahead - behind)
        u, v, turn = ocean[2, k, rows, :], ocean[3, k, rows, :], coriolis[rows, :]
        accel_u = wet * (turn * v - grad_lon - (lon[0, b] + lat[0, b]))
        accel_v = wet * (-turn * u - grad_lat - (lon[1, b] + lat[1, b]))
        result[b] = (accel_u, accel_v, wet * u, wet * v, pressure[b])
    return result


EARLY = (2, 3, 0)
OUTER = (0, BLOCKS - 1)
INNER = tuple(range(1, BLOCKS - 1))


def early_kernel(ocean, levels, lat):
    def level(k, carry):
        terms = lat_terms(ocean, levels, k, EARLY, range(BLOCKS))
        for n in range(len(EARLY)):
            for b in range(BLOCKS):
                lat[n, k, pl.ds(8 * b, 8), :] = terms[n, b]
        return carry

    over_levels(level)


def outer_kernel(
    ocean, levels, surface, coriolis, own, swap_0, swap_1, lat,
    accel, even_out, odd_out, sums, own_pressure, west_flux, packed, cum, cum_halo, lev_halo, pressure,
):
    sub = row_index()
    even_lat = even_tile("lat")
    west_faces(
        own, (swap_0, swap_1), levels, (2, 3), (0, 1, 2, 3), packed, lev_halo, west_flux, OUTER
    )
    cum[...] = jnp.zeros_like(cum)
    cum_halo[...] = jnp.zeros_like(cum_halo)
    sums[...] = jnp.zeros_like(sums)

    def send(index, south, north):
        even_out[index] = jnp.where(even_lat, north, south)
        odd_out[index] = jnp.where(even_lat, south, north)

    first, last_rows = pl.ds(0, 8), pl.ds(ROWS - 8, 8)

    def level(k, carry):
        u0, u3 = ocean[2, k, first, :], ocean[2, k, last_rows, :]
        v0, v3 = ocean[3, k, first, :], ocean[3, k, last_rows, :]
        send(k, jnp.where(sub < 5, u0, roll(v0, 5, 0)), jnp.where(sub < 3, roll(v3, 3, 0), u3))
        given = {(n, b): lat[n, k, pl.ds(8 * b, 8), :] for n in range(2) for b in OUTER}
        terms = momentum_level(
            ocean, levels, coriolis, k, packed, lev_halo, west_flux, cum, cum_halo, OUTER, given
        )
        for side, b in enumerate(OUTER):
            pressure[side, k] = terms[b][4]
            for n in range(2):
                accel[n, k, side] = terms[b][n]
            for n in range(4):
                sums[n, pl.ds(8 * b, 8), :] += terms[b][n]
        return carry

    over_levels(level)
    for m in range(LEVELS // 4):
        south = north = jnp.zeros((8, COLS), F32)
        for j in range(4):
            k = 4 * m + j
            south = jnp.where(sub // 2 == j, roll(ocean[3, k, first, :], 2 * j - 3, 0), south)
            north = jnp.where(sub // 2 == 3 - j, roll(ocean[3, k, last_rows, :], 3 - 2 * j, 0), north)
        send(SPARE + m, south, north)
    for m in range(LEVELS // 8):
        south = north = jnp.zeros((8, COLS), F32)
        for j in range(8):
            k = 8 * m + j
            south = jnp.where(sub == j, roll(pressure[0, k], j, 0), south)
            north = jnp.where(sub == 7 - j, roll(pressure[1, k], -j, 0), north)
        send(PRESSURE + m, south, north)
        own_pressure[0, m] = south
        own_pressure[1, m] = north
    flat = [sums.at[0], sums.at[1], surface.at[0], surface.at[1], surface.at[2], levels]
    for n, field in enumerate(flat):
        send(FLAT + n, field[first, :].astype(F32), field[last_rows, :].astype(F32))


def inner_kernel(
    ocean, levels, coriolis, own, swap_0, swap_1, lat, outer_accel, outer_sums,
    accel, sums, west_flux, packed, cum, cum_halo, lev_halo,
):
    west_faces(
        own, (swap_0, swap_1), levels, (2, 3), (0, 1, 2, 3), packed, lev_halo, west_flux, INNER
    )
    cum[...] = jnp.zeros_like(cum)
    cum_halo[...] = jnp.zeros_like(cum_halo)
    sums[...] = outer_sums[...]

    def level(k, carry):
        given = {(n, b): lat[n, k, pl.ds(8 * b, 8), :] for n in range(2) for b in INNER}
        terms = momentum_level(
            ocean, levels, coriolis, k, packed, lev_halo, west_flux, cum, cum_halo, INNER, given
        )
        for b in INNER:
            rows = pl.ds(8 * b, 8)
            for n in range(4):
                if n < 2:
                    accel[n, k, rows, :] = terms[b][n]
                sums[n, rows, :] += terms[b][n]
        for n in range(2):
            for side, b in enumerate(OUTER):
                accel[n, k, pl.ds(8 * b, 8), :] = outer_accel[n, k, side]
        return carry

    over_levels(level)


def tracer_rows(ocean, even_out, odd_out):
    sub = row_index()
    even_lat = even_tile("lat")
    first, last_rows = pl.ds(0, 8), pl.ds(ROWS - 8, 8)

    def level(k, carry):
        south = jnp.where(sub < 5, ocean[0, k, first, :], roll(ocean[1, k, first, :], 5, 0))
        north = jnp.where(sub < 3, roll(ocean[1, k, last_rows, :], 3, 0), ocean[0, k, last_rows, :])
        even_out[k] = jnp.where(even_lat, north, south)
        odd_out[k] = jnp.where(even_lat, south, north)
        return carry

    over_levels(level)


def tracer_kernel(q, ocean, levels, own, swap_0, swap_1, *rest):
    early = EARLY.index(q) if q in EARLY else None
    lat_part = rest[0]
    tracer, west_flux, packed, lev_halo = rest[-4:] if early is None else rest[-6:-5] + rest[-3:]
    if early is not None:
        tracer_rows(ocean, rest[-5], rest[-4])
    blocks = range(BLOCKS)
    west_faces(own, (swap_0, swap_1), levels, (q,), (q, 2), packed, lev_halo, west_flux, blocks)

    def level(k, carry):
        halo_of = halo_reader(packed, k)
        lon = lon_terms(ocean, levels, k, halo_of, lev_halo, (q,), west_flux, blocks)
        if early is None:
            lat = lat_terms(ocean, levels, k, (q,), blocks)
        else:
            lat = {(0, b): lat_part[early, k, pl.ds(8 * b, 8), :] for b in blocks}
        for b in blocks:
            rows = pl.ds(8 * b, 8)
            wet = wet_of(levels[rows, :].astype(F32), k)
            tracer[k, rows, :] = wet * (ocean[q, k, rows, :] - TRACER_STEP * (lon[0, b] + lat[0, b]))
        return carry

    over_levels(level)


def window(low_block, high_block, d):
    if d == 8:
        return high_block
    return roll(jnp.where(row_index() >= d, low_block, high_block), -d, 0)


def edge_blocks(ocean, arrived, q, k, side):
    own = ocean[q, k, pl.ds(0 if side == 0 else ROWS - 8, 8), :]
    piece = arrived[k + LEVELS if q == 3 else k]
    if q == 1:
        piece = roll(piece, 5 if side == 0 else 3, 0)
    return (piece, own) if side == 0 else (own, piece)


def edge_levels(levels, arrived, side):
    own = levels[pl.ds(0 if side == 0 else ROWS - 8, 8), :].astype(F32)
    return (arrived[PLACED - 1], own) if side == 0 else (own, arrived[PLACED - 1])


def edge_terms(ocean, k, arrived, side, lev5, lev6, quantities, rows_arrived=None):
    sub = row_index()
    v = edge_blocks(ocean, arrived, 3, k, side)
    arrived = arrived if rows_arrived is None else rows_arrived
    speed = 0.5 * (window(*v, 5) + window(*v, 6)) * wet_of(jnp.minimum(lev5, lev6), k)
    terms = []
    for q in quantities:
        x = v if q == 3 else edge_blocks(ocean, arrived, q, k, side)
        flux = upwind_flux(speed, *[window(*x, d) for d in (3, 4, 5, 6, 7, 8)])
        flux = jnp.where(sub < 5, flux, 0.0)
        terms.append(flux - jnp.where(sub == 0, 0.0, roll(flux, 1, 0)))
    return terms


def own_rows(term, side):
    sub = row_index()
    if side == 0:
        return jnp.where(sub < 3, roll(term, -3, 0), 0.0)
    return jnp.where(sub >= 5, roll(term, 5, 0), 0.0)


def halo_rows(term, side):
    sub = row_index()
    if side == 0:
        return jnp.where(sub >= 5, roll(term, 5, 0), 0.0)
    return jnp.where(sub < 3, roll(term, -3, 0), 0.0)


def sort_arrival(first, second, sign):
    even_lat = even_tile("lat")
    at_south = lax.axis_index("lat") == 0
    at_fold = lax.axis_index("lat") == lax.axis_size("lat") - 1
    turned_row, turned_lane = 7 - row_index(), COLS - 1 - lane_index()
    south = jnp.where(at_south, 0.0, jnp.where(even_lat, second, first))
    north = jnp.where(even_lat, first, second)
    turned = jnp.take_along_axis(jnp.take_along_axis(north, turned_lane, axis=1), turned_row, axis=0)
    return south, jnp.where(at_fold, turned * sign, north)


def place_arrivals(up, down, own_pressure, south, north, grads):
    sub = row_index()
    for m in range(LEVELS // 4):
        south_spare, north_spare = sort_arrival(up[SPARE + m], down[SPARE + m], -1.0)
        for j in range(4):
            k = 4 * m + j
            south[k], north[k] = from_south, from_north = sort_arrival(up[k], down[k], -1.0)
            south[LEVELS + k] = jnp.where(sub < 5, roll(south_spare, 2 * j - 3, 0), roll(from_south, 5, 0))
            north[LEVELS + k] = jnp.where(sub < 3, roll(from_north, 3, 0), roll(north_spare, 3 - 2 * j, 0))
    for m in range(LEVELS // 8):
        far_south, far_north = sort_arrival(up[PRESSURE + m], down[PRESSURE + m], 1.0)
        own_south, own_north = own_pressure[0, m], own_pressure[1, m]
        for j in range(8):
            k = 8 * m + j
            ahead, behind = roll(own_south, 2 - j, 0), roll(far_south, 3 - (7 - j), 0)
            grads[0, k] = 0.5 * jnp.where(sub == 2, ahead, jnp.where(sub == 3, -behind, 0.0))
            ahead, behind = roll(far_north, 2 - j, 0), roll(own_north, 3 - (7 - j), 0)
            grads[1, k] = 0.5 * jnp.where(sub == 2, ahead, jnp.where(sub == 3, -behind, 0.0))
    for n, sign in enumerate((-1.0, -1.0, 1.0, -1.0, -1.0, 1.0)):
        south[2 * LEVELS + n], north[2 * LEVELS + n] = sort_arrival(up[FLAT + n], down[FLAT + n], sign)


def edge_kernel(
    ocean, levels, surface, sums, own_pressure, up, down, after,
    edges, fields, packed, means, south, north, total, grads,
):
    del after
    place_arrivals(up, down, own_pressure, south, north, grads)
    total[...] = jnp.zeros_like(total)
    arrived = (south, north)

    def level(k, carry):
        for side in range(2):
            lev = edge_levels(levels, arrived[side], side)
            lev5, lev6 = window(*lev, 5), window(*lev, 6)
            terms = edge_terms(ocean, k, arrived[side], side, lev5, lev6, (2, 3))
            wet = wet_of(lev5, k)
            for n, term in enumerate((-wet * terms[0], -wet * (terms[1] + grads[side, k]))):
                total[side, n] += term
                edges[side, n, k] = own_rows(term, side)
        return carry

    over_levels(level)
    rim = ROWS + 16
    own = pl.ds(8, ROWS)
    for n in range(3):
        fields[n, pl.ds(0, 8), :] = south[2 * LEVELS + 2 + n]
        fields[n, own, :] = surface[n]
        fields[n, pl.ds(rim - 8, 8), :] = north[2 * LEVELS + 2 + n]
    fields[3, pl.ds(0, 8), :] = south[PLACED - 1]
    fields[3, own, :] = levels[...].astype(F32)
    fields[3, pl.ds(rim - 8, 8), :] = north[PLACED - 1]
    for n in range(2):
        fields[4 + n, pl.ds(0, 8), :] = south[2 * LEVELS + n] + halo_rows(total[0, n], 0)
        fields[4 + n, own, :] = sums[n]
        fields[4 + n, pl.ds(8, 8), :] += own_rows(total[0, n], 0)
        fields[4 + n, pl.ds(ROWS, 8), :] += own_rows(total[1, n], 1)
        fields[4 + n, pl.ds(rim - 8, 8), :] = north[2 * LEVELS + n] + halo_rows(total[1, n], 1)
    for n in range(2):
        safe = jnp.maximum(THICKNESS * levels[...].astype(F32), THICKNESS)
        means[n] = THICKNESS * (sums[2 + n] + TRACER_STEP * fields[4 + n, own, :]) / safe
    for b in range(rim // 8):
        rows = pl.ds(8 * b, 8)
        safe = jnp.maximum(THICKNESS * fields[3, rows, :], THICKNESS)
        group = lane_index() // 16
        out = jnp.zeros((8, COLS), F32)
        for n in range(6):
            if n >= 4:
                fields[n, rows, :] = THICKNESS * fields[n, rows, :] / safe
            out = jnp.where(group == n, roll(fields[n, rows, :], 16 * n + 8, 1), out)
        packed[rows, :] = out


def tracer_edge_kernel(ocean, levels, south, north, up, down, edges, rows_south, rows_north):
    arrived = (south, north)
    rows_arrived = (rows_south, rows_north)

    def place(k, carry):
        rows_south[k], rows_north[k] = sort_arrival(up[k], down[k], 1.0)
        return carry

    over_levels(place)

    def level(k, carry):
        for side in range(2):
            lev = edge_levels(levels, arrived[side], side)
            lev5, lev6 = window(*lev, 5), window(*lev, 6)
            wet = wet_of(lev5, k)
            terms = edge_terms(ocean, k, arrived[side], side, lev5, lev6, (0, 1), rows_arrived[side])
            for n in range(2):
                edges[side, n, k] = own_rows(-wet * terms[n], side)
        return carry

    over_levels(level)


def final_kernel(
    ocean, levels, accel, temperature, salinity, edges, tracer_edges, fields, means, swap_0, swap_1,
    ocean_out, surface_out, shift,
):
    rim = ROWS + 16
    lane = lane_index(rim)
    even = even_tile("lon")
    low = jnp.where(even, swap_1[...], swap_0[...])
    high = jnp.where(even, swap_0[...], swap_1[...])
    halos = jnp.where(lane % 16 < 8, low, high)
    both = []
    for n in range(6):
        both.append((fields[n], roll(halos, -(16 * n + 8), 1)))
    height, mean_u, mean_v, level_map, force_lon, force_lat = both
    depth = tuple(THICKNESS * x for x in level_map)
    sea = tuple(jnp.where(x > 0.0, 1.0, 0.0) for x in level_map)

    def d_lon(x):
        main, halo = x
        result = []
        for here, other in ((main, halo), (halo, main)):
            ahead = roll(jnp.where(lane == 0, other, here), -1, 1)
            behind = roll(jnp.where(lane == COLS - 1, other, here), 1, 1)
            result.append(0.5 * (ahead - behind))
        return result

    def d_lat(x):
        return [0.5 * (roll(part, -1, 0) - roll(part, 1, 0)) for part in x]

    def times(x, y):
        return [p * q for p, q in zip(x, y)]

    for _ in range(NSUB):
        along, across = d_lon(times(depth, mean_u)), d_lat(times(depth, mean_v))
        height = [s * (h - SURFACE_STEP * (p + q)) for s, h, p, q in zip(sea, height, along, across)]
        mean_u = [
            s * (m + SURFACE_STEP * (f - d)) for s, m, f, d in zip(sea, mean_u, force_lon, d_lon(height))
        ]
        mean_v = [
            s * (m + SURFACE_STEP * (f - d)) for s, m, f, d in zip(sea, mean_v, force_lat, d_lat(height))
        ]
    for n, field in enumerate((height, mean_u, mean_v)):
        surface_out[n] = field[0][8 : 8 + ROWS]
    shift[0] = mean_u[0][8 : 8 + ROWS] - means[0]
    shift[1] = mean_v[0][8 : 8 + ROWS] - means[1]

    def level(k, carry):
        for b in range(BLOCKS):
            rows = pl.ds(8 * b, 8)
            wet = wet_of(levels[rows, :].astype(F32), k)
            for n in range(2):
                tracer, force = (temperature, salinity)[n][k, rows, :], accel[n, k, rows, :]
                if b in (0, BLOCKS - 1):
                    side = min(b, 1)
                    tracer = tracer + TRACER_STEP * tracer_edges[side, n, k]
                    force = force + edges[side, n, k]
                ocean_out[n, k, rows, :] = tracer
                ocean_out[2 + n, k, rows, :] = wet * (
                    ocean[2 + n, k, rows, :] + TRACER_STEP * force + shift[n, rows, :]
                )
        return carry

    over_levels(level)


def swapped(pairs):
    return list(pairs) + [(b, a) for a, b in pairs]


def swap_lon(x):
    count = lax.axis_size("lon")
    first = swapped([(i, i + 1) for i in range(0, count, 2)])
    second = swapped([(i, (i + 1) % count) for i in range(1, count, 2)])
    second = lax.ppermute(x, "lon", second)
    return lax.ppermute(x, "lon", first), second


def swap_lat(x, y):
    lon_count, lat_count = lax.axis_size("lon"), lax.axis_size("lat")
    first, second = [], []
    for p in range(lon_count):
        base = p * lat_count
        first += [(base + r, base + r + 1) for r in range(0, lat_count, 2)]
        second += [(base + r, base + r + 1) for r in range(1, lat_count - 1, 2)]
        if p < lon_count // 2:
            second.append((base + lat_count - 1, (lon_count - p) * lat_count - 1))
    y = lax.ppermute(y, ("lon", "lat"), swapped(second))
    x = lax.ppermute(x, ("lon", "lat"), swapped(first))
    return x, y


def call(kernel, outs, scratch=(), operands=1, unread=0, cost=1000000, limit=16):
    def vmem():
        return pl.BlockSpec(memory_space=pltpu.VMEM)

    specs = [vmem()] * operands
    specs += [pl.BlockSpec(memory_space=pl.ANY)] * unread
    single = len(outs) == 1
    shapes = [jax.ShapeDtypeStruct(shape, F32) for shape in outs]
    return pl.pallas_call(
        kernel,
        out_shape=shapes[0] if single else shapes,
        in_specs=specs,
        out_specs=vmem() if single else [vmem() for _ in outs],
        scratch_shapes=[pltpu.VMEM(shape, F32) for shape in scratch],
        cost_estimate=pl.CostEstimate(flops=cost, bytes_accessed=cost, transcendentals=0),
        compiler_params=pltpu.CompilerParams(vmem_limit_bytes=limit << 20),
    )


def on_device(ocean, surface, levels):
    tile = (ROWS, COLS)
    rim = (ROWS + 16, COLS)
    own = pl.pallas_call(
        pack_kernel,
        out_shape=jax.ShapeDtypeStruct((5, *tile), F32),
        in_specs=[pl.BlockSpec(memory_space=pl.ANY)] * 2,
        out_specs=pl.BlockSpec(memory_space=pltpu.VMEM),
        scratch_shapes=[
            pltpu.VMEM(ocean.shape, F32),
            pltpu.VMEM(tile, jnp.int32),
            pltpu.SemaphoreType.DMA((4,)),
            pltpu.SemaphoreType.DMA(()),
        ],
    )(ocean, levels)
    lon_0, lon_1 = swap_lon(own)
    lat_index, lat_count = lax.axis_index("lat"), lax.axis_size("lat")
    own = jnp.where(lat_index < 0, 0.0, own)
    row = lat_index * ROWS + lax.broadcasted_iota(jnp.int32, tile, 0)
    latitude = (row.astype(F32) + 0.5) / float(lat_count * ROWS)
    coriolis = jnp.sin(math.pi * latitude - 0.5 * math.pi)
    momentum_scratch = [(2, *tile), (4, *tile), tile, tile, tile]
    half = (2, LEVELS, 2, 8, COLS)
    sent, placed, rows_sent = [(PIECES, 8, COLS)] * 2, [(PLACED, 8, COLS)] * 2, [(LEVELS, 8, COLS)] * 2
    lat_part = call(early_kernel, [(len(EARLY), LEVELS, *tile)], operands=2, cost=100000000)(ocean, levels)
    outer_accel, lat_0, lat_1, outer_sums, own_pressure = call(
        outer_kernel,
        [half, *sent, (4, *tile), (2, LEVELS // 8, 8, COLS)],
        scratch=[*momentum_scratch, (2, LEVELS, 8, COLS)],
        operands=8,
    )(ocean, levels, surface, coriolis, own, lon_0, lon_1, lat_part)
    lat_0, lat_1 = swap_lat(lat_0, lat_1)
    accel, sums = call(
        inner_kernel,
        [(2, LEVELS, *tile), (4, *tile)],
        scratch=momentum_scratch,
        operands=9,
        cost=100000000,
    )(ocean, levels, coriolis, own, lon_0, lon_1, lat_part, outer_accel, outer_sums)

    def tracer(q, after):
        return call(
            functools.partial(tracer_kernel, q),
            [(LEVELS, *tile)] + (rows_sent if q in EARLY else []),
            scratch=[(1, *tile), (3, *tile), tile],
            operands=5 + (q in EARLY),
            unread=1,
            cost=100000000,
        )(ocean, levels, own, lon_0, lon_1, *([lat_part] if q in EARLY else []), after)

    temperature, rows_0, rows_1 = tracer(0, sums)
    rows_0, rows_1 = swap_lat(rows_0, rows_1)
    edges, fields, packed, means, south, north = call(
        edge_kernel,
        [(2, 2, LEVELS, 8, COLS), (6, *rim), rim, (2, *tile), *placed],
        scratch=[(2, 2, 8, COLS), (2, LEVELS, 8, COLS)],
        operands=7,
        unread=1,
    )(ocean, levels, surface, sums, own_pressure, lat_0, lat_1, temperature)
    rim_0, rim_1 = swap_lon(packed)
    tracer_edges = call(
        tracer_edge_kernel, [(2, 2, LEVELS, 8, COLS)], scratch=rows_sent, operands=6, cost=100000000
    )(ocean, levels, south, north, rows_0, rows_1)
    salinity = tracer(1, means)
    return call(final_kernel, [(4, LEVELS, *tile), (3, *tile)], scratch=[(2, *tile)], operands=11)(
        ocean, levels, accel, temperature, salinity, edges, tracer_edges, fields, means, rim_0, rim_1
    )


def solution(mesh):
    return jax.shard_map(
        on_device,
        mesh=mesh,
        in_specs=(P(None, None, "lat", "lon"), P(None, "lat", "lon"), P("lat", "lon")),
        out_specs=(P(None, None, "lat", "lon"), P(None, "lat", "lon")),
        check_vma=False,
    )
```

```python
import functools
import math

import jax
import jax.numpy as jnp
from jax import lax
from jax.experimental import pallas as pl
from jax.experimental.pallas import tpu as pltpu
from jax.sharding import PartitionSpec as P


NSUB = 4
LEVELS = 16
ROWS = 32
COLS = 128
PER_STEP = 4
BLOCKS = ROWS // 8
THICKNESS = 1.0 / LEVELS
TRACER_STEP = 0.1
SURFACE_STEP = 1.2
PIECES = 2 * LEVELS + 6

F32 = jnp.float32


def over_levels(level):
    def step(i, carry):
        for j in range(PER_STEP):
            level(PER_STEP * i + j, carry)
        return carry

    lax.fori_loop(0, LEVELS // PER_STEP, step, 0)


def even_tile(axis):
    return lax.rem(lax.axis_index(axis), 2) == 0


def lane_index(rows=8):
    return lax.broadcasted_iota(jnp.int32, (rows, COLS), 1)


def row_index(rows=8):
    return lax.broadcasted_iota(jnp.int32, (rows, COLS), 0)


def roll(x, shift, axis):
    if isinstance(shift, int):
        shift %= x.shape[axis]
        if shift == 0:
            return x
    return pltpu.roll(x, shift, axis)


def upwind_flux(speed, qm2, qm1, q0, q1, q2, q3):
    ahead = speed >= 0.0
    a = jnp.where(ahead, qm2, q3)
    b = jnp.where(ahead, qm1, q2)
    c = jnp.where(ahead, q0, q1)
    d = jnp.where(ahead, q1, q0)
    e = jnp.where(ahead, q2, qm1)
    ab = a - b
    bc = b - c
    cd = c - d
    de = d - e
    x1 = ab - bc
    y1 = ab - 3.0 * bc
    x2 = bc - cd
    y2 = bc + cd
    x3 = cd - de
    y3 = 3.0 * cd - de
    third = 13.0 / 3.0
    s1 = third * (x1 * x1) + (y1 * y1 + 4e-6)
    s2 = third * (x2 * x2) + (y2 * y2 + 4e-6)
    s3 = third * (x3 * x3) + (y3 * y3 + 4e-6)
    r1 = s2 * s3
    r2 = s1 * s3
    r3 = s1 * s2
    w1 = r1 * r1
    w2 = 6.0 * (r2 * r2)
    w3 = 3.0 * (r3 * r3)
    top = w1 * (2.0 * ab - 5.0 * bc) - w2 * (bc + 2.0 * cd) + w3 * (de - 4.0 * cd)
    low = 6.0 * (w1 + w2 + w3)
    return speed * (c + top / low)


def density(t, s, wet):
    return wet * (t * (0.03 * s - 0.2 - 0.05 * t) + 0.8 * s)


def wet_of(level_map, k):
    return jnp.where(level_map > k, 1.0, 0.0).astype(F32)


def pack_kernel(ocean_hbm, levels_hbm, out, ocean, levels, sems, level_sem):
    copies = [pltpu.make_async_copy(ocean_hbm.at[q], ocean.at[q], sems.at[q]) for q in range(4)]
    level_copy = pltpu.make_async_copy(levels_hbm, levels, level_sem)
    for copy in copies:
        copy.start()
    level_copy.start()
    group = lane_index() // 8
    for q in range(4):
        copies[q].wait()
        for b in range(BLOCKS):
            rows = pl.ds(8 * b, 8)
            packed = jnp.zeros((8, COLS), F32)
            for k in range(LEVELS):
                packed = jnp.where(group == k, roll(ocean[q, k, rows, :], 8 * k + 4, 1), packed)
            out[q, rows, :] = packed
    level_copy.wait()
    for b in range(BLOCKS):
        rows = pl.ds(8 * b, 8)
        out[4, rows, :] = roll(levels[rows, :].astype(F32), 4, 1)


def low_piece(q, rows, even, swaps):
    return jnp.where(even, swaps[1][q, rows, :], swaps[0][q, rows, :])


def halo_pack(q, rows, even, swaps):
    from_low = lane_index() % 8 < 4
    high = jnp.where(even, swaps[0][q, rows, :], swaps[1][q, rows, :])
    return jnp.where(from_low, low_piece(q, rows, even, swaps), high)


def next_lon(main, halo, step):
    lane = lane_index()
    if step > 0:
        return roll(jnp.where(lane < step, halo, main), -step, 1)
    return roll(jnp.where(lane >= COLS + step, halo, main), -step, 1)


def lon_shifts(main, halo):
    return [main if d == 0 else next_lon(main, halo, d) for d in (-2, -1, 0, 1, 2, 3)]


def west_faces(own, swaps, levels, quantities, halo_quantities, packed, lev_halo, west_flux, blocks):
    lane = lane_index()
    from_low = lane % 8 < 4
    level_of = lane // 8
    even = even_tile("lon")
    for b in blocks:
        rows = pl.ds(8 * b, 8)
        lev = levels[rows, :].astype(F32)
        own_col = lev[:, 0:1]
        west_col = low_piece(4, rows, even, swaps)[:, 3:4]
        both = jnp.minimum(own_col, west_col)
        wet = jnp.where(both > level_of.astype(F32), 1.0, 0.0)
        u = jnp.where(from_low, low_piece(2, rows, even, swaps), own[2, rows, :])
        speed = 0.5 * (u + roll(u, -1, 1)) * wet
        for n, q in enumerate(quantities):
            x = jnp.where(from_low, low_piece(q, rows, even, swaps), own[q, rows, :])
            west_flux[n, rows, :] = upwind_flux(speed, *[roll(x, -d, 1) for d in (-2, -1, 0, 1, 2, 3)])
        for q in halo_quantities:
            packed[q, rows, :] = halo_pack(q, rows, even, swaps)
        lev_halo[rows, :] = roll(halo_pack(4, rows, even, swaps), -4, 1)


def lat_shift(ocean, q, k, b, d):
    start = 8 * b + d
    if 0 <= start and start + 8 <= ROWS:
        return ocean[q, k, start : start + 8, :]
    return roll(ocean[q, k, pl.ds(8 * b, 8), :], -d, 0)


def level_map_shift(levels, b, d):
    start = 8 * b + d
    if 0 <= start and start + 8 <= ROWS:
        return levels[start : start + 8, :].astype(F32)
    return roll(levels[pl.ds(8 * b, 8), :].astype(F32), -d, 0)


def lat_terms(ocean, levels, k, quantities, blocks):
    sub = row_index()
    result, last = {}, {}
    for b in blocks:
        rows = pl.ds(8 * b, 8)
        wet = wet_of(levels[rows, :].astype(F32), k)
        wet_north = wet_of(level_map_shift(levels, b, 1), k)
        speed = 0.5 * (ocean[3, k, rows, :] + lat_shift(ocean, 3, k, b, 1)) * (wet * wet_north)
        for n, q in enumerate(quantities):
            north = upwind_flux(speed, *[lat_shift(ocean, q, k, b, d) for d in (-2, -1, 0, 1, 2, 3)])
            if b == 0:
                north = jnp.where(sub >= 2, north, 0.0)
            if b == BLOCKS - 1:
                north = jnp.where(sub <= 4, north, 0.0)
            last[n, b] = roll(north, 1, 0)
            south = jnp.where(sub == 0, last.get((n, b - 1), 0.0), last[n, b])
            result[n, b] = north - south
    return result


def lon_terms(ocean, levels, k, halo_of, lev_halo, quantities, west_flux, blocks):
    lane = lane_index()
    unplace = 124 - 8 * k
    result = {}
    for b in blocks:
        rows = pl.ds(8 * b, 8)
        lev = levels[rows, :].astype(F32)
        wet = wet_of(lev, k)
        u = ocean[2, k, rows, :]
        wet_east = wet_of(next_lon(lev, lev_halo[rows, :], 1), k)
        speed = 0.5 * (u + next_lon(u, halo_of(2, rows), 1)) * (wet * wet_east)
        for n, q in enumerate(quantities):
            main = ocean[q, k, rows, :]
            east = upwind_flux(speed, *lon_shifts(main, halo_of(q, rows)))
            west = pltpu.roll(west_flux[n, rows, :], unplace, 1)
            west = roll(jnp.where(lane == COLS - 1, west, east), 1, 1)
            result[n, b] = east - west
    return result


def halo_reader(packed, k):
    halo = {}

    def halo_of(q, rows):
        key = (q, rows.start)
        if key not in halo:
            halo[key] = pltpu.roll(packed[q, rows, :], 124 - 8 * k, 1)
        return halo[key]

    return halo_of


def momentum_level(ocean, levels, coriolis, k, packed, lev_halo, west_flux, cum, cum_halo, blocks, lat):
    sub = row_index()
    halo_of = halo_reader(packed, k)
    lon = lon_terms(ocean, levels, k, halo_of, lev_halo, (2, 3), west_flux, blocks)
    pressure, pressure_halo = [], {}
    for b in range(BLOCKS):
        rows = pl.ds(8 * b, 8)
        here = density(ocean[0, k, rows, :], ocean[1, k, rows, :], wet_of(levels[rows, :].astype(F32), k))
        total = cum[rows, :] + here
        cum[rows, :] = total
        pressure.append(THICKNESS * (total - 0.5 * here))
    for b in blocks:
        rows = pl.ds(8 * b, 8)
        here = density(halo_of(0, rows), halo_of(1, rows), wet_of(lev_halo[rows, :], k))
        total = cum_halo[rows, :] + here
        cum_halo[rows, :] = total
        pressure_halo[b] = THICKNESS * (total - 0.5 * here)
    result = {}
    for b in blocks:
        rows = pl.ds(8 * b, 8)
        wet = wet_of(levels[rows, :].astype(F32), k)
        grad_lon = 0.5 * (
            next_lon(pressure[b], pressure_halo[b], 1) - next_lon(pressure[b], pressure_halo[b], -1)
        )
        ahead = pressure[b] if b == BLOCKS - 1 else jnp.where(sub == 0, pressure[b + 1], pressure[b])
        behind = pressure[b] if b == 0 else jnp.where(sub == 7, pressure[b - 1], pressure[b])
        grad_lat = 0.5 * (roll(ahead, -1, 0) - roll(behind, 1, 0))
        if b == 0:
            grad_lat = jnp.where(sub >= 1, grad_lat, 0.0)
        if b == BLOCKS - 1:
            grad_lat = jnp.where(sub <= 6, grad_lat, 0.0)
        u, v, turn = ocean[2, k, rows, :], ocean[3, k, rows, :], coriolis[rows, :]
        accel_u = wet * (turn * v - grad_lon - (lon[0, b] + lat[0, b]))
        accel_v = wet * (-turn * u - grad_lat - (lon[1, b] + lat[1, b]))
        result[b] = (accel_u, accel_v, wet * u, wet * v)
    return result


EARLY = (2, 3, 0)
OUTER = (0, BLOCKS - 1)
INNER = tuple(range(1, BLOCKS - 1))


def early_kernel(ocean, levels, lat):
    def level(k, carry):
        terms = lat_terms(ocean, levels, k, EARLY, range(BLOCKS))
        for n in range(len(EARLY)):
            for b in range(BLOCKS):
                lat[n, k, pl.ds(8 * b, 8), :] = terms[n, b]
        return carry

    over_levels(level)


def outer_kernel(
    ocean, levels, surface, coriolis, own, swap_0, swap_1, lat,
    accel, even_out, odd_out, sums, west_flux, packed, cum, cum_halo, lev_halo,
):
    sub = row_index()
    even_lat = even_tile("lat")
    west_faces(
        own, (swap_0, swap_1), levels, (2, 3), (0, 1, 2, 3), packed, lev_halo, west_flux, OUTER
    )
    cum[...] = jnp.zeros_like(cum)
    cum_halo[...] = jnp.zeros_like(cum_halo)
    sums[...] = jnp.zeros_like(sums)

    def send(index, south, north):
        even_out[index] = jnp.where(even_lat, north, south)
        odd_out[index] = jnp.where(even_lat, south, north)

    first, last_rows = pl.ds(0, 8), pl.ds(ROWS - 8, 8)

    def level(k, carry):
        for pair in range(2):
            t0, t3 = ocean[pair, k, first, :], ocean[pair, k, last_rows, :]
            u0, u3 = ocean[pair + 2, k, first, :], ocean[pair + 2, k, last_rows, :]
            send(
                pair * LEVELS + k,
                jnp.where(sub < 5, u0, roll(t0, 5, 0)),
                jnp.where(sub < 3, roll(t3, 3, 0), u3),
            )
        given = {(n, b): lat[n, k, pl.ds(8 * b, 8), :] for n in range(2) for b in OUTER}
        terms = momentum_level(
            ocean, levels, coriolis, k, packed, lev_halo, west_flux, cum, cum_halo, OUTER, given
        )
        for side, b in enumerate(OUTER):
            for n in range(2):
                accel[n, k, side] = terms[b][n]
            for n in range(4):
                sums[n, pl.ds(8 * b, 8), :] += terms[b][n]
        return carry

    over_levels(level)
    flat = [sums.at[0], sums.at[1], surface.at[0], surface.at[1], surface.at[2], levels]
    for n, field in enumerate(flat):
        send(2 * LEVELS + n, field[first, :].astype(F32), field[last_rows, :].astype(F32))


def inner_kernel(
    ocean, levels, coriolis, own, swap_0, swap_1, lat, outer_accel, outer_sums,
    accel, sums, west_flux, packed, cum, cum_halo, lev_halo,
):
    west_faces(
        own, (swap_0, swap_1), levels, (2, 3), (0, 1, 2, 3), packed, lev_halo, west_flux, INNER
    )
    cum[...] = jnp.zeros_like(cum)
    cum_halo[...] = jnp.zeros_like(cum_halo)
    sums[...] = outer_sums[...]

    def level(k, carry):
        given = {(n, b): lat[n, k, pl.ds(8 * b, 8), :] for n in range(2) for b in INNER}
        terms = momentum_level(
            ocean, levels, coriolis, k, packed, lev_halo, west_flux, cum, cum_halo, INNER, given
        )
        for b in INNER:
            rows = pl.ds(8 * b, 8)
            for n in range(4):
                if n < 2:
                    accel[n, k, rows, :] = terms[b][n]
                sums[n, rows, :] += terms[b][n]
        for n in range(2):
            for side, b in enumerate(OUTER):
                accel[n, k, pl.ds(8 * b, 8), :] = outer_accel[n, k, side]
        return carry

    over_levels(level)


def tracer_kernel(q, ocean, levels, own, swap_0, swap_1, *rest):
    early = EARLY.index(q) if q in EARLY else None
    lat_part = rest[0]
    tracer, west_flux, packed, lev_halo = rest[-4:]
    blocks = range(BLOCKS)
    west_faces(own, (swap_0, swap_1), levels, (q,), (q, 2), packed, lev_halo, west_flux, blocks)

    def level(k, carry):
        halo_of = halo_reader(packed, k)
        lon = lon_terms(ocean, levels, k, halo_of, lev_halo, (q,), west_flux, blocks)
        if early is None:
            lat = lat_terms(ocean, levels, k, (q,), blocks)
        else:
            lat = {(0, b): lat_part[early, k, pl.ds(8 * b, 8), :] for b in blocks}
        for b in blocks:
            rows = pl.ds(8 * b, 8)
            wet = wet_of(levels[rows, :].astype(F32), k)
            tracer[k, rows, :] = wet * (ocean[q, k, rows, :] - TRACER_STEP * (lon[0, b] + lat[0, b]))
        return carry

    over_levels(level)


def window(low_block, high_block, d):
    if d == 8:
        return high_block
    return roll(jnp.where(row_index() >= d, low_block, high_block), -d, 0)


def edge_blocks(ocean, arrived, q, k, side):
    own = ocean[q, k, pl.ds(0 if side == 0 else ROWS - 8, 8), :]
    piece = arrived[(q % 2) * LEVELS + k]
    if side == 0:
        return (roll(piece, 5, 0) if q < 2 else piece), own
    return own, (roll(piece, 3, 0) if q < 2 else piece)


def edge_levels(levels, arrived, side):
    own = levels[pl.ds(0 if side == 0 else ROWS - 8, 8), :].astype(F32)
    return (arrived[PIECES - 1], own) if side == 0 else (own, arrived[PIECES - 1])


def edge_terms(ocean, k, arrived, side, lev5, lev6, quantities):
    sub = row_index()
    v = edge_blocks(ocean, arrived, 3, k, side)
    speed = 0.5 * (window(*v, 5) + window(*v, 6)) * wet_of(jnp.minimum(lev5, lev6), k)
    terms = []
    for q in quantities:
        x = v if q == 3 else edge_blocks(ocean, arrived, q, k, side)
        flux = upwind_flux(speed, *[window(*x, d) for d in (3, 4, 5, 6, 7, 8)])
        flux = jnp.where(sub < 5, flux, 0.0)
        terms.append(flux - jnp.where(sub == 0, 0.0, roll(flux, 1, 0)))
    return terms


def own_rows(term, side):
    sub = row_index()
    if side == 0:
        return jnp.where(sub < 3, roll(term, -3, 0), 0.0)
    return jnp.where(sub >= 5, roll(term, 5, 0), 0.0)


def halo_rows(term, side):
    sub = row_index()
    if side == 0:
        return jnp.where(sub >= 5, roll(term, 5, 0), 0.0)
    return jnp.where(sub < 3, roll(term, -3, 0), 0.0)


def place_arrivals(up, down, south, north):
    even_lat = even_tile("lat")
    at_south = lax.axis_index("lat") == 0
    at_fold = lax.axis_index("lat") == lax.axis_size("lat") - 1
    turned_row, turned_lane = 7 - row_index(), COLS - 1 - lane_index()
    pair_sign = jnp.where(row_index() < 5, -1.0, 1.0)

    def piece(n, sign):
        south[n] = jnp.where(at_south, 0.0, jnp.where(even_lat, down[n], up[n]))
        here = jnp.where(even_lat, up[n], down[n])
        turned = jnp.take_along_axis(jnp.take_along_axis(here, turned_lane, axis=1), turned_row, axis=0)
        north[n] = jnp.where(at_fold, turned * sign, here)

    for n in range(2 * LEVELS):
        piece(n, pair_sign)
    for n, sign in enumerate((-1.0, -1.0, 1.0, -1.0, -1.0, 1.0)):
        piece(2 * LEVELS + n, sign)


def edge_kernel(
    ocean, levels, surface, sums, up, down, after,
    edges, fields, packed, means, south, north, cum, total,
):
    del after
    place_arrivals(up, down, south, north)
    sub = row_index()
    cum[...] = jnp.zeros_like(cum)
    total[...] = jnp.zeros_like(total)
    arrived = (south, north)

    def level(k, carry):
        for side in range(2):
            lev = edge_levels(levels, arrived[side], side)
            lev5, lev6 = window(*lev, 5), window(*lev, 6)
            terms = edge_terms(ocean, k, arrived[side], side, lev5, lev6, (2, 3))
            t = edge_blocks(ocean, arrived[side], 0, k, side)
            s = edge_blocks(ocean, arrived[side], 1, k, side)
            pressure = []
            for half in range(2):
                here = density(t[half], s[half], wet_of(lev[half], k))
                column = cum[side, half] + here
                cum[side, half] = column
                pressure.append(THICKNESS * (column - 0.5 * here))
            grad = 0.5 * (window(*pressure, 6) - window(*pressure, 4))
            grad = jnp.where((sub == 2) | (sub == 3), grad, 0.0)
            wet = wet_of(lev5, k)
            for n, term in enumerate((-wet * terms[0], -wet * (terms[1] + grad))):
                total[side, n] += term
                edges[side, n, k] = own_rows(term, side)
        return carry

    over_levels(level)
    rim = ROWS + 16
    own = pl.ds(8, ROWS)
    for n in range(3):
        fields[n, pl.ds(0, 8), :] = south[2 * LEVELS + 2 + n]
        fields[n, own, :] = surface[n]
        fields[n, pl.ds(rim - 8, 8), :] = north[2 * LEVELS + 2 + n]
    fields[3, pl.ds(0, 8), :] = south[PIECES - 1]
    fields[3, own, :] = levels[...].astype(F32)
    fields[3, pl.ds(rim - 8, 8), :] = north[PIECES - 1]
    for n in range(2):
        fields[4 + n, pl.ds(0, 8), :] = south[2 * LEVELS + n] + halo_rows(total[0, n], 0)
        fields[4 + n, own, :] = sums[n]
        fields[4 + n, pl.ds(8, 8), :] += own_rows(total[0, n], 0)
        fields[4 + n, pl.ds(ROWS, 8), :] += own_rows(total[1, n], 1)
        fields[4 + n, pl.ds(rim - 8, 8), :] = north[2 * LEVELS + n] + halo_rows(total[1, n], 1)
    for n in range(2):
        safe = jnp.maximum(THICKNESS * levels[...].astype(F32), THICKNESS)
        means[n] = THICKNESS * (sums[2 + n] + TRACER_STEP * fields[4 + n, own, :]) / safe
    for b in range(rim // 8):
        rows = pl.ds(8 * b, 8)
        safe = jnp.maximum(THICKNESS * fields[3, rows, :], THICKNESS)
        group = lane_index() // 16
        out = jnp.zeros((8, COLS), F32)
        for n in range(6):
            if n >= 4:
                fields[n, rows, :] = THICKNESS * fields[n, rows, :] / safe
            out = jnp.where(group == n, roll(fields[n, rows, :], 16 * n + 8, 1), out)
        packed[rows, :] = out


def tracer_edge_kernel(ocean, levels, south, north, edges):
    arrived = (south, north)

    def level(k, carry):
        for side in range(2):
            lev = edge_levels(levels, arrived[side], side)
            lev5, lev6 = window(*lev, 5), window(*lev, 6)
            wet = wet_of(lev5, k)
            terms = edge_terms(ocean, k, arrived[side], side, lev5, lev6, (0, 1))
            for n in range(2):
                edges[side, n, k] = own_rows(-wet * terms[n], side)
        return carry

    over_levels(level)


def final_kernel(
    ocean, levels, accel, temperature, salinity, edges, tracer_edges, fields, means, swap_0, swap_1,
    ocean_out, surface_out, shift, result, sems,
):
    copies = [pltpu.make_async_copy(result.at[n], ocean_out.at[n], sems.at[n]) for n in range(4)]

    def tracer_level(k, carry):
        for b in range(BLOCKS):
            rows = pl.ds(8 * b, 8)
            for n in range(2):
                tracer = (temperature, salinity)[n][k, rows, :]
                if b in (0, BLOCKS - 1):
                    tracer = tracer + TRACER_STEP * tracer_edges[min(b, 1), n, k]
                result[n, k, rows, :] = tracer
        return carry

    over_levels(tracer_level)
    copies[0].start()
    copies[1].start()
    rim = ROWS + 16
    lane = lane_index(rim)
    even = even_tile("lon")
    low = jnp.where(even, swap_1[...], swap_0[...])
    high = jnp.where(even, swap_0[...], swap_1[...])
    halos = jnp.where(lane % 16 < 8, low, high)
    both = []
    for n in range(6):
        both.append((fields[n], roll(halos, -(16 * n + 8), 1)))
    height, mean_u, mean_v, level_map, force_lon, force_lat = both
    depth = tuple(THICKNESS * x for x in level_map)
    sea = tuple(jnp.where(x > 0.0, 1.0, 0.0) for x in level_map)

    def d_lon(x):
        main, halo = x
        result = []
        for here, other in ((main, halo), (halo, main)):
            ahead = roll(jnp.where(lane == 0, other, here), -1, 1)
            behind = roll(jnp.where(lane == COLS - 1, other, here), 1, 1)
            result.append(0.5 * (ahead - behind))
        return result

    def d_lat(x):
        return [0.5 * (roll(part, -1, 0) - roll(part, 1, 0)) for part in x]

    def times(x, y):
        return [p * q for p, q in zip(x, y)]

    for _ in range(NSUB):
        along, across = d_lon(times(depth, mean_u)), d_lat(times(depth, mean_v))
        height = [s * (h - SURFACE_STEP * (p + q)) for s, h, p, q in zip(sea, height, along, across)]
        mean_u = [
            s * (m + SURFACE_STEP * (f - d)) for s, m, f, d in zip(sea, mean_u, force_lon, d_lon(height))
        ]
        mean_v = [
            s * (m + SURFACE_STEP * (f - d)) for s, m, f, d in zip(sea, mean_v, force_lat, d_lat(height))
        ]
    for n, field in enumerate((height, mean_u, mean_v)):
        surface_out[n] = field[0][8 : 8 + ROWS]
    shift[0] = mean_u[0][8 : 8 + ROWS] - means[0]
    shift[1] = mean_v[0][8 : 8 + ROWS] - means[1]

    for n in range(2):

        def level(k, carry, n=n):
            for b in range(BLOCKS):
                rows = pl.ds(8 * b, 8)
                wet = wet_of(levels[rows, :].astype(F32), k)
                force = accel[n, k, rows, :]
                if b in (0, BLOCKS - 1):
                    force = force + edges[min(b, 1), n, k]
                result[2 + n, k, rows, :] = wet * (
                    ocean[2 + n, k, rows, :] + TRACER_STEP * force + shift[n, rows, :]
                )
            return carry

        over_levels(level)
        copies[2 + n].start()
    for copy in copies:
        copy.wait()


def swapped(pairs):
    return list(pairs) + [(b, a) for a, b in pairs]


def swap_lon(x):
    count = lax.axis_size("lon")
    first = swapped([(i, i + 1) for i in range(0, count, 2)])
    second = swapped([(i, (i + 1) % count) for i in range(1, count, 2)])
    second = lax.ppermute(x, "lon", second)
    return lax.ppermute(x, "lon", first), second


def swap_lat(x, y):
    lon_count, lat_count = lax.axis_size("lon"), lax.axis_size("lat")
    first, second = [], []
    for p in range(lon_count):
        base = p * lat_count
        first += [(base + r, base + r + 1) for r in range(0, lat_count, 2)]
        second += [(base + r, base + r + 1) for r in range(1, lat_count - 1, 2)]
        if p < lon_count // 2:
            second.append((base + lat_count - 1, (lon_count - p) * lat_count - 1))
    y = lax.ppermute(y, ("lon", "lat"), swapped(second))
    x = lax.ppermute(x, ("lon", "lat"), swapped(first))
    return x, y


def call(kernel, outs, scratch=(), operands=1, unread=0, cost=1000000, limit=16):
    def vmem():
        return pl.BlockSpec(memory_space=pltpu.VMEM)

    specs = [vmem()] * operands
    specs += [pl.BlockSpec(memory_space=pl.ANY)] * unread
    single = len(outs) == 1
    shapes = [jax.ShapeDtypeStruct(shape, F32) for shape in outs]
    return pl.pallas_call(
        kernel,
        out_shape=shapes[0] if single else shapes,
        in_specs=specs,
        out_specs=vmem() if single else [vmem() for _ in outs],
        scratch_shapes=[pltpu.VMEM(shape, F32) for shape in scratch],
        cost_estimate=pl.CostEstimate(flops=cost, bytes_accessed=cost, transcendentals=0),
        compiler_params=pltpu.CompilerParams(vmem_limit_bytes=limit << 20),
    )


def on_device(ocean, surface, levels):
    tile = (ROWS, COLS)
    rim = (ROWS + 16, COLS)
    own = pl.pallas_call(
        pack_kernel,
        out_shape=jax.ShapeDtypeStruct((5, *tile), F32),
        in_specs=[pl.BlockSpec(memory_space=pl.ANY)] * 2,
        out_specs=pl.BlockSpec(memory_space=pltpu.VMEM),
        scratch_shapes=[
            pltpu.VMEM(ocean.shape, F32),
            pltpu.VMEM(tile, jnp.int32),
            pltpu.SemaphoreType.DMA((4,)),
            pltpu.SemaphoreType.DMA(()),
        ],
        compiler_params=pltpu.CompilerParams(vmem_limit_bytes=66900000),
    )(ocean, levels)
    lon_0, lon_1 = swap_lon(own)
    lat_index, lat_count = lax.axis_index("lat"), lax.axis_size("lat")
    own = jnp.where(lat_index < 0, 0.0, own)
    row = lat_index * ROWS + lax.broadcasted_iota(jnp.int32, tile, 0)
    latitude = (row.astype(F32) + 0.5) / float(lat_count * ROWS)
    coriolis = jnp.sin(math.pi * latitude - 0.5 * math.pi)
    momentum_scratch = [(2, *tile), (4, *tile), tile, tile, tile]
    half = (2, LEVELS, 2, 8, COLS)
    arrivals = [(PIECES, 8, COLS)] * 2
    lat_part = call(early_kernel, [(len(EARLY), LEVELS, *tile)], operands=2, cost=100000000)(ocean, levels)
    outer_accel, lat_0, lat_1, outer_sums = call(
        outer_kernel,
        [half, *arrivals, (4, *tile)],
        scratch=momentum_scratch,
        operands=8,
    )(ocean, levels, surface, coriolis, own, lon_0, lon_1, lat_part)
    lat_0, lat_1 = swap_lat(lat_0, lat_1)
    accel, sums = call(
        inner_kernel,
        [(2, LEVELS, *tile), (4, *tile)],
        scratch=momentum_scratch,
        operands=9,
        cost=100000000,
    )(ocean, levels, coriolis, own, lon_0, lon_1, lat_part, outer_accel, outer_sums)

    def tracer(q, after):
        return call(
            functools.partial(tracer_kernel, q),
            [(LEVELS, *tile)],
            scratch=[(1, *tile), (3, *tile), tile],
            operands=5 + (q in EARLY),
            unread=1,
            cost=100000000,
        )(ocean, levels, own, lon_0, lon_1, *([lat_part] if q in EARLY else []), after)

    temperature = tracer(0, sums)
    edges, fields, packed, means, south, north = call(
        edge_kernel,
        [(2, 2, LEVELS, 8, COLS), (6, *rim), rim, (2, *tile), *arrivals],
        scratch=[(2, 2, 8, COLS), (2, 2, 8, COLS)],
        operands=6,
        unread=1,
    )(ocean, levels, surface, sums, lat_0, lat_1, temperature)
    rim_0, rim_1 = swap_lon(packed)
    tracer_edges = call(
        tracer_edge_kernel, [(2, 2, LEVELS, 8, COLS)], operands=4, cost=100000000
    )(ocean, levels, south, north)
    salinity = tracer(1, means)
    vmem = pl.BlockSpec(memory_space=pltpu.VMEM)
    return pl.pallas_call(
        final_kernel,
        out_shape=[jax.ShapeDtypeStruct((4, LEVELS, *tile), F32), jax.ShapeDtypeStruct((3, *tile), F32)],
        in_specs=[vmem] * 11,
        out_specs=[pl.BlockSpec(memory_space=pl.ANY), vmem],
        scratch_shapes=[
            pltpu.VMEM((2, *tile), F32),
            pltpu.VMEM((4, LEVELS, *tile), F32),
            pltpu.SemaphoreType.DMA((4,)),
        ],
        compiler_params=pltpu.CompilerParams(vmem_limit_bytes=16 << 20),
    )(ocean, levels, accel, temperature, salinity, edges, tracer_edges, fields, means, rim_0, rim_1)


def solution(mesh):
    return jax.shard_map(
        on_device,
        mesh=mesh,
        in_specs=(P(None, None, "lat", "lon"), P(None, "lat", "lon"), P("lat", "lon")),
        out_specs=(P(None, None, "lat", "lon"), P(None, "lat", "lon")),
        check_vma=False,
    )
```

```python
import functools
import math

import jax
import jax.numpy as jnp
from jax import lax
from jax.experimental import pallas as pl
from jax.experimental.pallas import tpu as pltpu
from jax.sharding import PartitionSpec as P


NSUB = 4
LEVELS = 16
ROWS = 32
COLS = 128
PER_STEP = 4
BLOCKS = ROWS // 8
THICKNESS = 1.0 / LEVELS
TRACER_STEP = 0.1
SURFACE_STEP = 1.2
PIECES = 2 * LEVELS + 6

F32 = jnp.float32


def over_levels(level):
    def step(i, carry):
        for j in range(PER_STEP):
            level(PER_STEP * i + j, carry)
        return carry

    lax.fori_loop(0, LEVELS // PER_STEP, step, 0)


def even_tile(axis):
    return lax.rem(lax.axis_index(axis), 2) == 0


def lane_index(rows=8):
    return lax.broadcasted_iota(jnp.int32, (rows, COLS), 1)


def row_index(rows=8):
    return lax.broadcasted_iota(jnp.int32, (rows, COLS), 0)


def roll(x, shift, axis):
    if isinstance(shift, int):
        shift %= x.shape[axis]
        if shift == 0:
            return x
    return pltpu.roll(x, shift, axis)


def upwind_flux(speed, qm2, qm1, q0, q1, q2, q3):
    ahead = speed >= 0.0
    a = jnp.where(ahead, qm2, q3)
    b = jnp.where(ahead, qm1, q2)
    c = jnp.where(ahead, q0, q1)
    d = jnp.where(ahead, q1, q0)
    e = jnp.where(ahead, q2, qm1)
    ab = a - b
    bc = b - c
    cd = c - d
    de = d - e
    x1 = ab - bc
    y1 = ab - 3.0 * bc
    x2 = bc - cd
    y2 = bc + cd
    x3 = cd - de
    y3 = 3.0 * cd - de
    third = 13.0 / 3.0
    s1 = third * (x1 * x1) + (y1 * y1 + 4e-6)
    s2 = third * (x2 * x2) + (y2 * y2 + 4e-6)
    s3 = third * (x3 * x3) + (y3 * y3 + 4e-6)
    r1 = s2 * s3
    r2 = s1 * s3
    r3 = s1 * s2
    w1 = r1 * r1
    w2 = 6.0 * (r2 * r2)
    w3 = 3.0 * (r3 * r3)
    top = w1 * (2.0 * ab - 5.0 * bc) - w2 * (bc + 2.0 * cd) + w3 * (de - 4.0 * cd)
    low = 6.0 * (w1 + w2 + w3)
    return speed * (c + top / low)


def density(t, s, wet):
    return wet * (t * (0.03 * s - 0.2 - 0.05 * t) + 0.8 * s)


def wet_of(level_map, k):
    return jnp.where(level_map > k, 1.0, 0.0).astype(F32)


def pack_kernel(ocean_hbm, levels_hbm, out, ocean, levels, sems, level_sem):
    copies = [pltpu.make_async_copy(ocean_hbm.at[q], ocean.at[q], sems.at[q]) for q in range(4)]
    level_copy = pltpu.make_async_copy(levels_hbm, levels, level_sem)
    for copy in copies:
        copy.start()
    level_copy.start()
    lane = lane_index()
    group = lane // 8
    for q in range(4):
        copies[q].wait()
        for b in range(BLOCKS):
            rows = pl.ds(8 * b, 8)
            packed = jnp.zeros((8, COLS), F32)
            for k in range(LEVELS):
                packed = jnp.where(group == k, roll(ocean[q, k, rows, :], 8 * k + 4, 1), packed)
            out[q, rows, :] = packed
    level_copy.wait()
    for b in range(BLOCKS):
        rows = pl.ds(8 * b, 8)
        lev = levels[rows, :].astype(F32)
        packed = jnp.where(lane == 7, roll(lev, 8, 1), out[0, rows, :])
        out[0, rows, :] = jnp.where(lane == 15, roll(lev, 15, 1), packed)


def low_piece(q, rows, even, swaps):
    return jnp.where(even, swaps[1][q, rows, :], swaps[0][q, rows, :])


def high_piece(q, rows, even, swaps):
    return jnp.where(even, swaps[0][q, rows, :], swaps[1][q, rows, :])


def halo_pack(q, rows, even, swaps):
    from_low = lane_index() % 8 < 4
    return jnp.where(from_low, low_piece(q, rows, even, swaps), high_piece(q, rows, even, swaps))


def next_lon(main, halo, step):
    lane = lane_index()
    if step > 0:
        return roll(jnp.where(lane < step, halo, main), -step, 1)
    return roll(jnp.where(lane >= COLS + step, halo, main), -step, 1)


def lon_shifts(main, halo):
    return [main if d == 0 else next_lon(main, halo, d) for d in (-2, -1, 0, 1, 2, 3)]


def west_faces(own, swaps, levels, quantities, halo_quantities, packed, lev_halo, west_flux, blocks):
    lane = lane_index()
    from_low = lane % 8 < 4
    level_of = lane // 8
    even = even_tile("lon")
    for b in blocks:
        rows = pl.ds(8 * b, 8)
        lev = levels[rows, :].astype(F32)
        own_col = lev[:, 0:1]
        west_col = low_piece(0, rows, even, swaps)[:, 7:8]
        both = jnp.minimum(own_col, west_col)
        wet = jnp.where(both > level_of.astype(F32), 1.0, 0.0)
        u = jnp.where(from_low, low_piece(2, rows, even, swaps), own[2, rows, :])
        speed = 0.5 * (u + roll(u, -1, 1)) * wet
        for n, q in enumerate(quantities):
            x = jnp.where(from_low, low_piece(q, rows, even, swaps), own[q, rows, :])
            west_flux[n, rows, :] = upwind_flux(speed, *[roll(x, -d, 1) for d in (-2, -1, 0, 1, 2, 3)])
        for q in halo_quantities:
            packed[q, rows, :] = halo_pack(q, rows, even, swaps)
        last_col, first_col = low_piece(0, rows, even, swaps), high_piece(0, rows, even, swaps)
        lev_halo[rows, :] = jnp.where(lane == COLS - 1, roll(last_col, -8, 1), roll(first_col, -15, 1))


def lat_shift(ocean, q, k, b, d):
    start = 8 * b + d
    if 0 <= start and start + 8 <= ROWS:
        return ocean[q, k, start : start + 8, :]
    return roll(ocean[q, k, pl.ds(8 * b, 8), :], -d, 0)


def level_map_shift(levels, b, d):
    start = 8 * b + d
    if 0 <= start and start + 8 <= ROWS:
        return levels[start : start + 8, :].astype(F32)
    return roll(levels[pl.ds(8 * b, 8), :].astype(F32), -d, 0)


def lat_terms(ocean, levels, k, quantities, blocks):
    sub = row_index()
    result, last = {}, {}
    for b in blocks:
        rows = pl.ds(8 * b, 8)
        wet = wet_of(levels[rows, :].astype(F32), k)
        wet_north = wet_of(level_map_shift(levels, b, 1), k)
        speed = 0.5 * (ocean[3, k, rows, :] + lat_shift(ocean, 3, k, b, 1)) * (wet * wet_north)
        for n, q in enumerate(quantities):
            north = upwind_flux(speed, *[lat_shift(ocean, q, k, b, d) for d in (-2, -1, 0, 1, 2, 3)])
            if b == 0:
                north = jnp.where(sub >= 2, north, 0.0)
            if b == BLOCKS - 1:
                north = jnp.where(sub <= 4, north, 0.0)
            last[n, b] = roll(north, 1, 0)
            south = jnp.where(sub == 0, last.get((n, b - 1), 0.0), last[n, b])
            result[n, b] = north - south
    return result


def lon_terms(ocean, levels, k, halo_of, lev_halo, quantities, west_flux, blocks):
    lane = lane_index()
    unplace = 124 - 8 * k
    result = {}
    for b in blocks:
        rows = pl.ds(8 * b, 8)
        lev = levels[rows, :].astype(F32)
        wet = wet_of(lev, k)
        u = ocean[2, k, rows, :]
        wet_east = wet_of(next_lon(lev, lev_halo[rows, :], 1), k)
        speed = 0.5 * (u + next_lon(u, halo_of(2, rows), 1)) * (wet * wet_east)
        for n, q in enumerate(quantities):
            main = ocean[q, k, rows, :]
            east = upwind_flux(speed, *lon_shifts(main, halo_of(q, rows)))
            west = pltpu.roll(west_flux[n, rows, :], unplace, 1)
            west = roll(jnp.where(lane == COLS - 1, west, east), 1, 1)
            result[n, b] = east - west
    return result


def halo_reader(packed, k):
    halo = {}

    def halo_of(q, rows):
        key = (q, rows.start)
        if key not in halo:
            halo[key] = pltpu.roll(packed[q, rows, :], 124 - 8 * k, 1)
        return halo[key]

    return halo_of


def momentum_level(ocean, levels, coriolis, k, packed, lev_halo, west_flux, cum, cum_halo, blocks, lat):
    sub = row_index()
    halo_of = halo_reader(packed, k)
    lon = lon_terms(ocean, levels, k, halo_of, lev_halo, (2, 3), west_flux, blocks)
    pressure, pressure_halo = [], {}
    for b in range(BLOCKS):
        rows = pl.ds(8 * b, 8)
        here = density(ocean[0, k, rows, :], ocean[1, k, rows, :], wet_of(levels[rows, :].astype(F32), k))
        total = cum[rows, :] + here
        cum[rows, :] = total
        pressure.append(THICKNESS * (total - 0.5 * here))
    for b in blocks:
        rows = pl.ds(8 * b, 8)
        here = density(halo_of(0, rows), halo_of(1, rows), wet_of(lev_halo[rows, :], k))
        total = cum_halo[rows, :] + here
        cum_halo[rows, :] = total
        pressure_halo[b] = THICKNESS * (total - 0.5 * here)
    result = {}
    for b in blocks:
        rows = pl.ds(8 * b, 8)
        wet = wet_of(levels[rows, :].astype(F32), k)
        grad_lon = 0.5 * (
            next_lon(pressure[b], pressure_halo[b], 1) - next_lon(pressure[b], pressure_halo[b], -1)
        )
        ahead = pressure[b] if b == BLOCKS - 1 else jnp.where(sub == 0, pressure[b + 1], pressure[b])
        behind = pressure[b] if b == 0 else jnp.where(sub == 7, pressure[b - 1], pressure[b])
        grad_lat = 0.5 * (roll(ahead, -1, 0) - roll(behind, 1, 0))
        if b == 0:
            grad_lat = jnp.where(sub >= 1, grad_lat, 0.0)
        if b == BLOCKS - 1:
            grad_lat = jnp.where(sub <= 6, grad_lat, 0.0)
        u, v, turn = ocean[2, k, rows, :], ocean[3, k, rows, :], coriolis[rows, :]
        accel_u = wet * (turn * v - grad_lon - (lon[0, b] + lat[0, b]))
        accel_v = wet * (-turn * u - grad_lat - (lon[1, b] + lat[1, b]))
        result[b] = (accel_u, accel_v, wet * u, wet * v)
    return result


EARLY = (2, 3, 0)
OUTER = (0, BLOCKS - 1)
INNER = tuple(range(1, BLOCKS - 1))


def early_kernel(ocean, levels, lat):
    def level(k, carry):
        terms = lat_terms(ocean, levels, k, EARLY, range(BLOCKS))
        for n in range(len(EARLY)):
            for b in range(BLOCKS):
                lat[n, k, pl.ds(8 * b, 8), :] = terms[n, b]
        return carry

    over_levels(level)


def outer_kernel(
    ocean, levels, surface, coriolis, own, swap_0, swap_1, lat,
    accel, even_out, odd_out, sums, west_flux, packed, cum, cum_halo, lev_halo,
):
    sub = row_index()
    even_lat = even_tile("lat")
    west_faces(
        own, (swap_0, swap_1), levels, (2, 3), (0, 1, 2, 3), packed, lev_halo, west_flux, OUTER
    )
    cum[...] = jnp.zeros_like(cum)
    cum_halo[...] = jnp.zeros_like(cum_halo)
    sums[...] = jnp.zeros_like(sums)

    def send(index, south, north):
        even_out[index] = jnp.where(even_lat, north, south)
        odd_out[index] = jnp.where(even_lat, south, north)

    first, last_rows = pl.ds(0, 8), pl.ds(ROWS - 8, 8)

    def level(k, carry):
        for pair in range(2):
            t0, t3 = ocean[pair, k, first, :], ocean[pair, k, last_rows, :]
            u0, u3 = ocean[pair + 2, k, first, :], ocean[pair + 2, k, last_rows, :]
            send(
                pair * LEVELS + k,
                jnp.where(sub < 5, u0, roll(t0, 5, 0)),
                jnp.where(sub < 3, roll(t3, 3, 0), u3),
            )
        given = {(n, b): lat[n, k, pl.ds(8 * b, 8), :] for n in range(2) for b in OUTER}
        terms = momentum_level(
            ocean, levels, coriolis, k, packed, lev_halo, west_flux, cum, cum_halo, OUTER, given
        )
        for side, b in enumerate(OUTER):
            for n in range(2):
                accel[n, k, side] = terms[b][n]
            for n in range(4):
                sums[n, pl.ds(8 * b, 8), :] += terms[b][n]
        return carry

    over_levels(level)
    flat = [sums.at[0], sums.at[1], surface.at[0], surface.at[1], surface.at[2], levels]
    for n, field in enumerate(flat):
        send(2 * LEVELS + n, field[first, :].astype(F32), field[last_rows, :].astype(F32))


def inner_kernel(
    ocean, levels, coriolis, own, swap_0, swap_1, lat, outer_accel, outer_sums,
    accel, sums, west_flux, packed, cum, cum_halo, lev_halo,
):
    west_faces(
        own, (swap_0, swap_1), levels, (2, 3), (0, 1, 2, 3), packed, lev_halo, west_flux, INNER
    )
    cum[...] = jnp.zeros_like(cum)
    cum_halo[...] = jnp.zeros_like(cum_halo)
    sums[...] = outer_sums[...]

    def level(k, carry):
        given = {(n, b): lat[n, k, pl.ds(8 * b, 8), :] for n in range(2) for b in INNER}
        terms = momentum_level(
            ocean, levels, coriolis, k, packed, lev_halo, west_flux, cum, cum_halo, INNER, given
        )
        for b in INNER:
            rows = pl.ds(8 * b, 8)
            for n in range(4):
                if n < 2:
                    accel[n, k, rows, :] = terms[b][n]
                sums[n, rows, :] += terms[b][n]
        for n in range(2):
            for side, b in enumerate(OUTER):
                accel[n, k, pl.ds(8 * b, 8), :] = outer_accel[n, k, side]
        return carry

    over_levels(level)


def tracer_kernel(q, ocean, levels, own, swap_0, swap_1, *rest):
    early = EARLY.index(q) if q in EARLY else None
    lat_part = rest[0]
    tracer, west_flux, packed, lev_halo = rest[-4:]
    blocks = range(BLOCKS)
    west_faces(own, (swap_0, swap_1), levels, (q,), (q, 2), packed, lev_halo, west_flux, blocks)

    def level(k, carry):
        halo_of = halo_reader(packed, k)
        lon = lon_terms(ocean, levels, k, halo_of, lev_halo, (q,), west_flux, blocks)
        if early is None:
            lat = lat_terms(ocean, levels, k, (q,), blocks)
        else:
            lat = {(0, b): lat_part[early, k, pl.ds(8 * b, 8), :] for b in blocks}
        for b in blocks:
            rows = pl.ds(8 * b, 8)
            wet = wet_of(levels[rows, :].astype(F32), k)
            tracer[k, rows, :] = wet * (ocean[q, k, rows, :] - TRACER_STEP * (lon[0, b] + lat[0, b]))
        return carry

    over_levels(level)


def window(low_block, high_block, d):
    if d == 8:
        return high_block
    return roll(jnp.where(row_index() >= d, low_block, high_block), -d, 0)


def edge_blocks(ocean, arrived, q, k, side):
    own = ocean[q, k, pl.ds(0 if side == 0 else ROWS - 8, 8), :]
    piece = arrived[(q % 2) * LEVELS + k]
    if side == 0:
        return (roll(piece, 5, 0) if q < 2 else piece), own
    return own, (roll(piece, 3, 0) if q < 2 else piece)


def edge_levels(levels, arrived, side):
    own = levels[pl.ds(0 if side == 0 else ROWS - 8, 8), :].astype(F32)
    return (arrived[PIECES - 1], own) if side == 0 else (own, arrived[PIECES - 1])


def edge_terms(ocean, k, arrived, side, lev5, lev6, quantities):
    sub = row_index()
    v = edge_blocks(ocean, arrived, 3, k, side)
    speed = 0.5 * (window(*v, 5) + window(*v, 6)) * wet_of(jnp.minimum(lev5, lev6), k)
    terms = []
    for q in quantities:
        x = v if q == 3 else edge_blocks(ocean, arrived, q, k, side)
        flux = upwind_flux(speed, *[window(*x, d) for d in (3, 4, 5, 6, 7, 8)])
        flux = jnp.where(sub < 5, flux, 0.0)
        terms.append(flux - jnp.where(sub == 0, 0.0, roll(flux, 1, 0)))
    return terms


def own_rows(term, side):
    sub = row_index()
    if side == 0:
        return jnp.where(sub < 3, roll(term, -3, 0), 0.0)
    return jnp.where(sub >= 5, roll(term, 5, 0), 0.0)


def halo_rows(term, side):
    sub = row_index()
    if side == 0:
        return jnp.where(sub >= 5, roll(term, 5, 0), 0.0)
    return jnp.where(sub < 3, roll(term, -3, 0), 0.0)


def place_arrivals(up, down, south, north):
    even_lat = even_tile("lat")
    at_south = lax.axis_index("lat") == 0
    at_fold = lax.axis_index("lat") == lax.axis_size("lat") - 1
    turned_row, turned_lane = 7 - row_index(), COLS - 1 - lane_index()
    pair_sign = jnp.where(row_index() < 5, -1.0, 1.0)

    def piece(n, sign):
        south[n] = jnp.where(at_south, 0.0, jnp.where(even_lat, down[n], up[n]))
        here = jnp.where(even_lat, up[n], down[n])
        turned = jnp.take_along_axis(jnp.take_along_axis(here, turned_lane, axis=1), turned_row, axis=0)
        north[n] = jnp.where(at_fold, turned * sign, here)

    for n in range(2 * LEVELS):
        piece(n, pair_sign)
    for n, sign in enumerate((-1.0, -1.0, 1.0, -1.0, -1.0, 1.0)):
        piece(2 * LEVELS + n, sign)


def edge_kernel(
    ocean, levels, surface, sums, up, down, after,
    edges, fields, packed, means, south, north, cum, total,
):
    del after
    place_arrivals(up, down, south, north)
    sub = row_index()
    cum[...] = jnp.zeros_like(cum)
    total[...] = jnp.zeros_like(total)
    arrived = (south, north)

    def level(k, carry):
        for side in range(2):
            lev = edge_levels(levels, arrived[side], side)
            lev5, lev6 = window(*lev, 5), window(*lev, 6)
            terms = edge_terms(ocean, k, arrived[side], side, lev5, lev6, (2, 3))
            t = edge_blocks(ocean, arrived[side], 0, k, side)
            s = edge_blocks(ocean, arrived[side], 1, k, side)
            pressure = []
            for half in range(2):
                here = density(t[half], s[half], wet_of(lev[half], k))
                column = cum[side, half] + here
                cum[side, half] = column
                pressure.append(THICKNESS * (column - 0.5 * here))
            grad = 0.5 * (window(*pressure, 6) - window(*pressure, 4))
            grad = jnp.where((sub == 2) | (sub == 3), grad, 0.0)
            wet = wet_of(lev5, k)
            for n, term in enumerate((-wet * terms[0], -wet * (terms[1] + grad))):
                total[side, n] += term
                edges[side, n, k] = own_rows(term, side)
        return carry

    over_levels(level)
    rim = ROWS + 16
    own = pl.ds(8, ROWS)
    for n in range(3):
        fields[n, pl.ds(0, 8), :] = south[2 * LEVELS + 2 + n]
        fields[n, own, :] = surface[n]
        fields[n, pl.ds(rim - 8, 8), :] = north[2 * LEVELS + 2 + n]
    fields[3, pl.ds(0, 8), :] = south[PIECES - 1]
    fields[3, own, :] = levels[...].astype(F32)
    fields[3, pl.ds(rim - 8, 8), :] = north[PIECES - 1]
    for n in range(2):
        fields[4 + n, pl.ds(0, 8), :] = south[2 * LEVELS + n] + halo_rows(total[0, n], 0)
        fields[4 + n, own, :] = sums[n]
        fields[4 + n, pl.ds(8, 8), :] += own_rows(total[0, n], 0)
        fields[4 + n, pl.ds(ROWS, 8), :] += own_rows(total[1, n], 1)
        fields[4 + n, pl.ds(rim - 8, 8), :] = north[2 * LEVELS + n] + halo_rows(total[1, n], 1)
    for n in range(2):
        safe = jnp.maximum(THICKNESS * levels[...].astype(F32), THICKNESS)
        means[n] = THICKNESS * (sums[2 + n] + TRACER_STEP * fields[4 + n, own, :]) / safe
    for b in range(rim // 8):
        rows = pl.ds(8 * b, 8)
        safe = jnp.maximum(THICKNESS * fields[3, rows, :], THICKNESS)
        group = lane_index() // 16
        out = jnp.zeros((8, COLS), F32)
        for n in range(6):
            if n >= 4:
                fields[n, rows, :] = THICKNESS * fields[n, rows, :] / safe
            out = jnp.where(group == n, roll(fields[n, rows, :], 16 * n + 8, 1), out)
        packed[rows, :] = out


def tracer_edge_kernel(ocean, levels, south, north, edges):
    arrived = (south, north)

    def level(k, carry):
        for side in range(2):
            lev = edge_levels(levels, arrived[side], side)
            lev5, lev6 = window(*lev, 5), window(*lev, 6)
            wet = wet_of(lev5, k)
            terms = edge_terms(ocean, k, arrived[side], side, lev5, lev6, (0, 1))
            for n in range(2):
                edges[side, n, k] = own_rows(-wet * terms[n], side)
        return carry

    over_levels(level)


def final_kernel(
    ocean, levels, accel, temperature, salinity, edges, tracer_edges, fields, means, swap_0, swap_1,
    ocean_out, surface_out, shift,
):
    rim = ROWS + 16
    lane = lane_index(rim)
    even = even_tile("lon")
    low = jnp.where(even, swap_1[...], swap_0[...])
    high = jnp.where(even, swap_0[...], swap_1[...])
    halos = jnp.where(lane % 16 < 8, low, high)
    both = []
    for n in range(6):
        both.append((fields[n], roll(halos, -(16 * n + 8), 1)))
    height, mean_u, mean_v, level_map, force_lon, force_lat = both
    depth = tuple(THICKNESS * x for x in level_map)
    sea = tuple(jnp.where(x > 0.0, 1.0, 0.0) for x in level_map)

    def d_lon(x):
        main, halo = x
        result = []
        for here, other in ((main, halo), (halo, main)):
            ahead = roll(jnp.where(lane == 0, other, here), -1, 1)
            behind = roll(jnp.where(lane == COLS - 1, other, here), 1, 1)
            result.append(0.5 * (ahead - behind))
        return result

    def d_lat(x):
        return [0.5 * (roll(part, -1, 0) - roll(part, 1, 0)) for part in x]

    def times(x, y):
        return [p * q for p, q in zip(x, y)]

    for _ in range(NSUB):
        along, across = d_lon(times(depth, mean_u)), d_lat(times(depth, mean_v))
        height = [s * (h - SURFACE_STEP * (p + q)) for s, h, p, q in zip(sea, height, along, across)]
        mean_u = [
            s * (m + SURFACE_STEP * (f - d)) for s, m, f, d in zip(sea, mean_u, force_lon, d_lon(height))
        ]
        mean_v = [
            s * (m + SURFACE_STEP * (f - d)) for s, m, f, d in zip(sea, mean_v, force_lat, d_lat(height))
        ]
    for n, field in enumerate((height, mean_u, mean_v)):
        surface_out[n] = field[0][8 : 8 + ROWS]
    shift[0] = mean_u[0][8 : 8 + ROWS] - means[0]
    shift[1] = mean_v[0][8 : 8 + ROWS] - means[1]

    def level(k, carry):
        for b in range(BLOCKS):
            rows = pl.ds(8 * b, 8)
            wet = wet_of(levels[rows, :].astype(F32), k)
            for n in range(2):
                tracer, force = (temperature, salinity)[n][k, rows, :], accel[n, k, rows, :]
                if b in (0, BLOCKS - 1):
                    side = min(b, 1)
                    tracer = tracer + TRACER_STEP * tracer_edges[side, n, k]
                    force = force + edges[side, n, k]
                ocean_out[n, k, rows, :] = tracer
                ocean_out[2 + n, k, rows, :] = wet * (
                    ocean[2 + n, k, rows, :] + TRACER_STEP * force + shift[n, rows, :]
                )
        return carry

    over_levels(level)


def swapped(pairs):
    return list(pairs) + [(b, a) for a, b in pairs]


def swap_lon(x):
    count = lax.axis_size("lon")
    first = swapped([(i, i + 1) for i in range(0, count, 2)])
    second = swapped([(i, (i + 1) % count) for i in range(1, count, 2)])
    second = lax.ppermute(x, "lon", second)
    return lax.ppermute(x, "lon", first), second


def swap_lat(x, y):
    lon_count, lat_count = lax.axis_size("lon"), lax.axis_size("lat")
    first, second = [], []
    for p in range(lon_count):
        base = p * lat_count
        first += [(base + r, base + r + 1) for r in range(0, lat_count, 2)]
        second += [(base + r, base + r + 1) for r in range(1, lat_count - 1, 2)]
        if p < lon_count // 2:
            second.append((base + lat_count - 1, (lon_count - p) * lat_count - 1))
    y = lax.ppermute(y, ("lon", "lat"), swapped(second))
    x = lax.ppermute(x, ("lon", "lat"), swapped(first))
    return x, y


def call(kernel, outs, scratch=(), operands=1, unread=0, cost=1000000, limit=16):
    def vmem():
        return pl.BlockSpec(memory_space=pltpu.VMEM)

    specs = [vmem()] * operands
    specs += [pl.BlockSpec(memory_space=pl.ANY)] * unread
    single = len(outs) == 1
    shapes = [jax.ShapeDtypeStruct(shape, F32) for shape in outs]
    return pl.pallas_call(
        kernel,
        out_shape=shapes[0] if single else shapes,
        in_specs=specs,
        out_specs=vmem() if single else [vmem() for _ in outs],
        scratch_shapes=[pltpu.VMEM(shape, F32) for shape in scratch],
        cost_estimate=pl.CostEstimate(flops=cost, bytes_accessed=cost, transcendentals=0),
        compiler_params=pltpu.CompilerParams(vmem_limit_bytes=limit << 20),
    )


def on_device(ocean, surface, levels):
    tile = (ROWS, COLS)
    rim = (ROWS + 16, COLS)
    own = pl.pallas_call(
        pack_kernel,
        out_shape=jax.ShapeDtypeStruct((4, *tile), F32),
        in_specs=[pl.BlockSpec(memory_space=pl.ANY)] * 2,
        out_specs=pl.BlockSpec(memory_space=pltpu.VMEM),
        scratch_shapes=[
            pltpu.VMEM(ocean.shape, F32),
            pltpu.VMEM(tile, jnp.int32),
            pltpu.SemaphoreType.DMA((4,)),
            pltpu.SemaphoreType.DMA(()),
        ],
    )(ocean, levels)
    lon_0, lon_1 = swap_lon(own)
    lat_index, lat_count = lax.axis_index("lat"), lax.axis_size("lat")
    own = jnp.where(lat_index < 0, 0.0, own)
    row = lat_index * ROWS + lax.broadcasted_iota(jnp.int32, tile, 0)
    latitude = (row.astype(F32) + 0.5) / float(lat_count * ROWS)
    coriolis = jnp.sin(math.pi * latitude - 0.5 * math.pi)
    momentum_scratch = [(2, *tile), (4, *tile), tile, tile, tile]
    half = (2, LEVELS, 2, 8, COLS)
    arrivals = [(PIECES, 8, COLS)] * 2
    lat_part = call(early_kernel, [(len(EARLY), LEVELS, *tile)], operands=2, cost=100000000)(ocean, levels)
    outer_accel, lat_0, lat_1, outer_sums = call(
        outer_kernel,
        [half, *arrivals, (4, *tile)],
        scratch=momentum_scratch,
        operands=8,
    )(ocean, levels, surface, coriolis, own, lon_0, lon_1, lat_part)
    lat_0, lat_1 = swap_lat(lat_0, lat_1)
    accel, sums = call(
        inner_kernel,
        [(2, LEVELS, *tile), (4, *tile)],
        scratch=momentum_scratch,
        operands=9,
        cost=100000000,
    )(ocean, levels, coriolis, own, lon_0, lon_1, lat_part, outer_accel, outer_sums)

    def tracer(q, after):
        return call(
            functools.partial(tracer_kernel, q),
            [(LEVELS, *tile)],
            scratch=[(1, *tile), (3, *tile), tile],
            operands=5 + (q in EARLY),
            unread=1,
            cost=100000000,
        )(ocean, levels, own, lon_0, lon_1, *([lat_part] if q in EARLY else []), after)

    temperature = tracer(0, sums)
    edges, fields, packed, means, south, north = call(
        edge_kernel,
        [(2, 2, LEVELS, 8, COLS), (6, *rim), rim, (2, *tile), *arrivals],
        scratch=[(2, 2, 8, COLS), (2, 2, 8, COLS)],
        operands=6,
        unread=1,
    )(ocean, levels, surface, sums, lat_0, lat_1, temperature)
    rim_0, rim_1 = swap_lon(packed)
    tracer_edges = call(
        tracer_edge_kernel, [(2, 2, LEVELS, 8, COLS)], operands=4, cost=100000000
    )(ocean, levels, south, north)
    salinity = tracer(1, means)
    return call(final_kernel, [(4, LEVELS, *tile), (3, *tile)], scratch=[(2, *tile)], operands=11)(
        ocean, levels, accel, temperature, salinity, edges, tracer_edges, fields, means, rim_0, rim_1
    )


def solution(mesh):
    return jax.shard_map(
        on_device,
        mesh=mesh,
        in_specs=(P(None, None, "lat", "lon"), P(None, "lat", "lon"), P("lat", "lon")),
        out_specs=(P(None, None, "lat", "lon"), P(None, "lat", "lon")),
        check_vma=False,
    )
```
